32 devices in a mesh: dp: 8 (over z, x), mp: 4 (over y, core).
Axes of the slice: x: 2, y: 2, z: 4, core: 2. Of those that a mesh axis runs over, the one named last changes fastest.
Arguments:
- tokens: bfloat16 [24576, 768], P('dp')
- out_cot: bfloat16 [24576, 768], P('dp'), may hold values from -6.1035156e-05 to 6.1035156e-05
- seg_ids: int32 [24, 1024], P('dp'), may hold values from 0 to 16, as said below
- valid_mask: int32 [24, 1024], P('dp'), may hold values from 0 to 1, as said below
- last_pos: int32 [24, 16], P('dp'), may hold values from 0 to 1023, as said below
- pairs: int32 [384, 128], P('dp'), may hold values from 0 to 1, as said below
- images: bfloat16 [128, 768], P('dp')
- q_weight: bfloat16 [768, 768], P('dp', 'mp'), may hold values from -0.21875 to 0.21875
- k_weight: bfloat16 [768, 768], P('dp', 'mp'), may hold values from -0.21875 to 0.21875
- v_weight: bfloat16 [768, 768], P('dp', 'mp'), may hold values from -0.21875 to 0.21875
- o_weight: bfloat16 [768, 768], P('mp', 'dp'), may hold values from -0.875 to 0.875
- up_weight: bfloat16 [768, 3072], P('dp', 'mp'), may hold values from -0.21875 to 0.21875
- down_weight: bfloat16 [3072, 768], P('mp', 'dp'), may hold values from -0.21875 to 0.21875
- q_bias: float32 [768], replicated, may hold values from -3 to 3
- v_bias: float32 [768], replicated, may hold values from -3 to 3
- o_bias: float32 [768], replicated, may hold values from -2 to 2
- up_bias: float32 [3072], replicated, may hold values from -3 to 3
- down_bias: float32 [768], replicated, may hold values from -2 to 2
- gain_one: float32 [768], replicated, may hold values from 0.5 to 1.5
- shift_one: float32 [768], replicated, may hold values from -1 to 1
- gain_two: float32 [768], replicated, may hold values from 0.5 to 1.5
- shift_two: float32 [768], replicated, may hold values from -1 to 1
- log_scale: float32 [1], replicated, may hold values from 2 to 2.6
- logit_bias: float32 [1], replicated, may hold values from -6 to -3
Outputs:
- layer_out: bfloat16 [24576, 768], P('dp')
- grad_tokens: float32 [24576, 768], P('dp')
- grad_q_weight: float32 [768, 768], P('dp', 'mp')
- grad_k_weight: float32 [768, 768], P('dp', 'mp')
- grad_v_weight: float32 [768, 768], P('dp', 'mp')
- grad_o_weight: float32 [768, 768], P('mp', 'dp')
- grad_up_weight: float32 [768, 3072], P('dp', 'mp')
- grad_down_weight: float32 [3072, 768], P('mp', 'dp')
- grad_q_bias: float32 [768], P('mp')
- grad_v_bias: float32 [768], P('mp')
- grad_o_bias: float32 [768], replicated
- grad_up_bias: float32 [3072], P('mp')
- grad_down_bias: float32 [768], replicated
- grad_gain_one: float32 [768], replicated
- grad_shift_one: float32 [768], replicated
- grad_gain_two: float32 [768], replicated
- grad_shift_two: float32 [768], replicated
- grad_log_scale: float32 [1], replicated
- grad_logit_bias: float32 [1], replicated
The draws below stay inside these ranges and needn't reach their ends.
Inputs may be any that keep to these rules, and one draw needn't show every extreme that they name: `seg_ids`: each packed row holds 16 captions one after another from its first token; the tokens of the caption in slot c carry id c and the padding after the last caption carries id 16. A caption has 16 to 64 tokens, every row has one of 64 tokens, and some row is filled to its end by captions of 64 tokens. `valid_mask`: 1 exactly where seg_ids is below 16. last_pos[r, c] is the position of the last token with id c in row r. `pairs`: every caption belongs to exactly one image; every image has 2 to 5 captions, and some image has 5.
All inputs are finite; a program needn't handle non-finite values.
Results may differ from the reference program's by a relative error of at most 0.017.
Values may be sent and summed in bfloat16 or wider, within the bound.
No kernel may reach another device: no remote copies, remote signals or barrier semaphores. Data moves between devices by JAX's collectives and lax.ppermute only.
A program may use at most 256 MiB of HBM per device.

```python
from functools import partial
import jax
import jax.numpy as jnp
from jax import lax

D = 768
HEADS = 12
HEAD_DIM = 64
FF = 3072
CAP_ROW = 16
CAP_LEN = 64
SEQ = 1024
ROWS = 24
TOKENS = 24576
CAPS = 384
IMGS = 128
N_MP = 4


CAPTION_SPLITS = [[2, 2, 3, 5], [5, 3, 2, 2], [3, 3, 3, 3], [2, 4, 4, 2], [4, 2, 2, 4], [2, 5, 2, 3], [3, 2, 5, 2], [4, 4, 2, 2]]


def layout(key):
    base_key = jax.random.fold_in(key, 11)
    lengths = jax.random.randint(jax.random.fold_in(base_key, 1), (ROWS, CAP_ROW), CAP_LEN // 4, CAP_LEN + 1)
    full_at = jax.random.randint(jax.random.fold_in(base_key, 2), (ROWS, 1), 0, CAP_ROW)
    slot_ids = jnp.arange(CAP_ROW)[None, :]
    lengths = jnp.where(slot_ids == full_at, CAP_LEN, lengths)
    packed_row = jax.random.randint(jax.random.fold_in(base_key, 3), (), 0, ROWS)
    row_index = jnp.arange(ROWS)[:, None]
    lengths = jnp.where(row_index == packed_row, CAP_LEN, lengths)
    end_points = jnp.cumsum(lengths, axis=1)
    positions = jnp.arange(SEQ)[None, :, None]
    segment = jnp.sum((positions >= end_points[:, None, :]).astype(jnp.int32), axis=2)
    return (segment.astype(jnp.int32), (end_points - 1).astype(jnp.int32))


def owners_of(key):
    base_key = jax.random.fold_in(key, 23)
    groups = IMGS // 4
    split_table = jnp.array(CAPTION_SPLITS, dtype=jnp.int32)
    split_pick = jax.random.randint(jax.random.fold_in(base_key, 1), (groups,), 0, 8)
    split_pick = split_pick.at[0].set(0)
    counts = split_table[split_pick]
    end_points = jnp.cumsum(counts, axis=1)
    slot_index = jnp.arange(12)[None, :, None]
    local_image = jnp.sum((slot_index >= end_points[:, None, :]).astype(jnp.int32), axis=2)
    image_of = (local_image + 4 * jnp.arange(groups)[:, None]).reshape(-1)
    caption_order = jax.random.permutation(jax.random.fold_in(base_key, 2), CAPS)
    return image_of[caption_order].astype(jnp.int32)


def token_values(key):
    base_key = jax.random.fold_in(key, 37)
    return jax.random.normal(base_key, (TOKENS, D), jnp.float32)


def draw_tokens(key, part):
    return token_values(key).astype(jnp.bfloat16)


def draw_seg_ids(key, part):
    return layout(key)[0]


def draw_valid_mask(key, part):
    return (layout(key)[0] < CAP_ROW).astype(jnp.int32)


def draw_last_pos(key, part):
    return layout(key)[1]


def draw_pairs(key, part):
    owners = owners_of(key)
    return (owners[:, None] == jnp.arange(IMGS)[None, :]).astype(jnp.int32)


def draw_images(key, part):
    values = token_values(key).reshape(ROWS, SEQ, D)
    last_points = layout(key)[1]
    pooled = values[jnp.arange(ROWS)[:, None], last_points].reshape(CAPS, D)
    summed = jax.ops.segment_sum(pooled, owners_of(key), num_segments=IMGS)
    noise_part = jax.random.normal(jax.random.fold_in(key, 41), (IMGS, D), jnp.float32)
    return (summed + 1.5 * noise_part).astype(jnp.bfloat16)


def with_spikes(drawn, rng, source, target, blocks, factor):
    def block_of(dim):
        return (jnp.arange(drawn.shape[dim]) // (drawn.shape[dim] // blocks)).reshape((-1,) + (1,) * (drawn.ndim - 1 - dim))

    near = jax.random.permutation(rng, blocks)[block_of(target)]
    other_side = (block_of(target) + blocks // 2) % blocks
    return jnp.where((block_of(source) == near) | (block_of(source) == other_side), factor * drawn, drawn)


def block_scale(stream_key, dims, cuts, least, largest):
    def one(axis_at, blocks):
        draws = jax.random.uniform(jax.random.fold_in(jax.random.fold_in(stream_key, 6), axis_at), (blocks,), jnp.float32, least / len(cuts), largest / len(cuts))
        return jnp.repeat(jnp.exp(draws), dims[axis_at] // blocks).reshape((-1,) + (1,) * (len(dims) - axis_at - 1))

    level = one(*cuts[0])
    for cut in cuts[1:]:
        level = level * one(*cut)
    return level


def noise(stream_key, shape, scale, limit, shards=(), kind=jnp.bfloat16):
    values = jax.random.normal(stream_key, shape, jnp.float32) * scale
    if len(shards) > 0:
        values = block_scale(stream_key, shape, shards, -0.22, 0.18) * values
    return jnp.clip(values, min=-limit, max=limit).astype(kind)


def gaussian_with(key, dims, width, most, pieces, heavy, kind=jnp.bfloat16):
    values = width * jax.random.normal(key, dims, jnp.float32)
    if pieces:
        values = values * block_scale(key, dims, pieces, -0.22, 0.18)
    return jnp.clip(with_spikes(values, jax.random.fold_in(key, 3), *heavy), -most, most).astype(kind)


def setup_inputs(seed: int = 0) -> dict:
    seeds = jax.random.split(jax.random.key(seed), 25)
    return {
        "tokens": draw_tokens(jax.random.fold_in(seeds[24], 71), 0),
        "out_cot": gaussian_with(seeds[1], (TOKENS, D), (3.0 / (CAPS * D)), 6.103515625e-05, ((0, 8),), (0, 1, 8, 2.0)),
        "seg_ids": draw_seg_ids(jax.random.fold_in(seeds[24], 71), 0),
        "valid_mask": draw_valid_mask(jax.random.fold_in(seeds[24], 71), 0),
        "last_pos": draw_last_pos(jax.random.fold_in(seeds[24], 71), 0),
        "pairs": draw_pairs(jax.random.fold_in(seeds[24], 71), 0),
        "images": draw_images(jax.random.fold_in(seeds[24], 71), 0),
        "q_weight": noise(seeds[7], (D, D), D ** -0.5, 0.21875, ((0, 8), (1, 4))),
        "k_weight": noise(seeds[8], (D, D), D ** -0.5, 0.21875, ((0, 8), (1, 4))),
        "v_weight": noise(seeds[9], (D, D), D ** -0.5, 0.21875, ((0, 8), (1, 4))),
        "o_weight": noise(seeds[10], (D, D), (D // 16) ** -0.5, 0.875, ((0, 4), (1, 8))),
        "up_weight": noise(seeds[11], (D, FF), D ** -0.5, 0.21875, ((0, 8), (1, 4))),
        "down_weight": noise(seeds[12], (FF, D), (FF // 4) ** -0.5, 0.21875, ((0, 4), (1, 8))),
        "q_bias": noise(seeds[13], (D,), 0.5, 3.0, (), jnp.float32),
        "v_bias": noise(seeds[14], (D,), 0.5, 3.0, (), jnp.float32),
        "o_bias": noise(seeds[15], (D,), 0.3, 2.0, (), jnp.float32),
        "up_bias": noise(seeds[16], (FF,), 0.5, 3.0, (), jnp.float32),
        "down_bias": noise(seeds[17], (D,), 0.3, 2.0, (), jnp.float32),
        "gain_one": jnp.clip(1.0 + 0.1 * jax.random.normal(seeds[18], (D,), jnp.float32), 0.5, 1.5),
        "shift_one": noise(seeds[19], (D,), 0.2, 1.0, (), jnp.float32),
        "gain_two": jnp.clip(1.0 + 0.1 * jax.random.normal(seeds[20], (D,), jnp.float32), 0.5, 1.5),
        "shift_two": noise(seeds[21], (D,), 0.2, 1.0, (), jnp.float32),
        "log_scale": jnp.clip(jax.random.uniform(seeds[22], (1,), jnp.float32, 2.0, 2.6), 2.0, 2.6),
        "logit_bias": jnp.clip(jax.random.uniform(seeds[23], (1,), jnp.float32, -6.0, -3.0), -6.0, -3.0),
    }


EPSILON = 1e-06
MASKED = -1000000000.0
PRECISE = lax.Precision.HIGHEST

@jax.custom_vjp
def low(v):
    return lax.optimization_barrier(v.astype(jnp.bfloat16)).astype(jnp.float32)

@jax.custom_vjp
def low_back(v):
    return v

def low_keep(v):
    return (low(v), None)

def low_pass(kept, grad):
    return (grad,)

def back_keep(v):
    return (v, None)

def back_low(kept, grad):
    return (low(grad),)
low.defvjp(low_keep, low_pass)
low_back.defvjp(back_keep, back_low)

def matmul(left, right):
    return jnp.dot(left, right, precision=PRECISE, preferred_element_type=jnp.float32)

def layer_norm(values, gain_vec, shift_vec):
    center = values - lax.optimization_barrier(jnp.mean(values, axis=-1, keepdims=True))
    spread = lax.optimization_barrier(jnp.mean(center * center, axis=-1, keepdims=True))
    return center * lax.rsqrt(spread + EPSILON) * gain_vec + shift_vec

def head_attention(queries, key_rows, value_rows, allowed, head_count):
    seq_len = queries.shape[0]
    query_heads = queries.reshape(seq_len, head_count, HEAD_DIM)
    key_heads = key_rows.reshape(seq_len, head_count, HEAD_DIM)
    value_heads = value_rows.reshape(seq_len, head_count, HEAD_DIM)
    scores = low_back(jnp.einsum('qhd,khd->hqk', query_heads, key_heads, precision=PRECISE))
    scores = jnp.where(allowed[None], scores, MASKED)
    softmax_out = low(jax.nn.softmax(scores, axis=-1))
    head_mix = jnp.einsum('hqk,khd->qhd', softmax_out, value_heads, precision=PRECISE)
    return head_mix.reshape(seq_len, head_count * HEAD_DIM)

def row_forward(params, token_row, segment_row, valid_row):
    q_w, k_w, v_w, o_w, up_w, down_w, q_b, v_b, o_b, up_b, down_b, gain_a, shift_a, gain_b, shift_b = params
    places = jnp.arange(SEQ)
    allowed = (segment_row[:, None] == segment_row[None, :]) & ((valid_row[None, :] > 0) | (places[:, None] == places[None, :]))
    factor = HEAD_DIM ** (-0.5)
    group_cols = D // N_MP
    group_heads = HEADS // N_MP
    group_hidden = FF // N_MP
    h_one = low(layer_norm(token_row, gain_a, shift_a))
    attn_total = jnp.zeros_like(token_row)
    for head_group in range(N_MP):
        columns = slice(head_group * group_cols, (head_group + 1) * group_cols)
        h_use = low_back(h_one)
        queries = low(low_back((matmul(h_use, q_w[:, columns]) + q_b[columns]) * factor))
        key_rows = low(low_back(matmul(h_use, k_w[:, columns])))
        value_rows = low(low_back(matmul(h_use, v_w[:, columns]) + v_b[columns]))
        attended = low(low_back(head_attention(queries, key_rows, value_rows, allowed, group_heads)))
        attn_total = attn_total + low(low_back(matmul(attended, o_w[columns, :])))
    after_attn = token_row + attn_total + o_b
    h_two = low(layer_norm(after_attn, gain_b, shift_b))
    mlp_total = jnp.zeros_like(token_row)
    for hidden_group in range(N_MP):
        hidden_cols = slice(hidden_group * group_hidden, (hidden_group + 1) * group_hidden)
        h_use = low_back(h_two)
        pre_act = low_back(matmul(h_use, up_w[:, hidden_cols]) + up_b[hidden_cols])
        activation = low(jax.nn.gelu(pre_act, approximate=True))
        mlp_total = mlp_total + low(low_back(matmul(activation, down_w[hidden_cols, :])))
    return after_attn + mlp_total + down_b

def reference(tokens, out_cot, seg_ids, valid_mask, last_pos, pairs, images, q_weight, k_weight, v_weight, o_weight, up_weight, down_weight, q_bias, v_bias, o_bias, up_bias, down_bias, gain_one, shift_one, gain_two, shift_two, log_scale, logit_bias):
    weights = (q_weight.astype(jnp.float32), k_weight.astype(jnp.float32), v_weight.astype(jnp.float32), o_weight.astype(jnp.float32), up_weight.astype(jnp.float32), down_weight.astype(jnp.float32))
    vectors = (q_bias, v_bias, o_bias, up_bias, down_bias, gain_one, shift_one, gain_two, shift_two)
    params = weights + vectors
    token_rows = tokens.astype(jnp.float32).reshape(ROWS, SEQ, D)
    cotangent = out_cot.astype(jnp.float32).reshape(ROWS, SEQ, D)
    image_vals = images.astype(jnp.float32)
    image_unit = image_vals * lax.rsqrt(lax.optimization_barrier(jnp.sum(image_vals * image_vals, axis=1, keepdims=True)) + EPSILON)
    pair_signs = 2.0 * pairs.astype(jnp.float32) - 1.0
    row_ids = jnp.arange(ROWS)[:, None]

    def objective(rows_in, params_in, scale_log, bias_logit):
        row_step = jax.checkpoint(partial(row_forward, params_in))

        def visit_row(state_carry, row_item):
            return (state_carry, row_step(row_item[0], row_item[1], row_item[2]))
        _, result = lax.scan(visit_row, jnp.zeros((), jnp.float32), (rows_in, seg_ids, valid_mask))
        pooled = result[row_ids, last_pos].reshape(CAPS, D)
        text_unit = pooled * lax.rsqrt(lax.optimization_barrier(jnp.sum(pooled * pooled, axis=1, keepdims=True)) + EPSILON)
        logits = jnp.exp(scale_log[0]) * matmul(text_unit, image_unit.T) + bias_logit[0]
        loss_value = -jnp.sum(jax.nn.log_sigmoid(pair_signs * logits)) / CAPS
        return (jnp.sum(result * cotangent) + loss_value, result)
    objective_value, pullback, result = jax.vjp(objective, token_rows, params, log_scale, logit_bias, has_aux=True)
    grad_rows, grad_params, grad_scale, grad_shift = pullback(jnp.ones((), jnp.float32))
    return (result.reshape(TOKENS, D).astype(jnp.bfloat16), grad_rows.reshape(TOKENS, D), grad_params[0], grad_params[1], grad_params[2], grad_params[3], grad_params[4], grad_params[5], grad_params[6], grad_params[7], grad_params[8], grad_params[9], grad_params[10], grad_params[11], grad_params[12], grad_params[13], grad_params[14], grad_scale, grad_shift)
```

```python
import jax
import jax.numpy as jnp
from jax import lax
from jax.experimental import pallas as pl
from jax.experimental.pallas import tpu as pltpu
from jax.sharding import PartitionSpec as P

HEAD_DIM = 64
HALO = 64
QUAD = 4 * HEAD_DIM
EPSILON = 1e-06
MASKED = -1000000000.0
PRECISE = lax.Precision.HIGHEST
F32 = jnp.float32
BF16 = jnp.bfloat16


def _head_masks(rows):
    lane = lax.broadcasted_iota(jnp.int32, (rows, QUAD), 1) // HEAD_DIM
    return [lane == h for h in range(4)]


def _stack_heads(block, masks):
    zero = jnp.zeros_like(block)
    return jnp.concatenate([jnp.where(m, block, zero) for m in masks], axis=0)


def _pick_heads(stacked, masks):
    rows = stacked.shape[0] // 4
    out = stacked[:rows]
    for h in range(1, 4):
        out = jnp.where(masks[h], stacked[h * rows : (h + 1) * rows], out)
    return out


def _nt(a, b):
    return lax.dot_general(a, b, (((1,), (1,)), ((), ())), preferred_element_type=F32)


def _tn(a, b):
    return lax.dot_general(a, b, (((0,), (0,)), ((), ())), preferred_element_type=F32)


def _nn(a, b):
    return lax.dot_general(a, b, (((1,), (0,)), ((), ())), preferred_element_type=F32)


def _probs(q_stack, k_win, allowed):
    scores = jnp.where(allowed, _nt(q_stack, k_win), MASKED)
    top = jnp.max(scores, axis=-1, keepdims=True)
    e = jnp.exp(scores - top)
    return e / jnp.sum(e, axis=-1, keepdims=True)


def _allowed(fq_ref, fk_ref, b, lo):
    fq = fq_ref[pl.ds(lo, HALO), :]
    fk = fk_ref[b]
    allowed = fq == fk
    return jnp.concatenate([allowed] * 4, axis=0)


def _attend_kernel(q_ref, k_ref, v_ref, fq_ref, fk_ref, o_ref):
    total = q_ref.shape[0]
    masks = _head_masks(HALO)

    def step(b, carry):
        lo = pl.multiple_of(b * HALO, HALO)
        kw = pl.multiple_of(jnp.clip(lo - HALO, 0, total - 3 * HALO), HALO)
        allowed = _allowed(fq_ref, fk_ref, b, lo)
        for c in range(q_ref.shape[1] // QUAD):
            cols = slice(c * QUAD, (c + 1) * QUAD)
            q_stack = _stack_heads(q_ref[pl.ds(lo, HALO), cols], masks)
            p = _probs(q_stack, k_ref[pl.ds(kw, 3 * HALO), cols], allowed).astype(BF16)
            mix = _nn(p, v_ref[pl.ds(kw, 3 * HALO), cols])
            o_ref[pl.ds(lo, HALO), cols] = _pick_heads(mix, masks).astype(BF16)
        return carry

    lax.fori_loop(0, total // HALO, step, 0)


def _attend_back_kernel(
    q_ref, k_ref, v_ref, do_ref, fq_ref, fk_ref, dq_ref, dk_ref, dv_ref, dk_acc, dv_acc
):
    total = q_ref.shape[0]
    masks = _head_masks(HALO)
    dk_acc[...] = jnp.zeros_like(dk_acc)
    dv_acc[...] = jnp.zeros_like(dv_acc)

    def step(b, carry):
        lo = pl.multiple_of(b * HALO, HALO)
        kw = pl.multiple_of(jnp.clip(lo - HALO, 0, total - 3 * HALO), HALO)
        allowed = _allowed(fq_ref, fk_ref, b, lo)
        for c in range(q_ref.shape[1] // QUAD):
            cols = slice(c * QUAD, (c + 1) * QUAD)
            q_stack = _stack_heads(q_ref[pl.ds(lo, HALO), cols], masks)
            k_win = k_ref[pl.ds(kw, 3 * HALO), cols]
            p = _probs(q_stack, k_win, allowed)
            do_stack = _stack_heads(do_ref[pl.ds(lo, HALO), cols], masks)
            dp = _nt(do_stack, v_ref[pl.ds(kw, 3 * HALO), cols])
            ds = (p * (dp - jnp.sum(p * dp, axis=-1, keepdims=True))).astype(BF16)
            dv_acc[pl.ds(kw, 3 * HALO), cols] += _tn(p.astype(BF16), do_stack)
            dk_acc[pl.ds(kw, 3 * HALO), cols] += _tn(ds, q_stack)
            dq_ref[pl.ds(lo, HALO), cols] = _pick_heads(_nn(ds, k_win), masks).astype(BF16)
        return carry

    lax.fori_loop(0, total // HALO, step, 0)
    dk_ref[...] = dk_acc[...].astype(BF16)
    dv_ref[...] = dv_acc[...].astype(BF16)


def _vmem(n):
    return [pl.BlockSpec(memory_space=pltpu.VMEM)] * n


def attend(q, k, v, fq, fk):
    return pl.pallas_call(
        _attend_kernel,
        out_shape=jax.ShapeDtypeStruct(q.shape, BF16),
        in_specs=_vmem(5),
        out_specs=_vmem(1)[0],
        compiler_params=pltpu.CompilerParams(vmem_limit_bytes=40 << 20),
        name="attend",
    )(q, k, v, fq, fk)


def attend_back(q, k, v, do, fq, fk):
    out = jax.ShapeDtypeStruct(q.shape, BF16)
    return pl.pallas_call(
        _attend_back_kernel,
        out_shape=(out, out, out),
        in_specs=_vmem(6),
        out_specs=tuple(_vmem(3)),
        scratch_shapes=[pltpu.VMEM(q.shape, F32), pltpu.VMEM(q.shape, F32)],
        compiler_params=pltpu.CompilerParams(vmem_limit_bytes=48 << 20),
        name="attend_back",
    )(q, k, v, do, fq, fk)


def _flip(a, axis, bit):
    n = lax.axis_size(axis)
    return lax.ppermute(a, axis, [(i, i ^ bit) for i in range(n)])


class Moves:
    def __init__(self):
        self.n = lax.axis_size("dp")
        self.nz = self.n // 2
        at = lax.axis_index("dp")
        self.z, self.x = at // 2, at % 2
        self.line = self.n == 8

    def z_step(self, a, t, sign, growing):
        nz = self.nz
        pairs = []
        for i in range(nz):
            j = i + sign
            if 0 <= j < nz:
                away = i if sign > 0 else nz - 1 - i
                if (away >= t - 1) if growing else (away <= t - 1):
                    pairs.append((i, j))
        return lax.ppermute(
            a, "dp", [(2 * i + x, 2 * j + x) for i, j in pairs for x in range(2)]
        )

    def z_gather(self, a):
        right, left = [a], [a]
        for t in range(1, self.nz):
            right.append(self.z_step(right[-1], t, 1, True))
            left.append(self.z_step(left[-1], t, -1, True))
        return lax.dynamic_slice_in_dim(
            jnp.stack(right[:0:-1] + left), self.nz - 1 - self.z, self.nz, axis=0
        )

    def z_scatter(self, a):
        def own(at):
            return lax.dynamic_index_in_dim(a, at, 0, keepdims=False)

        nz = self.nz
        right = own(jnp.minimum(self.z + nz - 1, nz - 1))
        left = own(jnp.maximum(self.z - (nz - 1), 0))
        for t in range(1, nz):
            right = self.z_step(right, t, 1, False)
            left = self.z_step(left, t, -1, False)
            if t < nz - 1:
                right = add_low(right, own(jnp.minimum(self.z + nz - 1 - t, nz - 1)))
                left = add_low(left, own(jnp.maximum(self.z - (nz - 1 - t), 0)))
        return (own(self.z).astype(F32) + right.astype(F32)) + left.astype(F32)

    def x_gather(self, a):
        other = _flip(a, "dp", 1)
        first = self.x == 0
        return jnp.stack(
            [jnp.where(first, a, other), jnp.where(first, other, a)], axis=a.ndim - 2
        )

    def x_scatter(self, a, axis):
        give = lax.dynamic_index_in_dim(a, 1 - self.x, axis, keepdims=False)
        keep = lax.dynamic_index_in_dim(a, self.x, axis, keepdims=False)
        return add_low(keep, _flip(give, "dp", 1))

    def gather(self, a, order):
        cols = a.shape[1]
        if not self.line:
            mine = lax.all_gather(a, "dp", axis=0, tiled=True)
            far = _flip(mine, "mp", 2)
        elif order == "zxy":
            mine = self.x_gather(self.z_gather(a)).reshape(-1, cols)
            far = _flip(mine, "mp", 2)
        elif order == "zyx":
            near = self.z_gather(a)
            far = _flip(near, "mp", 2)
            mine = self.x_gather(near).reshape(-1, cols)
            far = self.x_gather(far).reshape(-1, cols)
        else:
            both = jnp.stack([a, _flip(a, "mp", 2)])
            both = self.z_gather(self.x_gather(both))
            mine = both[:, 0].reshape(-1, cols)
            far = both[:, 1].reshape(-1, cols)
        return [mine, _flip(mine, "mp", 1), far, _flip(far, "mp", 1)]

    def scatter(self, parts, order):
        cols = parts[0].shape[1]
        mine = add_low(parts[0], _flip(parts[1], "mp", 1))
        far = add_low(parts[2], _flip(parts[3], "mp", 1))
        if not self.line:
            mine = add_low(mine, _flip(far, "mp", 2))
            return lax.psum_scatter(mine, "dp", scatter_dimension=0, tiled=True).astype(F32)
        rows = mine.shape[0] // self.n
        shape = (self.nz, 2, rows, cols)
        if order == "yxz":
            mine = add_low(mine, _flip(far, "mp", 2)).reshape(shape)
            return self.z_scatter(self.x_scatter(mine, 1))
        if order == "xyz":
            mine = self.x_scatter(mine.reshape(shape), 1)
            far = self.x_scatter(far.reshape(shape), 1)
            return self.z_scatter(add_low(mine, _flip(far, "mp", 2)))
        both = self.x_scatter(jnp.stack([mine.reshape(shape), far.reshape(shape)], axis=1), 2)
        both = self.z_scatter(both).astype(BF16)
        return both[0].astype(F32) + _flip(both[1], "mp", 2).astype(F32)

    def gather_small(self, a):
        if not self.line:
            return lax.all_gather(a, "dp", axis=0, tiled=True)
        at = lax.axis_index("dp")
        for bit in (1, 2, 4):
            other = _flip(a, "dp", bit)
            low = (at & bit) == 0
            a = jnp.concatenate([jnp.where(low, a, other), jnp.where(low, other, a)], axis=0)
        return a

    def total(self, a):
        if not self.line:
            return lax.psum(a, ("dp", "mp"))
        for axis, bit in (("mp", 1), ("mp", 2), ("dp", 1), ("dp", 2), ("dp", 4)):
            a = a + _flip(a, axis, bit)
        return a


def add_low(a, b):
    return (a.astype(F32) + b.astype(F32)).astype(BF16)


def share_rows(block, at, rows, dtype):
    cols = block.shape[1]
    out = jnp.zeros((4 * rows, cols), dtype)
    near = _flip(block, "mp", 1)
    far = _flip(block, "mp", 2)
    cross = _flip(far, "mp", 1)
    for bits, piece in ((0, block), (1, near), (2, far), (3, cross)):
        out = lax.dynamic_update_slice_in_dim(out, piece.astype(dtype), (at ^ bits) * rows, 0)
    return out


def norm_parts(values):
    center = values - jnp.mean(values, axis=-1, keepdims=True)
    factor = lax.rsqrt(jnp.mean(center * center, axis=-1, keepdims=True) + EPSILON)
    return (center * factor, factor)


def norm_back(grad_rows, normed, factor, gain_vec):
    shaped = grad_rows * gain_vec
    first_mean = jnp.mean(shaped, axis=-1, keepdims=True)
    second_mean = jnp.mean(shaped * normed, axis=-1, keepdims=True)
    return factor * (shaped - first_mean - normed * second_mean)


def gelu_parts(u):
    k = 0.7978845608028654
    t = jnp.tanh(k * (u + 0.044715 * (u * u * u)))
    value = 0.5 * u * (1.0 + t)
    slope = 0.5 * (1.0 + t) + 0.5 * u * (1.0 - t * t) * (k * (1.0 + 3.0 * 0.044715 * (u * u)))
    return value, slope


def body(
    tokens,
    out_cot,
    seg_ids,
    valid_mask,
    last_pos,
    pairs,
    images,
    q_weight,
    k_weight,
    v_weight,
    o_weight,
    up_weight,
    down_weight,
    q_bias,
    v_bias,
    o_bias,
    up_bias,
    down_bias,
    gain_one,
    shift_one,
    gain_two,
    shift_two,
    log_scale,
    logit_bias,
):
    mv = Moves()
    groups = 4
    assert lax.axis_size("mp") == groups
    row_count, seq_len = seg_ids.shape
    token_count, width = tokens.shape
    piece = token_count // groups
    caption_total = pairs.shape[0] * lax.axis_size("dp")
    factor_q = HEAD_DIM ** (-0.5)
    at = lax.axis_index("mp")
    shard = q_weight.shape[1]
    hidden = up_weight.shape[1]

    image_rows = mv.gather_small(images).astype(F32)
    qk = mv.gather(jnp.concatenate([q_weight, k_weight], axis=1), "zxy")
    vo = mv.gather(jnp.concatenate([v_weight, o_weight.T], axis=1), "zyx")
    half = hidden // 2
    up_a = mv.gather(up_weight[:, :half], "zxy")
    up_b = mv.gather(up_weight[:, half:], "zyx")
    down_t = mv.gather(down_weight.T, "yxz")

    start = at * piece
    tail = jnp.minimum(start + piece, token_count - HALO)

    def window(a):
        return jnp.concatenate(
            [
                lax.dynamic_slice_in_dim(a, start, piece),
                lax.dynamic_slice_in_dim(a, tail, HALO),
            ],
            axis=0,
        )

    flat_at = jnp.arange(token_count, dtype=jnp.int32)
    row_of = flat_at // seq_len
    caption_id = jnp.where(
        valid_mask.reshape(-1) > 0,
        row_of * (last_pos.shape[1] * 2) + seg_ids.reshape(-1),
        (1 << 20) + flat_at,
    )
    inside = at < groups - 1
    ids = window(caption_id)
    tail_ids = jnp.where(inside, ids[piece:], -2 - jnp.arange(HALO, dtype=jnp.int32))
    ids = jnp.concatenate([ids[:piece], tail_ids])
    before = jnp.where(
        at > 0, lax.dynamic_index_in_dim(caption_id, jnp.maximum(start - 1, 0), keepdims=False), -1
    )
    owned = jnp.concatenate([ids[:piece] != before, (tail_ids == ids[piece - 1]) & inside])
    count = piece + HALO
    places = start + jnp.arange(count, dtype=jnp.int32)
    fq = ids[:, None]
    blocks = count // HALO
    fk = jnp.stack(
        [
            ids[min(max(b - 1, 0), blocks - 3) * HALO :][: 3 * HALO][None, :]
            for b in range(blocks)
        ]
    )
    rel = at ^ jnp.arange(groups, dtype=jnp.int32)

    def by_group(vec):
        return vec.reshape(groups, -1)[rel]

    x_rows = window(tokens).astype(F32)
    normed_one, factor_one = norm_parts(x_rows)
    h_one = (normed_one * gain_one + shift_one).astype(BF16)
    w_q = jnp.concatenate([w[:, :shard] for w in qk], axis=1)
    w_k = jnp.concatenate([w[:, shard:] for w in qk], axis=1)
    w_v = jnp.concatenate([w[:, :shard] for w in vo], axis=1)
    w_ot = jnp.concatenate([w[:, shard:] for w in vo], axis=1)
    queries = ((_nn(h_one, w_q) + by_group(q_bias).reshape(-1)) * factor_q).astype(BF16)
    keys = _nn(h_one, w_k).astype(BF16)
    vals = (_nn(h_one, w_v) + by_group(v_bias).reshape(-1)).astype(BF16)
    attended = attend(queries, keys, vals, fq, fk)
    after_attn = x_rows + _nt(attended, w_ot) + o_bias

    normed_two, factor_two = norm_parts(after_attn)
    h_two = (normed_two * gain_two + shift_two).astype(BF16)
    ups = [jnp.concatenate([a, b], axis=1) for a, b in zip(up_a, up_b)]
    up_parts = by_group(up_bias)
    pre_acts = [_nn(h_two, ups[g]) + up_parts[g] for g in range(groups)]
    acts = [gelu_parts(u)[0].astype(BF16) for u in pre_acts]
    mlp = _nt(acts[0], down_t[0])
    for g in range(1, groups):
        mlp = mlp + _nt(acts[g], down_t[g])
    result = after_attn + mlp + down_bias

    flat_last = (
        last_pos + seq_len * jnp.arange(row_count, dtype=jnp.int32)[:, None]
    ).reshape(-1)
    chosen = ((flat_last[:, None] == places[None, :]) & owned[None, :]).astype(F32)
    mine = jnp.sum(chosen, axis=1)
    pooled = jnp.dot(chosen, result, precision=PRECISE)
    image_unit = image_rows * lax.rsqrt(
        jnp.sum(image_rows * image_rows, axis=1, keepdims=True) + EPSILON
    )
    pair_signs = 2.0 * pairs.astype(F32) - 1.0

    def caption_loss(pooled_rows, scale_log, bias_logit):
        text_unit = pooled_rows * lax.rsqrt(
            jnp.sum(pooled_rows * pooled_rows, axis=1, keepdims=True) + EPSILON
        )
        logits = (
            jnp.exp(scale_log[0])
            * jnp.dot(text_unit, image_unit.T, precision=PRECISE, preferred_element_type=F32)
            + bias_logit[0]
        )
        return -jnp.sum(mine[:, None] * jax.nn.log_sigmoid(pair_signs * logits)) / caption_total

    _, loss_pull = jax.vjp(caption_loss, pooled, log_scale, logit_bias)
    pooled_grad, scale_grad, logit_grad = loss_pull(jnp.ones((), F32))
    spread = lax.dot_general(
        chosen, pooled_grad, (((0,), (0,)), ((), ())), precision=PRECISE
    )
    g_rows = jnp.where(owned[:, None], window(out_cot).astype(F32), 0.0) + spread

    tail_out = lax.ppermute(
        result[piece:].astype(BF16), "mp", [(i, i + 1) for i in range(groups - 1)]
    )

    def settle(rows_low, tail_low):
        head = jnp.where(owned[:HALO, None], rows_low[:HALO], tail_low)
        return jnp.concatenate([head, rows_low[HALO:piece]], axis=0)

    layer_out = share_rows(settle(result.astype(BF16), tail_out), at, piece, BF16)

    g_low = g_rows.astype(BF16)
    up_grads, down_grads, up_bias_grads = [], [], []
    d_h_two = None
    for g in range(groups):
        d_act = _nn(g_low, down_t[g])
        d_pre = (d_act * gelu_parts(pre_acts[g])[1]).astype(BF16)
        up_bias_grads.append(jnp.sum(d_pre.astype(F32), axis=0))
        up_grads.append(_tn(h_two, d_pre).astype(BF16))
        down_grads.append(_tn(g_low, acts[g]).astype(BF16))
        term = _nt(d_pre, ups[g])
        d_h_two = term if d_h_two is None else d_h_two + term
    grad_down = mv.scatter(down_grads, "yxz").T
    grad_up = mv.scatter(up_grads, "xyz")

    d_after = g_rows + norm_back(d_h_two, normed_two, factor_two, gain_two)
    d_after_low = d_after.astype(BF16)
    o_grad = _tn(d_after_low, attended).astype(BF16)
    d_attended = _nn(d_after_low, w_ot).astype(BF16)
    d_q, d_k, d_v = attend_back(queries, keys, vals, d_attended, fq, fk)
    d_h_one = _nt(d_q, w_q) * factor_q + _nt(d_k, w_k) + _nt(d_v, w_v)
    d_tokens = d_after + norm_back(d_h_one, normed_one, factor_one, gain_one)
    d_tokens = d_tokens.astype(BF16)
    tail_grad = lax.ppermute(d_tokens[piece:], "mp", [(i, i + 1) for i in range(groups - 1)])
    grad_tokens = share_rows(settle(d_tokens, tail_grad), at, piece, F32)

    q_grad = (_tn(h_one, d_q) * factor_q).astype(BF16)
    k_grad = _tn(h_one, d_k).astype(BF16)
    v_grad = _tn(h_one, d_v).astype(BF16)

    def pair_up(a, b):
        return [
            jnp.concatenate(
                [a[:, g * shard : (g + 1) * shard], b[:, g * shard : (g + 1) * shard]], axis=1
            )
            for g in range(groups)
        ]

    grad_qk = mv.scatter(pair_up(q_grad, k_grad), "xyz")
    grad_vo = mv.scatter(pair_up(v_grad, o_grad), "yxz")

    def from_groups(parts):
        return jnp.stack(parts)[rel].reshape(-1)

    def split(vec):
        return [vec[g * shard : (g + 1) * shard] for g in range(groups)]

    vectors = [
        from_groups(split(factor_q * jnp.sum(d_q.astype(F32), axis=0))),
        from_groups(split(jnp.sum(d_v.astype(F32), axis=0))),
        jnp.sum(d_after, axis=0),
        from_groups(up_bias_grads),
        jnp.sum(g_rows, axis=0),
        jnp.sum(d_h_one * normed_one, axis=0),
        jnp.sum(d_h_one, axis=0),
        jnp.sum(d_h_two * normed_two, axis=0),
        jnp.sum(d_h_two, axis=0),
        scale_grad,
        logit_grad,
    ]
    summed = mv.total(jnp.concatenate(vectors))
    out_vectors = []
    offset = 0
    for vec in vectors:
        out_vectors.append(summed[offset : offset + vec.shape[0]])
        offset += vec.shape[0]
    for i, cols in ((0, shard), (1, shard), (3, hidden)):
        out_vectors[i] = lax.dynamic_slice_in_dim(out_vectors[i], at * cols, cols)

    return (
        layer_out,
        grad_tokens,
        grad_qk[:, :shard],
        grad_qk[:, shard:],
        grad_vo[:, :shard],
        grad_vo[:, shard:].T,
        grad_up,
        grad_down,
        *out_vectors,
    )


def solution(mesh):
    rows, weight, weight_t = P("dp", None), P("dp", "mp"), P("mp", "dp")
    placed = (rows,) * 7 + (weight,) * 3 + (weight_t, weight, weight_t) + (P(),) * 11
    return jax.shard_map(
        body,
        mesh=mesh,
        in_specs=placed,
        out_specs=(rows,) * 2
        + (weight,) * 3
        + (weight_t, weight, weight_t)
        + (P("mp"), P("mp"), P(), P("mp"))
        + (P(),) * 7,
        check_vma=False,
    )
```

```python
import functools

import jax
import jax.numpy as jnp
from jax import lax
from jax.experimental import pallas as pl
from jax.experimental.pallas import tpu as pltpu
from jax.sharding import PartitionSpec as P

HEAD_DIM = 64
HALO = 64
QUAD = 4 * HEAD_DIM
EPSILON = 1e-06
MASKED = -1000000000.0
PRECISE = lax.Precision.HIGHEST
F32 = jnp.float32
BF16 = jnp.bfloat16


def _head_masks(rows):
    lane = lax.broadcasted_iota(jnp.int32, (rows, QUAD), 1) // HEAD_DIM
    return [lane == h for h in range(4)]


def _stack_heads(block, masks):
    zero = jnp.zeros_like(block)
    return jnp.concatenate([jnp.where(m, block, zero) for m in masks], axis=0)


def _pick_heads(stacked, masks):
    rows = stacked.shape[0] // 4
    out = stacked[:rows]
    for h in range(1, 4):
        out = jnp.where(masks[h], stacked[h * rows : (h + 1) * rows], out)
    return out


def _nt(a, b):
    return lax.dot_general(a, b, (((1,), (1,)), ((), ())), preferred_element_type=F32)


def _tn(a, b):
    return lax.dot_general(a, b, (((0,), (0,)), ((), ())), preferred_element_type=F32)


def _nn(a, b):
    return lax.dot_general(a, b, (((1,), (0,)), ((), ())), preferred_element_type=F32)


def _probs(q_stack, k_win, allowed):
    scores = jnp.where(allowed, _nt(q_stack, k_win), MASKED)
    top = jnp.max(scores, axis=-1, keepdims=True)
    e = jnp.exp(scores - top)
    return e / jnp.sum(e, axis=-1, keepdims=True)


def _allowed(fq_ref, fk_ref, b, lo):
    fq = fq_ref[pl.ds(lo, HALO), :]
    fk = fk_ref[b]
    allowed = fq == fk
    return jnp.concatenate([allowed] * 4, axis=0)


def _attend_kernel(q_ref, k_ref, v_ref, fq_ref, fk_ref, o_ref):
    total = q_ref.shape[0]
    masks = _head_masks(HALO)

    def step(b, carry):
        lo = pl.multiple_of(b * HALO, HALO)
        kw = pl.multiple_of(jnp.clip(lo - HALO, 0, total - 3 * HALO), HALO)
        allowed = _allowed(fq_ref, fk_ref, b, lo)
        for c in range(q_ref.shape[1] // QUAD):
            cols = slice(c * QUAD, (c + 1) * QUAD)
            q_stack = _stack_heads(q_ref[pl.ds(lo, HALO), cols], masks)
            p = _probs(q_stack, k_ref[pl.ds(kw, 3 * HALO), cols], allowed).astype(BF16)
            mix = _nn(p, v_ref[pl.ds(kw, 3 * HALO), cols])
            o_ref[pl.ds(lo, HALO), cols] = _pick_heads(mix, masks).astype(BF16)
        return carry

    lax.fori_loop(0, total // HALO, step, 0)


def _attend_back_kernel(
    q_ref, k_ref, v_ref, do_ref, fq_ref, fk_ref, dq_ref, dk_ref, dv_ref, dk_acc, dv_acc
):
    total = q_ref.shape[0]
    masks = _head_masks(HALO)
    dk_acc[...] = jnp.zeros_like(dk_acc)
    dv_acc[...] = jnp.zeros_like(dv_acc)

    def step(b, carry):
        lo = pl.multiple_of(b * HALO, HALO)
        kw = pl.multiple_of(jnp.clip(lo - HALO, 0, total - 3 * HALO), HALO)
        allowed = _allowed(fq_ref, fk_ref, b, lo)
        for c in range(q_ref.shape[1] // QUAD):
            cols = slice(c * QUAD, (c + 1) * QUAD)
            q_stack = _stack_heads(q_ref[pl.ds(lo, HALO), cols], masks)
            k_win = k_ref[pl.ds(kw, 3 * HALO), cols]
            p = _probs(q_stack, k_win, allowed)
            do_stack = _stack_heads(do_ref[pl.ds(lo, HALO), cols], masks)
            dp = _nt(do_stack, v_ref[pl.ds(kw, 3 * HALO), cols])
            ds = (p * (dp - jnp.sum(p * dp, axis=-1, keepdims=True))).astype(BF16)
            dv_acc[pl.ds(kw, 3 * HALO), cols] += _tn(p.astype(BF16), do_stack)
            dk_acc[pl.ds(kw, 3 * HALO), cols] += _tn(ds, q_stack)
            dq_ref[pl.ds(lo, HALO), cols] = _pick_heads(_nn(ds, k_win), masks).astype(BF16)
        return carry

    lax.fori_loop(0, total // HALO, step, 0)
    dk_ref[...] = dk_acc[...].astype(BF16)
    dv_ref[...] = dv_acc[...].astype(BF16)


def _vmem(n):
    return [pl.BlockSpec(memory_space=pltpu.VMEM)] * n


def attend(q, k, v, fq, fk):
    return pl.pallas_call(
        _attend_kernel,
        out_shape=jax.ShapeDtypeStruct(q.shape, BF16),
        in_specs=_vmem(5),
        out_specs=_vmem(1)[0],
        compiler_params=pltpu.CompilerParams(vmem_limit_bytes=40 << 20),
        name="attend",
    )(q, k, v, fq, fk)


def attend_back(q, k, v, do, fq, fk):
    out = jax.ShapeDtypeStruct(q.shape, BF16)
    return pl.pallas_call(
        _attend_back_kernel,
        out_shape=(out, out, out),
        in_specs=_vmem(6),
        out_specs=tuple(_vmem(3)),
        scratch_shapes=[pltpu.VMEM(q.shape, F32), pltpu.VMEM(q.shape, F32)],
        compiler_params=pltpu.CompilerParams(vmem_limit_bytes=48 << 20),
        name="attend_back",
    )(q, k, v, do, fq, fk)


def _flip(a, axis, bit):
    n = lax.axis_size(axis)
    return lax.ppermute(a, axis, [(i, i ^ bit) for i in range(n)])


class Moves:
    def __init__(self):
        self.n = lax.axis_size("dp")
        at = lax.axis_index("dp")
        self.z, self.x = at // 2, at % 2
        self.near = self.n == 8

    def z_all(self, a):
        return [a] + [_flip(a, "dp", 2 * j) for j in range(1, 4)]

    def plane_all(self, a):
        return [a, _flip(a, "dp", 1), _flip(a, "mp", 2), self.cross_flip(a)]

    def cross_flip(self, a):
        return lax.ppermute(
            a,
            ("dp", "mp"),
            [(4 * d + m, 4 * (d ^ 1) + (m ^ 2)) for d in range(self.n) for m in range(4)],
        )

    def core_all(self, parts):
        return [_flip(a, "mp", 1) for a in parts]

    def gather_far(self, a):
        mine = lax.all_gather(a, "dp", axis=0, tiled=True)
        far = _flip(mine, "mp", 2)
        return jnp.stack([mine, _flip(mine, "mp", 1), far, _flip(far, "mp", 1)])

    def to_core(self, parts):
        return _flip(jnp.stack([parts[1], parts[3]]), "mp", 1)

    def to_plane(self, parts, got):
        cols = parts[0].shape[1]
        mine, far = parts[0], parts[2]
        if not self.near:
            mine, far = add_low(mine, got[0]), add_low(far, got[1])
            return [add_low(mine, _flip(far, "mp", 2))]
        shape = (self.n // 2, 2, mine.shape[0] // self.n, cols)

        def side(a, b, at):
            def cut(v):
                return lax.dynamic_index_in_dim(v.reshape(shape), at, 1, keepdims=False)

            return add_low(cut(a), cut(b))

        return [
            side(mine, got[0], self.x),
            _flip(side(mine, got[0], 1 - self.x), "dp", 1),
            _flip(side(far, got[1], self.x), "mp", 2),
            self.cross_flip(side(far, got[1], 1 - self.x)),
        ]

    def to_z(self, held):
        if not self.near:
            return [lax.psum_scatter(held[0], "dp", scatter_dimension=0, tiled=True)]
        total = sum(h.astype(F32) for h in held).astype(BF16)

        def cut(j):
            return lax.dynamic_index_in_dim(total, self.z ^ j, 0, keepdims=False)

        return [cut(0)] + [_flip(cut(j), "dp", 2 * j) for j in range(1, 4)]

    def gather_small(self, a):
        if not self.near:
            return lax.all_gather(a, "dp", axis=0, tiled=True)
        at = lax.axis_index("dp")
        for bit in (1, 2, 4):
            other = _flip(a, "dp", bit)
            low = (at & bit) == 0
            a = jnp.concatenate([jnp.where(low, a, other), jnp.where(low, other, a)], axis=0)
        return a

    def total(self, a):
        if not self.near:
            return lax.psum(a, ("dp", "mp"))
        for axis, bit in (("mp", 1), ("mp", 2), ("dp", 1), ("dp", 2), ("dp", 4)):
            a = a + _flip(a, axis, bit)
        return a


def _place_kernel(plan, rows, at_ref, *refs):
    out, sem = refs[-2], refs[-1]
    z, x = at_ref[0], at_ref[1]
    copies = []
    for n, (src, first, zrel, dx, group, col) in enumerate(plan):
        slot = pl.multiple_of(((z ^ zrel) * 2 + (x ^ dx)) * rows, rows)
        width = refs[src].shape[-1]
        copies.append(
            pltpu.make_async_copy(
                refs[src].at[first],
                out.at[group, pl.ds(slot, rows), pl.ds(col, width)],
                sem.at[n],
            )
        )
    for c in copies:
        c.start()
    for c in copies:
        c.wait()


def place(mv, arrays, plan, n, cols):
    rows = arrays[0].shape[1]
    at = jnp.stack([mv.z, mv.x]).astype(jnp.int32)
    return pl.pallas_call(
        functools.partial(_place_kernel, plan, rows),
        out_shape=jax.ShapeDtypeStruct((4, n * rows, cols), BF16),
        in_specs=[pl.BlockSpec(memory_space=pltpu.SMEM)]
        + [pl.BlockSpec(memory_space=pl.ANY)] * len(arrays),
        out_specs=pl.BlockSpec(memory_space=pltpu.VMEM),
        scratch_shapes=[pltpu.SemaphoreType.DMA((len(plan),))],
        compiler_params=pltpu.CompilerParams(vmem_limit_bytes=32 << 20),
        name="place",
    )(at, *arrays)


def fence(*trees):
    return lax.optimization_barrier(trees)


def add_low(a, b):
    return (a.astype(F32) + b.astype(F32)).astype(BF16)


def share_rows(block, at, rows, dtype):
    cols = block.shape[1]
    out = jnp.zeros((4 * rows, cols), dtype)
    near = _flip(block, "mp", 1)
    far = _flip(block, "mp", 2)
    cross = _flip(far, "mp", 1)
    for bits, piece in ((0, block), (1, near), (2, far), (3, cross)):
        out = lax.dynamic_update_slice_in_dim(out, piece.astype(dtype), (at ^ bits) * rows, 0)
    return out


def norm_parts(values):
    center = values - jnp.mean(values, axis=-1, keepdims=True)
    factor = lax.rsqrt(jnp.mean(center * center, axis=-1, keepdims=True) + EPSILON)
    return (center * factor, factor)


def norm_back(grad_rows, normed, factor, gain_vec):
    shaped = grad_rows * gain_vec
    first_mean = jnp.mean(shaped, axis=-1, keepdims=True)
    second_mean = jnp.mean(shaped * normed, axis=-1, keepdims=True)
    return factor * (shaped - first_mean - normed * second_mean)


def gelu_parts(u):
    k = 0.7978845608028654
    t = jnp.tanh(k * (u + 0.044715 * (u * u * u)))
    value = 0.5 * u * (1.0 + t)
    slope = 0.5 * (1.0 + t) + 0.5 * u * (1.0 - t * t) * (k * (1.0 + 3.0 * 0.044715 * (u * u)))
    return value, slope


def body(
    tokens,
    out_cot,
    seg_ids,
    valid_mask,
    last_pos,
    pairs,
    images,
    q_weight,
    k_weight,
    v_weight,
    o_weight,
    up_weight,
    down_weight,
    q_bias,
    v_bias,
    o_bias,
    up_bias,
    down_bias,
    gain_one,
    shift_one,
    gain_two,
    shift_two,
    log_scale,
    logit_bias,
):
    mv = Moves()
    groups = 4
    assert lax.axis_size("mp") == groups
    row_count, seq_len = seg_ids.shape
    token_count, width = tokens.shape
    piece = token_count // groups
    caption_total = pairs.shape[0] * lax.axis_size("dp")
    factor_q = HEAD_DIM ** (-0.5)
    at = lax.axis_index("mp")
    shard = q_weight.shape[1]
    hidden = up_weight.shape[1]

    own_a = jnp.concatenate([q_weight, k_weight, v_weight, o_weight.T], axis=1)
    own_u = up_weight
    down_t = down_weight.T
    half = hidden // 2
    own_d1, own_d2 = down_t[:, :half], down_t[:, half:]
    if mv.near:
        a_z = mv.z_all(own_a)
        d2_plane = mv.plane_all(own_d2)
    image_rows = mv.gather_small(images).astype(F32)

    start = at * piece
    tail = jnp.minimum(start + piece, token_count - HALO)

    def window(a):
        return jnp.concatenate(
            [
                lax.dynamic_slice_in_dim(a, start, piece),
                lax.dynamic_slice_in_dim(a, tail, HALO),
            ],
            axis=0,
        )

    flat_at = jnp.arange(token_count, dtype=jnp.int32)
    row_of = flat_at // seq_len
    caption_id = jnp.where(
        valid_mask.reshape(-1) > 0,
        row_of * (last_pos.shape[1] * 2) + seg_ids.reshape(-1),
        (1 << 20) + flat_at,
    )
    inside = at < groups - 1
    ids = window(caption_id)
    tail_ids = jnp.where(inside, ids[piece:], -2 - jnp.arange(HALO, dtype=jnp.int32))
    ids = jnp.concatenate([ids[:piece], tail_ids])
    before = jnp.where(
        at > 0, lax.dynamic_index_in_dim(caption_id, jnp.maximum(start - 1, 0), keepdims=False), -1
    )
    owned = jnp.concatenate([ids[:piece] != before, (tail_ids == ids[piece - 1]) & inside])
    count = piece + HALO
    places = start + jnp.arange(count, dtype=jnp.int32)
    fq = ids[:, None]
    blocks = count // HALO
    fk = jnp.stack(
        [
            ids[min(max(b - 1, 0), blocks - 3) * HALO :][: 3 * HALO][None, :]
            for b in range(blocks)
        ]
    )
    rel = at ^ jnp.arange(groups, dtype=jnp.int32)

    def by_group(vec):
        return vec.reshape(groups, -1)[rel]

    x_rows = window(tokens).astype(F32)
    normed_one, factor_one = norm_parts(x_rows)
    h_one = (normed_one * gain_one + shift_one).astype(BF16)
    if mv.near:
        n = mv.n
        stages = range(4)
        plane_steps = [(dx, dy) for dy in range(2) for dx in range(2)]
        a_z, d2_plane, own_u, own_d1, h_one, image_rows = fence(
            a_z, d2_plane, own_u, own_d1, h_one, image_rows
        )
        a_plane = mv.plane_all(jnp.stack(a_z))
        u_z = mv.z_all(own_u)
        d2_z = mv.z_all(jnp.stack(d2_plane))
        a_plane, u_z, own_d1 = fence(a_plane, u_z, own_d1)
        a_core = mv.core_all(a_plane)
        u_plane = mv.plane_all(jnp.stack(u_z))
        d1_z = mv.z_all(own_d1)

        def plane_plan(first):
            return [
                (first + core * 4 + i, zrel, zrel, dx, core + 2 * dy, 0)
                for core in range(2)
                for i, (dx, dy) in enumerate(plane_steps)
                for zrel in stages
            ]

        w_a = place(mv, a_plane + a_core, plane_plan(0), n, own_a.shape[1])
    else:
        w_a, w_u, w_d = (mv.gather_far(v) for v in (own_a, own_u, down_t))

    def column(i):
        return jnp.concatenate(
            [w_a[g, :, i * shard : (i + 1) * shard] for g in range(groups)], axis=1
        )

    w_q, w_k, w_v, w_ot = (column(i) for i in range(4))
    queries = ((_nn(h_one, w_q) + by_group(q_bias).reshape(-1)) * factor_q).astype(BF16)
    keys = _nn(h_one, w_k).astype(BF16)
    vals = (_nn(h_one, w_v) + by_group(v_bias).reshape(-1)).astype(BF16)
    attended = attend(queries, keys, vals, fq, fk)
    after_attn = x_rows + _nt(attended, w_ot) + o_bias

    normed_two, factor_two = norm_parts(after_attn)
    h_two = (normed_two * gain_two + shift_two).astype(BF16)
    if mv.near:
        h_two, u_plane, d1_z = fence(h_two, u_plane, d1_z)
        u_core = mv.core_all(u_plane)
        d1_plane = mv.plane_all(jnp.stack(d1_z))
        w_u = place(mv, u_plane + u_core, plane_plan(0), n, hidden)
    up_parts = by_group(up_bias)
    pre_acts = [_nn(h_two, w_u[g]) + up_parts[g] for g in range(groups)]
    acts = [gelu_parts(u)[0].astype(BF16) for u in pre_acts]
    if mv.near:
        acts, d1_plane, d2_z = fence(acts, d1_plane, d2_z)
        d1_core = mv.core_all(d1_plane)
        d2_core = mv.core_all(d2_z)
        z_plan = [
            (8 + core * 4 + zrel, i, zrel, dx, core + 2 * dy, half)
            for core in range(2)
            for zrel in stages
            for i, (dx, dy) in enumerate(plane_steps)
        ]
        w_d = place(
            mv, d1_plane + d1_core + d2_z + d2_core, plane_plan(0) + z_plan, n, hidden
        )
    mlp = _nt(acts[0], w_d[0])
    for g in range(1, groups):
        mlp = mlp + _nt(acts[g], w_d[g])
    result = after_attn + mlp + down_bias

    flat_last = (
        last_pos + seq_len * jnp.arange(row_count, dtype=jnp.int32)[:, None]
    ).reshape(-1)
    chosen = ((flat_last[:, None] == places[None, :]) & owned[None, :]).astype(F32)
    mine = jnp.sum(chosen, axis=1)
    pooled = jnp.dot(chosen, result, precision=PRECISE)
    image_unit = image_rows * lax.rsqrt(
        jnp.sum(image_rows * image_rows, axis=1, keepdims=True) + EPSILON
    )
    pair_signs = 2.0 * pairs.astype(F32) - 1.0

    def caption_loss(pooled_rows, scale_log, bias_logit):
        text_unit = pooled_rows * lax.rsqrt(
            jnp.sum(pooled_rows * pooled_rows, axis=1, keepdims=True) + EPSILON
        )
        logits = (
            jnp.exp(scale_log[0])
            * jnp.dot(text_unit, image_unit.T, precision=PRECISE, preferred_element_type=F32)
            + bias_logit[0]
        )
        return -jnp.sum(mine[:, None] * jax.nn.log_sigmoid(pair_signs * logits)) / caption_total

    _, loss_pull = jax.vjp(caption_loss, pooled, log_scale, logit_bias)
    pooled_grad, scale_grad, logit_grad = loss_pull(jnp.ones((), F32))
    spread = lax.dot_general(
        chosen, pooled_grad, (((0,), (0,)), ((), ())), precision=PRECISE
    )
    g_rows = jnp.where(owned[:, None], window(out_cot).astype(F32), 0.0) + spread

    tail_out = lax.ppermute(
        result[piece:].astype(BF16), "mp", [(i, i + 1) for i in range(groups - 1)]
    )

    def settle(rows_low, tail_low):
        head = jnp.where(owned[:HALO, None], rows_low[:HALO], tail_low)
        return jnp.concatenate([head, rows_low[HALO:piece]], axis=0)

    layer_out = share_rows(settle(result.astype(BF16), tail_out), at, piece, BF16)

    g_low = g_rows.astype(BF16)
    down_grads = [_tn(g_low, acts[g]).astype(BF16) for g in range(groups)]
    down_grads, g_low = fence(down_grads, g_low)
    down_got = mv.to_core(down_grads)
    up_grads, up_bias_grads = [], []
    d_h_two = None
    for g in range(groups):
        if g == 2:
            down_got, d_h_two, g_low = fence(down_got, d_h_two, g_low)
            down_held = mv.to_plane(down_grads, down_got)
        d_act = _nn(g_low, w_d[g])
        d_pre = (d_act * gelu_parts(pre_acts[g])[1]).astype(BF16)
        up_bias_grads.append(jnp.sum(d_pre.astype(F32), axis=0))
        up_grads.append(_tn(h_two, d_pre).astype(BF16))
        term = _nt(d_pre, w_u[g])
        d_h_two = term if d_h_two is None else d_h_two + term
    up_grads, d_h_two = fence(up_grads, d_h_two)
    up_got = mv.to_core(up_grads)

    d_after = g_rows + norm_back(d_h_two, normed_two, factor_two, gain_two)
    d_after_low = d_after.astype(BF16)
    o_grad = _tn(d_after_low, attended).astype(BF16)
    d_attended = _nn(d_after_low, w_ot).astype(BF16)
    quads = []
    for c in range(width // QUAD):
        cols = slice(c * QUAD, (c + 1) * QUAD)
        if c == 1:
            up_got, d_attended = fence(up_got, d_attended)
            up_held = mv.to_plane(up_grads, up_got)
        if c == 2:
            down_held, d_attended, quads = fence(down_held, d_attended, quads)
            down_pieces = mv.to_z(down_held)
        quads.append(
            attend_back(
                queries[:, cols], keys[:, cols], vals[:, cols], d_attended[:, cols], fq, fk
            )
        )
    up_held, quads, down_pieces = fence(up_held, quads, down_pieces)
    up_pieces = mv.to_z(up_held)
    d_q, d_k, d_v = (jnp.concatenate(parts, axis=1) for parts in zip(*quads))
    d_h_one = _nt(d_q, w_q) * factor_q + _nt(d_k, w_k) + _nt(d_v, w_v)
    d_tokens = d_after + norm_back(d_h_one, normed_one, factor_one, gain_one)
    d_tokens = d_tokens.astype(BF16)
    tail_grad = lax.ppermute(d_tokens[piece:], "mp", [(i, i + 1) for i in range(groups - 1)])
    settled = settle(d_tokens, tail_grad)
    settled, d_q, d_k, d_v = fence(settled, d_q, d_k, d_v)
    grad_tokens = share_rows(settled, at, piece, F32)

    mixed = [
        (_tn(h_one, d_q) * factor_q).astype(BF16),
        _tn(h_one, d_k).astype(BF16),
        _tn(h_one, d_v).astype(BF16),
        o_grad,
    ]
    attn_grads = [
        jnp.concatenate([m[:, g * shard : (g + 1) * shard] for m in mixed], axis=1)
        for g in range(groups)
    ]
    attn_pieces = mv.to_z(mv.to_plane(attn_grads, mv.to_core(attn_grads)))

    def gathered(pieces):
        return sum(v.astype(F32) for v in pieces)

    grad_down = gathered(down_pieces).T
    grad_up = gathered(up_pieces)
    grad_attn = gathered(attn_pieces)

    def from_groups(parts):
        return jnp.stack(parts)[rel].reshape(-1)

    def split(vec):
        return [vec[g * shard : (g + 1) * shard] for g in range(groups)]

    vectors = [
        from_groups(split(factor_q * jnp.sum(d_q.astype(F32), axis=0))),
        from_groups(split(jnp.sum(d_v.astype(F32), axis=0))),
        jnp.sum(d_after, axis=0),
        from_groups(up_bias_grads),
        jnp.sum(g_rows, axis=0),
        jnp.sum(d_h_one * normed_one, axis=0),
        jnp.sum(d_h_one, axis=0),
        jnp.sum(d_h_two * normed_two, axis=0),
        jnp.sum(d_h_two, axis=0),
        scale_grad,
        logit_grad,
    ]
    summed = mv.total(jnp.concatenate(vectors))
    out_vectors = []
    offset = 0
    for vec in vectors:
        out_vectors.append(summed[offset : offset + vec.shape[0]])
        offset += vec.shape[0]
    for i, cols in ((0, shard), (1, shard), (3, hidden)):
        out_vectors[i] = lax.dynamic_slice_in_dim(out_vectors[i], at * cols, cols)

    return (
        layer_out,
        grad_tokens,
        grad_attn[:, :shard],
        grad_attn[:, shard : 2 * shard],
        grad_attn[:, 2 * shard : 3 * shard],
        grad_attn[:, 3 * shard :].T,
        grad_up,
        grad_down,
        *out_vectors,
    )


def solution(mesh):
    rows, weight, weight_t = P("dp", None), P("dp", "mp"), P("mp", "dp")
    placed = (rows,) * 7 + (weight,) * 3 + (weight_t, weight, weight_t) + (P(),) * 11
    return jax.shard_map(
        body,
        mesh=mesh,
        in_specs=placed,
        out_specs=(rows,) * 2
        + (weight,) * 3
        + (weight_t, weight, weight_t)
        + (P("mp"), P("mp"), P(), P("mp"))
        + (P(),) * 7,
        check_vma=False,
    )
```

```python
import functools

import jax
import jax.numpy as jnp
from jax import lax
from jax.experimental import pallas as pl
from jax.experimental.pallas import tpu as pltpu
from jax.sharding import PartitionSpec as P

HEAD_DIM = 64
HALO = 64
QUAD = 4 * HEAD_DIM
EPSILON = 1e-06
MASKED = -1000000000.0
PRECISE = lax.Precision.HIGHEST
F32 = jnp.float32
BF16 = jnp.bfloat16
VMEM = pltpu.VMEM
SMEM = pltpu.SMEM
GROUPS = 4
LIMIT = dict(plane_parts=10, qkv=62, attend=62, attend_back=40, up=62, down=62, down_grad=16, up_grad=24, middle=20, input=62, attn_grad=62, z_parts=6, spread=16)


def _nt(a, b):
    return lax.dot_general(a, b, (((1,), (1,)), ((), ())), preferred_element_type=F32)


def _tn(a, b):
    return lax.dot_general(a, b, (((0,), (0,)), ((), ())), preferred_element_type=F32)


def _nn(a, b, precision=None):
    return lax.dot_general(
        a, b, (((1,), (0,)), ((), ())), precision=precision, preferred_element_type=F32
    )


def norm_parts(values):
    center = values - jnp.mean(values, axis=-1, keepdims=True)
    factor = lax.rsqrt(jnp.mean(center * center, axis=-1, keepdims=True) + EPSILON)
    return (center * factor, factor)


def norm_back(grad_rows, normed, factor, gain_vec):
    shaped = grad_rows * gain_vec
    first_mean = jnp.mean(shaped, axis=-1, keepdims=True)
    second_mean = jnp.mean(shaped * normed, axis=-1, keepdims=True)
    return factor * (shaped - first_mean - normed * second_mean)


def gelu_parts(u):
    k = 0.7978845608028654
    sq = u * u
    t = jnp.tanh(k * (u + 0.044715 * (sq * u)))
    half = 0.5 * (1.0 + t)
    slope = half + 0.5 * u * (1.0 - t * t) * (k * (1.0 + 3.0 * 0.044715 * sq))
    return u * half, slope


def col_sum(a):
    return jnp.sum(a, axis=0, keepdims=True)


def staged(kernel, spaces, n_out, *refs):
    n_in = len(spaces)
    moved = [i for i, c in enumerate(spaces) if c == "v"]
    ins, outs = list(refs[:n_in]), refs[n_in : n_in + n_out]
    rest = refs[n_in + n_out :]
    in_bufs, out_bufs = rest[: len(moved)], rest[len(moved) : len(moved) + n_out]
    sem = rest[len(moved) + n_out]
    copies = [
        pltpu.make_async_copy(ins[i], buf, sem.at[n]) for n, (i, buf) in enumerate(zip(moved, in_bufs))
    ]
    for c in copies:
        c.start()
    for c in copies:
        c.wait()
    for i, buf in zip(moved, in_bufs):
        ins[i] = buf
    kernel(*ins, *out_bufs, *rest[len(moved) + n_out + 1 :])
    copies = [
        pltpu.make_async_copy(buf, ref, sem.at[len(moved) + n])
        for n, (buf, ref) in enumerate(zip(out_bufs, outs))
    ]
    for c in copies:
        c.start()
    for c in copies:
        c.wait()


def run(kernel, name, outs, ins, spaces=None, scratch=()):
    spaces = spaces or "v" * len(ins)
    moved = [a for a, c in zip(ins, spaces) if c == "v"]
    hbm, smem = pl.BlockSpec(memory_space=pltpu.HBM), pl.BlockSpec(memory_space=SMEM)
    return pl.pallas_call(
        functools.partial(staged, kernel, spaces, len(outs)),
        out_shape=tuple(jax.ShapeDtypeStruct(s, d) for s, d in outs),
        in_specs=[smem if c == "s" else hbm for c in spaces],
        out_specs=tuple(hbm for _ in outs),
        scratch_shapes=[VMEM(a.shape, a.dtype) for a in moved]
        + [VMEM(s, d) for s, d in outs]
        + [pltpu.SemaphoreType.DMA((len(moved) + len(outs),))]
        + list(scratch),
        compiler_params=pltpu.CompilerParams(vmem_limit_bytes=LIMIT[name] << 20),
        name=name,
    )(*ins)


def copies_of(plan, rows, at_ref, refs, buf, sem):
    z, x = at_ref[0], at_ref[1]
    out = [[] for _ in range(GROUPS)]
    for n, (src, first, zrel, dx, group, col, cut, wide) in enumerate(plan):
        slot = pl.multiple_of(((z ^ zrel) * 2 + (x ^ dx)) * rows, rows)
        out[group].append(
            pltpu.make_async_copy(
                refs[src].at[(*first, slice(None), pl.ds(cut, wide))],
                buf.at[group, pl.ds(slot, rows), pl.ds(col, wide)],
                sem.at[n],
            )
        )
    return out


def whole_copies(ref, buf, sem):
    return [[pltpu.make_async_copy(ref.at[g], buf.at[g], sem.at[g])] for g in range(GROUPS)]


class Weights:
    def __init__(self, arrays, plan, rows, cols):
        self.arrays, self.plan, self.rows, self.cols = arrays, plan, rows, cols

    def scratch(self, width):
        count = GROUPS if self.plan is None else len(self.plan)
        return [VMEM((GROUPS, width, self.cols), BF16), pltpu.SemaphoreType.DMA((count,))]

    def copies(self, at_ref, refs, buf, sem):
        if self.plan is None:
            return whole_copies(refs[0], buf, sem)
        return copies_of(self.plan, self.rows, at_ref, refs, buf, sem)


def _head_masks(rows):
    lane = lax.broadcasted_iota(jnp.int32, (rows, QUAD), 1) // HEAD_DIM
    return [lane == h for h in range(4)]


def _stack_heads(block, masks):
    zero = jnp.zeros_like(block)
    return jnp.concatenate([jnp.where(m, block, zero) for m in masks], axis=0)


def _pick_heads(stacked, masks):
    rows = stacked.shape[0] // 4
    out = stacked[:rows]
    for h in range(1, 4):
        out = jnp.where(masks[h], stacked[h * rows : (h + 1) * rows], out)
    return out


def _probs(q_stack, k_win, allowed):
    scores = jnp.where(allowed, _nt(q_stack, k_win), MASKED)
    top = jnp.max(scores, axis=-1, keepdims=True)
    e = jnp.exp(scores - top)
    return e * (1.0 / jnp.sum(e, axis=-1, keepdims=True))


def _allowed(fq_ref, fk_ref, b, lo):
    allowed = fq_ref[pl.ds(lo, HALO), :] == fk_ref[b]
    return jnp.concatenate([allowed] * 4, axis=0)


def _qkv_kernel(ws, width, shard, *refs):
    at_ref, x_ref, gain_ref, shift_ref, qb_ref, vb_ref = refs[:6]
    pieces = refs[6 : 6 + len(ws.arrays)]
    h_ref, q_ref, k_ref, v_ref, wq_ref, wk_ref, wv_ref, wo_ref, buf, sem = refs[
        6 + len(ws.arrays) :
    ]
    copies = ws.copies(at_ref, pieces, buf, sem)
    for group in copies:
        for c in group:
            c.start()
    h_ref[...] = (norm_parts(x_ref[...].astype(F32))[0] * gain_ref[...] + shift_ref[...]).astype(
        BF16
    )
    h = h_ref[...]
    for g in range(GROUPS):
        for c in copies[g]:
            c.wait()
        cols = slice(g * shard, (g + 1) * shard)
        r = _nn(h, buf[g])
        own = at_ref[2] ^ g
        q_ref[:, cols] = ((r[:, :shard] + qb_ref[own]) * HEAD_DIM ** (-0.5)).astype(BF16)
        k_ref[:, cols] = r[:, shard : 2 * shard].astype(BF16)
        v_ref[:, cols] = (r[:, 2 * shard : 3 * shard] + vb_ref[own]).astype(BF16)
        for i, ref in enumerate((wq_ref, wk_ref, wv_ref, wo_ref)):
            ref[:, cols] = buf[g, :, i * shard : (i + 1) * shard]


def _attend_kernel(
    q_ref, k_ref, v_ref, fq_ref, fk_ref, wo_ref, x_ref, ob_ref, gain_ref, shift_ref,
    o_ref, after_ref, h_ref,
):
    total = q_ref.shape[0]
    masks = _head_masks(HALO)

    def step(b, carry):
        lo = pl.multiple_of(b * HALO, HALO)
        kw = pl.multiple_of(jnp.clip(lo - HALO, 0, total - 3 * HALO), HALO)
        allowed = _allowed(fq_ref, fk_ref, b, lo)
        for c in range(q_ref.shape[1] // QUAD):
            cols = slice(c * QUAD, (c + 1) * QUAD)
            q_stack = _stack_heads(q_ref[pl.ds(lo, HALO), cols], masks)
            p = _probs(q_stack, k_ref[pl.ds(kw, 3 * HALO), cols], allowed).astype(BF16)
            mix = _nn(p, v_ref[pl.ds(kw, 3 * HALO), cols])
            o_ref[pl.ds(lo, HALO), cols] = _pick_heads(mix, masks).astype(BF16)
        return carry

    lax.fori_loop(0, total // HALO, step, 0)
    after_ref[...] = x_ref[...].astype(F32) + _nt(o_ref[...], wo_ref[...]) + ob_ref[...]
    h_ref[...] = (norm_parts(after_ref[...])[0] * gain_ref[...] + shift_ref[...]).astype(BF16)


def _attend_back_kernel(
    q_ref, k_ref, v_ref, do_ref, fq_ref, fk_ref, dq_ref, dk_ref, dv_ref, dk_acc, dv_acc
):
    total = q_ref.shape[0]
    masks = _head_masks(HALO)
    dk_acc[...] = jnp.zeros_like(dk_acc)
    dv_acc[...] = jnp.zeros_like(dv_acc)

    def step(b, carry):
        lo = pl.multiple_of(b * HALO, HALO)
        kw = pl.multiple_of(jnp.clip(lo - HALO, 0, total - 3 * HALO), HALO)
        allowed = _allowed(fq_ref, fk_ref, b, lo)
        q_stack = _stack_heads(q_ref[pl.ds(lo, HALO), :], masks)
        k_win = k_ref[pl.ds(kw, 3 * HALO), :]
        p = _probs(q_stack, k_win, allowed)
        do_stack = _stack_heads(do_ref[pl.ds(lo, HALO), :], masks)
        dp = _nt(do_stack, v_ref[pl.ds(kw, 3 * HALO), :])
        ds = (p * (dp - jnp.sum(p * dp, axis=-1, keepdims=True))).astype(BF16)
        dv_acc[pl.ds(kw, 3 * HALO), :] += _tn(p.astype(BF16), do_stack)
        dk_acc[pl.ds(kw, 3 * HALO), :] += _tn(ds, q_stack)
        dq_ref[pl.ds(lo, HALO), :] = _pick_heads(_nn(ds, k_win), masks).astype(BF16)
        return carry

    lax.fori_loop(0, total // HALO, step, 0)
    dk_ref[...] = dk_acc[...].astype(BF16)
    dv_ref[...] = dv_acc[...].astype(BF16)


def _attend_back_columns(c, *refs):
    fq_ref, fk_ref = refs[4:6]
    outs, bufs, sem = refs[6:9], refs[9:13], refs[13]
    copies = [
        pltpu.make_async_copy(ref.at[:, pl.ds(c * QUAD, QUAD)], buf, sem.at[n])
        for n, (ref, buf) in enumerate(zip(refs[:4], bufs))
    ]
    for copy in copies:
        copy.start()
    for copy in copies:
        copy.wait()
    _attend_back_kernel(*bufs, fq_ref, fk_ref, *outs, *refs[14:])


def attend_back(q, k, v, do, fq, fk, c):
    rows = q.shape[0]
    return run(
        functools.partial(_attend_back_columns, c),
        "attend_back",
        [((rows, QUAD), BF16)] * 3,
        [q, k, v, do, fq, fk],
        "aaaavv",
        scratch=[VMEM((rows, QUAD), BF16)] * 4
        + [pltpu.SemaphoreType.DMA((4,))]
        + [VMEM((rows, QUAD), F32)] * 2,
    )


def _up_kernel(ws, *refs):
    at_ref, h_ref, b_ref = refs[:3]
    pieces = refs[3 : 3 + len(ws.arrays)]
    act_ref, slope_ref, w_ref, buf, sem, pre = refs[3 + len(ws.arrays) :]
    g = pl.program_id(0)
    copies = ws.copies(at_ref, pieces, buf, sem)

    @pl.when(g == 0)
    def _():
        for group in copies:
            for c in group:
                c.start()

    for i in range(GROUPS):

        @pl.when(g == i)
        def _(i=i):
            for c in copies[i]:
                c.wait()

    w_ref[0] = buf[g]
    pre[...] = _nn(h_ref[...], buf[g])
    bias = b_ref[at_ref[2] ^ g]

    def step(i, carry):
        rows = pl.ds(pl.multiple_of(i * HALO, HALO), HALO)
        value, slope = gelu_parts(pre[rows, :] + bias)
        act_ref[0, rows, :] = value.astype(BF16)
        slope_ref[0, rows, :] = slope.astype(BF16)
        return carry

    lax.fori_loop(0, pre.shape[0] // HALO, step, 0)


def at_group(*shape):
    zeros = (0,) * (len(shape) - 1)
    return pl.BlockSpec((1,) + shape[1:], lambda g: (g,) + zeros)


def fixed(*shape):
    zeros = (0,) * len(shape)
    return pl.BlockSpec(shape, lambda g: zeros, pipeline_mode=pl.Buffered(1))


def up_stage(ws, at, h, bias):
    rows, width = h.shape
    hidden = ws.cols
    act = jax.ShapeDtypeStruct((GROUPS, rows, hidden), BF16)
    return pl.pallas_call(
        functools.partial(_up_kernel, ws),
        grid=(GROUPS,),
        out_shape=(act, act, jax.ShapeDtypeStruct((GROUPS, width, hidden), BF16)),
        in_specs=[pl.BlockSpec(memory_space=SMEM), fixed(rows, width), fixed(GROUPS, 1, hidden)]
        + [pl.BlockSpec(memory_space=pltpu.HBM)] * len(ws.arrays),
        out_specs=(
            at_group(GROUPS, rows, hidden),
            at_group(GROUPS, rows, hidden),
            at_group(GROUPS, width, hidden),
        ),
        scratch_shapes=ws.scratch(width) + [VMEM((rows, hidden), F32)],
        compiler_params=pltpu.CompilerParams(vmem_limit_bytes=LIMIT["up"] << 20),
        name="up",
    )(at, h, bias, *ws.arrays)


def _down_kernel(ws, total, *refs):
    (
        at_ref, last_ref, spot_ref, act_ref, after_ref, bias_ref, mine_ref, cot_ref, owned_ref, image_ref,
        pairs_ref, scale_ref, logit_ref,
    ) = refs[:13]
    pieces = refs[13 : 13 + len(ws.arrays)]
    out_ref, g_ref, low_ref, dbias_ref, dscale_ref, dlogit_ref, w_ref, buf, sem, acc, text_buf, image_buf = refs[
        13 + len(ws.arrays) :
    ]
    g = pl.program_id(0)
    copies = ws.copies(at_ref, pieces, buf, sem)

    @pl.when(g == 0)
    def _():
        for group in copies:
            for c in group:
                c.start()
        acc[...] = after_ref[...] + bias_ref[...]

    for i in range(GROUPS):

        @pl.when(g == i)
        def _(i=i):
            for c in copies[i]:
                c.wait()

    w_ref[0] = buf[g]
    acc[...] += _nt(act_ref[0], buf[g])

    @pl.when(g == GROUPS - 1)
    def _():
        out_ref[...] = acc[...].astype(BF16)
        caps = text_buf.shape[0]
        for c in range(caps):
            text_buf[c : c + 1, :] = acc[pl.ds(last_ref[c], 1), :]
        mine = mine_ref[...]
        pooled = text_buf[...]
        text_scale = lax.rsqrt(jnp.sum(pooled * pooled, axis=1, keepdims=True) + EPSILON)
        text = pooled * text_scale
        n_z, n_x, n_rows = image_ref.shape[:3]
        for z in range(n_z):
            for x in range(n_x):
                first = (z * n_x + x) * n_rows
                image_buf[first : first + n_rows, :] = image_ref[
                    z ^ spot_ref[0], x ^ spot_ref[1]
                ].astype(F32)
        image = image_buf[...]
        image = image * lax.rsqrt(jnp.sum(image * image, axis=1, keepdims=True) + EPSILON)
        scale = jnp.exp(scale_ref[...])
        dots = lax.dot_general(
            text, image, (((1,), (1,)), ((), ())), precision=PRECISE, preferred_element_type=F32
        )
        sign = 2.0 * pairs_ref[...].astype(F32) - 1.0
        logits = scale * dots + logit_ref[...]
        d_logits = (-1.0 / total) * mine * sign / (1.0 + jnp.exp(sign * logits))
        dlogit_ref[...] = jnp.sum(d_logits, keepdims=True)
        dscale_ref[...] = jnp.sum(d_logits * (scale * dots), keepdims=True)
        d_text = scale * _nn(d_logits, image, PRECISE)
        d_pooled = text_scale * (d_text - text * jnp.sum(d_text * text, axis=1, keepdims=True))
        g_ref[...] = cot_ref[...].astype(F32) * owned_ref[...]
        text_buf[...] = d_pooled
        for c in range(caps):
            g_ref[pl.ds(last_ref[c], 1), :] += text_buf[c : c + 1, :]
        rows = g_ref[...]
        low_ref[...] = rows.astype(BF16)
        dbias_ref[...] = col_sum(rows)


def down_stage(ws, at, last_at, spot, act, after, bias, mine, cot, owned, images, pairs, scale, logit, total):
    rows, width = after.shape
    hidden = ws.cols
    caps = mine.shape[0]
    one = jax.ShapeDtypeStruct((1, 1), F32)
    return pl.pallas_call(
        functools.partial(_down_kernel, ws, total),
        grid=(GROUPS,),
        out_shape=(
            jax.ShapeDtypeStruct((rows, width), BF16),
            jax.ShapeDtypeStruct((rows, width), F32),
            jax.ShapeDtypeStruct((rows, width), BF16),
            jax.ShapeDtypeStruct((1, width), F32),
            one,
            one,
            jax.ShapeDtypeStruct((GROUPS, width, hidden), BF16),
        ),
        in_specs=[
            pl.BlockSpec(memory_space=SMEM),
            pl.BlockSpec(memory_space=SMEM),
            pl.BlockSpec(memory_space=SMEM),
            at_group(GROUPS, rows, hidden),
            fixed(rows, width),
            fixed(1, width),
            fixed(caps, 1),
            fixed(rows, width),
            fixed(rows, 1),
            fixed(*images.shape),
            fixed(*pairs.shape),
            fixed(1, 1),
            fixed(1, 1),
        ]
        + [pl.BlockSpec(memory_space=pltpu.HBM)] * len(ws.arrays),
        out_specs=(
            fixed(rows, width),
            fixed(rows, width),
            fixed(rows, width),
            fixed(1, width),
            fixed(1, 1),
            fixed(1, 1),
            at_group(GROUPS, width, hidden),
        ),
        scratch_shapes=ws.scratch(width) + [VMEM((rows, width), F32), VMEM((caps, width), F32), VMEM((pairs.shape[1], width), F32)],
        compiler_params=pltpu.CompilerParams(vmem_limit_bytes=LIMIT["down"] << 20),
        name="down",
    )(
        at, last_at, spot, act, after, bias, mine, cot, owned, images, pairs,
        scale.reshape(1, 1), logit.reshape(1, 1), *ws.arrays,
    )


def _down_grad_kernel(low_ref, act_ref, give_ref, keep_ref):
    i = pl.program_id(0)
    grad = _tn(low_ref[...], act_ref[0]).astype(BF16)

    @pl.when(i < 2)
    def _():
        give_ref[0] = grad

    @pl.when(i >= 2)
    def _():
        keep_ref[0] = grad


def down_grad(low, act):
    rows, width = low.shape
    hidden = act.shape[2]
    out = jax.ShapeDtypeStruct((2, width, hidden), BF16)
    return pl.pallas_call(
        _down_grad_kernel,
        grid=(GROUPS,),
        out_shape=(out, out),
        in_specs=[
            fixed(rows, width),
            pl.BlockSpec((1, rows, hidden), lambda i: ((2 * i + 1) % 5, 0, 0)),
        ],
        out_specs=(
            pl.BlockSpec((1, width, hidden), lambda i: (jnp.minimum(i, 1), 0, 0)),
            pl.BlockSpec((1, width, hidden), lambda i: (jnp.maximum(i - 2, 0), 0, 0)),
        ),
        compiler_params=pltpu.CompilerParams(vmem_limit_bytes=LIMIT["down_grad"] << 20),
        name="down_grad",
    )(low, act)


def _up_grad_kernel(has_sum, low_ref, h_ref, slope_ref, wd_ref, wu_ref, *refs):
    i = pl.program_id(0)
    grad_ref, bias_ref, dh_ref, d_pre = refs[-4:]

    @pl.when(i == 0)
    def _():
        dh_ref[...] = refs[0][...] if has_sum else jnp.zeros_like(dh_ref)

    d_act = _nn(low_ref[...], wd_ref[0])
    d_pre[...] = (d_act * slope_ref[0].astype(F32)).astype(BF16)
    bias_ref[0] = col_sum(d_pre[...].astype(F32))
    grad_ref[0] = _tn(h_ref[...], d_pre[...]).astype(BF16)
    dh_ref[...] += _nt(d_pre[...], wu_ref[0])


def up_grad(low, h, slope, w_d, w_u, first, so_far=None):
    rows, width = low.shape
    hidden = slope.shape[2]

    def pair(a, b):
        return pl.BlockSpec((1, a, b), lambda i: (2 * i + first, 0, 0))

    extra = [] if so_far is None else [so_far]
    return pl.pallas_call(
        functools.partial(_up_grad_kernel, so_far is not None),
        grid=(2,),
        out_shape=(
            jax.ShapeDtypeStruct((2, width, hidden), BF16),
            jax.ShapeDtypeStruct((2, 1, hidden), F32),
            jax.ShapeDtypeStruct((rows, width), F32),
        ),
        in_specs=[
            fixed(rows, width),
            fixed(rows, width),
            pair(rows, hidden),
            pair(width, hidden),
            pair(width, hidden),
        ]
        + [fixed(rows, width)] * len(extra),
        out_specs=(
            at_group(2, width, hidden),
            at_group(2, 1, hidden),
            fixed(rows, width),
        ),
        scratch_shapes=[VMEM((rows, hidden), BF16)],
        compiler_params=pltpu.CompilerParams(vmem_limit_bytes=LIMIT["up_grad"] << 20),
        name="up_grad",
    )(low, h, slope, w_d, w_u, *extra)


def _middle_kernel(
    dh_ref, g_ref, after_ref, gain_ref, att_ref, wo_ref,
    after_grad_ref, datt_ref, ograd_ref, dgain_ref, dshift_ref, dob_ref,
):
    normed, factor = norm_parts(after_ref[...])
    dh = dh_ref[...]
    dgain_ref[...] = col_sum(dh * normed)
    dshift_ref[...] = col_sum(dh)
    d_after = g_ref[...] + norm_back(dh, normed, factor, gain_ref[...])
    after_grad_ref[...] = d_after
    dob_ref[...] = col_sum(d_after)
    low = d_after.astype(BF16)
    datt_ref[...] = _nn(low, wo_ref[...]).astype(BF16)
    ograd_ref[...] = _tn(low, att_ref[...]).astype(BF16)


def _input_kernel(quads, shard, *refs):
    dq, dk, dv = refs[:quads], refs[quads : 2 * quads], refs[2 * quads : 3 * quads]
    (
        wq_ref, wk_ref, wv_ref, after_grad_ref, x_ref, gain_ref, at_ref, up_a_ref, up_b_ref,
        ob_ref, db_ref, gain_two_ref, shift_two_ref, scale_ref, logit_ref,
    ) = refs[3 * quads : 3 * quads + 15]
    out_ref, vec_ref = refs[3 * quads + 15 :]
    vec_ref[...] = jnp.zeros_like(vec_ref)
    q_part = rest = None
    sums = ([], [])
    for c in range(quads):
        cols = slice(c * QUAD, (c + 1) * QUAD)
        terms = [_nt(d[c][...], w[:, cols]) for d, w in ((dq, wq_ref), (dk, wk_ref), (dv, wv_ref))]
        q_part = terms[0] if q_part is None else q_part + terms[0]
        both = terms[1] + terms[2]
        rest = both if rest is None else rest + both
        sums[0].append(col_sum(dq[c][...].astype(F32)) * HEAD_DIM ** (-0.5))
        sums[1].append(col_sum(dv[c][...].astype(F32)))
    me = at_ref[2]
    for i in range(2):
        whole = jnp.concatenate(sums[i], axis=1)
        for g in range(GROUPS):
            vec_ref[pl.ds(4 * i + (me ^ g), 1), :shard] = whole[:, g * shard : (g + 1) * shard]
    for g in range(GROUPS):
        ref = up_b_ref if g % 2 == 0 else up_a_ref
        vec_ref[pl.ds(8 + (me ^ g), 1), :] = ref[g // 2]
    dh = q_part * HEAD_DIM ** (-0.5) + rest
    normed, factor = norm_parts(x_ref[...].astype(F32))
    rows = [ob_ref[...], db_ref[...], col_sum(dh * normed), col_sum(dh)]
    rows += [gain_two_ref[...], shift_two_ref[...]]
    for i, v in enumerate(rows):
        vec_ref[12 + i : 13 + i, :] = v
    vec_ref[18:19, :1] = scale_ref[...]
    vec_ref[19:20, :1] = logit_ref[...]
    out_ref[...] = (after_grad_ref[...] + norm_back(dh, normed, factor, gain_ref[...])).astype(BF16)


def _attn_grad_kernel(quads, shard, *refs):
    h_ref, o_ref = refs[3 * quads : 3 * quads + 2]
    give_ref, keep_ref = refs[3 * quads + 2 :]
    place = {1: (give_ref, 0), 3: (give_ref, 1), 0: (keep_ref, 0), 2: (keep_ref, 1)}
    h = h_ref[...]
    for i in range(3):
        for c in range(quads):
            grad = _tn(h, refs[i * quads + c][...])
            if i == 0:
                grad = grad * HEAD_DIM ** (-0.5)
            grad = grad.astype(BF16)
            lo = c * QUAD
            while lo < (c + 1) * QUAD:
                g = lo // shard
                hi = min((g + 1) * shard, (c + 1) * QUAD)
                ref, slot = place[g]
                start = i * shard + lo - g * shard
                ref[slot, :, start : start + hi - lo] = grad[:, lo - c * QUAD : hi - c * QUAD]
                lo = hi
    for g in range(GROUPS):
        ref, slot = place[g]
        ref[slot, :, 3 * shard :] = o_ref[:, g * shard : (g + 1) * shard]


def _add(*vals):
    total = vals[0].astype(F32)
    for v in vals[1:]:
        total = total + v.astype(F32)
    return total.astype(BF16)


def _plane_kernel(at_ref, keep_ref, got_ref, *outs):
    for y in range(2):
        for dx in range(2):
            x = at_ref[1] ^ dx
            for z in range(keep_ref.shape[1]):
                outs[2 * y + dx][z] = _add(keep_ref[y, z, x], got_ref[y, z, x])


def _x_kernel(lo, hi, at_ref, keep_ref, got_ref, own_ref, give_ref):
    for dx, ref in enumerate((own_ref, give_ref)):
        x = at_ref[1] ^ dx
        for y in range(2):
            for z in range(keep_ref.shape[1]):
                ref[y, z] = _add(keep_ref[y, z, x, :, lo:hi], got_ref[y, z, x, :, lo:hi])


def _z_first_kernel(lo, hi, at_ref, keep_ref, got_ref, *outs):
    for j, ref in enumerate(outs):
        z = at_ref[0] ^ j
        for y in range(2):
            for x in range(2):
                ref[y, x] = _add(keep_ref[y, z, x, :, lo:hi], got_ref[y, z, x, :, lo:hi])


def by_block(mv, a):
    return a.reshape(2, mv.nz, 2, a.shape[1] // mv.n, a.shape[2])


def plane_parts(mv, keep, got):
    keep, got = by_block(mv, keep), by_block(mv, got)
    out = ((mv.nz,) + keep.shape[3:], BF16)
    return run(_plane_kernel, "plane_parts", [out] * 4, [mv.at, keep, got], "svv")


def x_parts(mv, keep, got, lo, hi):
    keep, got = by_block(mv, keep), by_block(mv, got)
    out = ((2, mv.nz, keep.shape[3], hi - lo), BF16)
    kernel = functools.partial(_x_kernel, lo, hi)
    return run(kernel, "plane_parts", [out] * 2, [mv.at, keep, got], "svv")


def z_first_parts(mv, keep, got, lo, hi):
    keep, got = by_block(mv, keep), by_block(mv, got)
    out = ((2, 2, keep.shape[3], hi - lo), BF16)
    kernel = functools.partial(_z_first_kernel, lo, hi)
    return run(kernel, "plane_parts", [out] * 4, [mv.at, keep, got], "svv")


def _z_kernel(count, at_ref, *refs):
    ins, outs = refs[:count], refs[count:]
    for j in range(4):
        b = at_ref[0] ^ j
        outs[j][...] = _add(*[r[b] for r in ins])


def _z_pair_kernel(at_ref, a_ref, b_ref, *outs):
    for j in range(4):
        b = at_ref[0] ^ j
        for y in range(2):
            outs[j][y] = _add(a_ref[y, b], b_ref[y, b])


def z_parts(mv, held):
    out = (held[0].shape[1:], BF16)
    kernel = functools.partial(_z_kernel, len(held))
    return run(kernel, "z_parts", [out] * 4, [mv.at, *held], "s" + "v" * len(held))


def z_pair_parts(mv, own, got):
    out = ((2,) + own.shape[2:], BF16)
    return run(_z_pair_kernel, "z_parts", [out] * 4, [mv.at, own, got], "svv")


def _x_last_kernel(at_ref, a_ref, b_ref, c_ref, d_ref, own_ref, give_ref):
    for dx, ref in enumerate((own_ref, give_ref)):
        x = at_ref[1] ^ dx
        for y in range(2):
            ref[y] = _add(a_ref[y, x], b_ref[y, x], c_ref[y, x], d_ref[y, x])


def x_last_parts(mv, held):
    out = ((2,) + held[0].shape[2:], BF16)
    return run(_x_last_kernel, "z_parts", [out] * 2, [mv.at, *held], "svvvv")


def _spread_kernel(piece, at_ref, keep_ref, *refs):
    out_ref = refs[-1]
    wins = [(refs[0],), (refs[1],), (refs[2], refs[3]), (refs[4], refs[5])]
    j = pl.program_id(0)
    here = j ^ at_ref[2]
    before = (j - 1) ^ at_ref[2]
    for i in range(4):

        @pl.when(here == i)
        def _(i=i):
            done = 0
            for ref in wins[i]:
                rows = min(ref.shape[0], piece - done)
                out_ref[done : done + rows, :] = ref[:rows, :].astype(out_ref.dtype)
                done += rows

    for i in range(4):

        @pl.when((before == i) & (j > 0))
        def _(i=i):
            ref = wins[i][-1]
            tail = ref[ref.shape[0] - HALO :, :].astype(out_ref.dtype)
            out_ref[:HALO, :] = jnp.where(keep_ref[0] > 0, out_ref[:HALO, :], tail)


def spread(at, keep, windows, piece, dtype):
    cols = windows[0].shape[1]
    return pl.pallas_call(
        functools.partial(_spread_kernel, piece),
        grid=(GROUPS,),
        out_shape=jax.ShapeDtypeStruct((GROUPS * piece, cols), dtype),
        in_specs=[pl.BlockSpec(memory_space=SMEM), at_group(GROUPS, HALO, 1)]
        + [fixed(*w.shape) for w in windows],
        out_specs=pl.BlockSpec((piece, cols), lambda j: (j, 0)),
        compiler_params=pltpu.CompilerParams(vmem_limit_bytes=LIMIT["spread"] << 20),
        name="spread",
    )(at, keep, *windows)


def _flip(a, axis, bit):
    n = lax.axis_size(axis)
    return lax.ppermute(a, axis, [(i, i ^ bit) for i in range(n)])


def fence(*trees):
    return lax.optimization_barrier(trees)


def add_low(a, b):
    return (a.astype(F32) + b.astype(F32)).astype(BF16)


class Moves:
    def __init__(self):
        self.n = lax.axis_size("dp")
        self.nz = self.n // 2
        at = lax.axis_index("dp")
        self.at = jnp.stack([at // 2, at % 2, lax.axis_index("mp")]).astype(jnp.int32)
        self.near = self.n == 8

    def z_all(self, a):
        return [a] + [_flip(a, "dp", 2 * j) for j in range(1, 4)]

    def cross_flip(self, a):
        return lax.ppermute(
            a,
            ("dp", "mp"),
            [(4 * d + m, 4 * (d ^ 1) + (m ^ 2)) for d in range(self.n) for m in range(4)],
        )

    def plane_all(self, a):
        return [a, _flip(a, "dp", 1), _flip(a, "mp", 2), self.cross_flip(a)]

    def core_all(self, parts):
        return [_flip(a, "mp", 1) for a in parts]

    def gather_far(self, a):
        mine = lax.all_gather(a, "dp", axis=0, tiled=True)
        far = _flip(mine, "mp", 2)
        whole = jnp.stack([mine, _flip(mine, "mp", 1), far, _flip(far, "mp", 1)])
        return Weights([whole], None, a.shape[0], a.shape[1])

    def to_core(self, give):
        return _flip(give, "mp", 1)

    def scatter_far(self, keep, got):
        both = add_low(keep, got)
        mine = add_low(both[0], _flip(both[1], "mp", 2))
        return lax.psum_scatter(mine, "dp", scatter_dimension=0, tiled=True).astype(F32)

    def plane_sides(self, parts):
        return [
            parts[0], _flip(parts[1], "dp", 1), _flip(parts[2], "mp", 2), self.cross_flip(parts[3]),
        ]

    def z_sides(self, parts):
        return [_flip(parts[j], "dp", 2 * j) for j in range(1, 4)]


PLANE = [(dx, dy) for dy in range(2) for dx in range(2)]


def z_then_plane(first, col, cut, wide):
    return [
        (first + 4 * core + i, (zrel,), zrel, dx, core + 2 * dy, col, cut, wide)
        for core in range(2)
        for i, (dx, dy) in enumerate(PLANE)
        for zrel in range(4)
    ]


def plane_then_z(first, col, cut, wide):
    return [
        (first + 4 * core + zrel, (i,), zrel, dx, core + 2 * dy, col, cut, wide)
        for core in range(2)
        for zrel in range(4)
        for i, (dx, dy) in enumerate(PLANE)
    ]


def body(
    tokens,
    out_cot,
    seg_ids,
    valid_mask,
    last_pos,
    pairs,
    images,
    q_weight,
    k_weight,
    v_weight,
    o_weight,
    up_weight,
    down_weight,
    q_bias,
    v_bias,
    o_bias,
    up_bias,
    down_bias,
    gain_one,
    shift_one,
    gain_two,
    shift_two,
    log_scale,
    logit_bias,
):
    mv = Moves()
    assert lax.axis_size("mp") == GROUPS
    row_count, seq_len = seg_ids.shape
    token_count, width = tokens.shape
    piece = token_count // GROUPS
    caption_total = pairs.shape[0] * mv.n
    at = lax.axis_index("mp")
    shard = q_weight.shape[1]
    hidden = up_weight.shape[1]
    block = q_weight.shape[0]
    quads = width // QUAD

    own_a = jnp.concatenate([q_weight, k_weight, v_weight, o_weight.T], axis=1)
    down_t = down_weight.T
    cut = QUAD
    if mv.near:
        a_z = mv.z_all(own_a)
        own_1 = jnp.concatenate([up_weight, down_t[:, :cut]], axis=1)
        w2_plane = mv.plane_all(down_t[:, cut:])
        pics = jnp.stack([images, _flip(images, "dp", 1)])
        a_z, tokens, out_cot, seg_ids, valid_mask, last_pos, own_1, w2_plane, pics = fence(
            a_z, tokens, out_cot, seg_ids, valid_mask, last_pos, own_1, w2_plane, pics
        )
        a_here = jnp.stack(a_z)
        a_plane = mv.plane_all(a_here)
        a_core = [mv.to_core(a_here)]
        w1_z = mv.z_all(own_1)

    start = at * piece
    tail = jnp.minimum(start + piece, token_count - HALO)

    def window(a):
        return jnp.concatenate(
            [
                lax.dynamic_slice_in_dim(a, start, piece),
                lax.dynamic_slice_in_dim(a, tail, HALO),
            ],
            axis=0,
        )

    flat_at = jnp.arange(token_count, dtype=jnp.int32)
    caption_id = jnp.where(
        valid_mask.reshape(-1) > 0,
        (flat_at // seq_len) * (last_pos.shape[1] * 2) + seg_ids.reshape(-1),
        (1 << 20) + flat_at,
    )
    inside = at < GROUPS - 1
    ids = window(caption_id)
    tail_ids = jnp.where(inside, ids[piece:], -2 - jnp.arange(HALO, dtype=jnp.int32))
    ids = jnp.concatenate([ids[:piece], tail_ids])
    before = jnp.where(
        at > 0, lax.dynamic_index_in_dim(caption_id, jnp.maximum(start - 1, 0), keepdims=False), -1
    )
    owned = jnp.concatenate([ids[:piece] != before, (tail_ids == ids[piece - 1]) & inside])
    by_piece = caption_id.reshape(GROUPS, piece)
    last_before = jnp.concatenate([jnp.full((1,), -1, jnp.int32), by_piece[:-1, -1]])
    keep_head = (by_piece[:, :HALO] != last_before[:, None]).astype(F32)[:, :, None]
    count = piece + HALO
    places = start + jnp.arange(count, dtype=jnp.int32)
    fq = ids[:, None]
    blocks = count // HALO
    by_block_ids = ids.reshape(blocks, HALO)
    first = jnp.concatenate([by_block_ids[:1], by_block_ids[: blocks - 2], by_block_ids[-3:-2]])
    second = jnp.concatenate([by_block_ids[1:2], by_block_ids[1 : blocks - 1], by_block_ids[-2:-1]])
    third = jnp.concatenate([by_block_ids[2:3], by_block_ids[2:], by_block_ids[-1:]])
    fk = jnp.concatenate([first, second, third], axis=1)[:, None, :]
    def by_group(vec):
        return vec.reshape(GROUPS, 1, -1)

    flat_last = (
        last_pos + seq_len * jnp.arange(row_count, dtype=jnp.int32)[:, None]
    ).reshape(-1)
    last_at = jnp.clip(flat_last - start, 0, count - 1)
    mine = jnp.any((flat_last[:, None] == places[None, :]) & owned[None, :], axis=1)
    mine = mine.astype(F32)[:, None]
    x_rows = window(tokens)
    cot = window(out_cot)
    owned_rows = owned.astype(F32)[:, None]

    def row(v):
        return v.reshape(1, -1)

    q_part, v_part, up_part = by_group(q_bias), by_group(v_bias), by_group(up_bias)
    if mv.near:
        small = (
            x_rows, cot, fq, fk, last_at, mine, owned_rows, keep_head, q_part, v_part, up_part,
        )
        a_plane, a_core, w1_z, w2_plane, pics, small = fence(
            a_plane, a_core, w1_z, w2_plane, pics, small
        )
        (x_rows, cot, fq, fk, last_at, mine, owned_rows, keep_head, q_part, v_part, up_part) = small
        spot = mv.at
        a_core += [mv.to_core(v) for v in a_plane[1:]]
        w_a = Weights(a_plane + a_core, z_then_plane(0, 0, 0, hidden), block, hidden)
        w1_here, w2_here = jnp.stack(w1_z), jnp.stack(w2_plane)
        w1_x, w1_y = _flip(w1_here, "dp", 1), _flip(w1_here, "mp", 2)
        w2_near = [_flip(w2_here, "dp", 2), _flip(w2_here, "dp", 4)]
    else:
        w_a, w_u, w_d = (mv.gather_far(v) for v in (own_a, up_weight, down_t))
        pics = lax.all_gather(images, "dp", axis=0, tiled=True).reshape(mv.nz, 2, -1, width)
        spot = jnp.zeros_like(mv.at)

    rows_low = ((count, width), BF16)
    square = ((width, width), BF16)
    h_one, queries, keys, vals, w_q, w_k, w_v, w_o = run(
        functools.partial(_qkv_kernel, w_a, width, shard),
        "qkv",
        [rows_low] * 4 + [square] * 4,
        [mv.at, x_rows, row(gain_one), row(shift_one), q_part, v_part, *w_a.arrays],
        "s" + "v" * 5 + "a" * len(w_a.arrays),
        scratch=w_a.scratch(width),
    )
    if mv.near:
        queries, keys, vals, w1_here, w2_here, w1_x, w1_y, w2_near, pics = fence(
            queries, keys, vals, w1_here, w2_here, w1_x, w1_y, w2_near, pics
        )
        pics = mv.z_all(pics)
        w1_cross, w2_last = mv.cross_flip(w1_here), _flip(w2_here, "dp", 6)
        w1_core = [mv.to_core(v) for v in (w1_here, w1_x, w1_y)]
    attended, after_attn, h_two = run(
        _attend_kernel,
        "attend",
        [rows_low, ((count, width), F32), rows_low],
        [queries, keys, vals, fq, fk, w_o, x_rows, row(o_bias), row(gain_two), row(shift_two)],
    )
    if mv.near:
        h_two, w1_cross, w2_last, w1_core, pics = fence(h_two, w1_cross, w2_last, w1_core, pics)
        pics = jnp.stack(pics)
        w1_all = [w1_here, w1_x, w1_y, w1_cross, *w1_core, mv.to_core(w1_cross)]
        w_u = Weights(w1_all, z_then_plane(0, 0, 0, hidden), block, hidden)
        w2_all = [w2_here, *w2_near, w2_last]
        w2_all = w2_all + [mv.to_core(v) for v in w2_all]
    acts, slopes, w_up = up_stage(w_u, mv.at, h_two, up_part)
    if mv.near:
        w2_all, acts = fence(w2_all, acts)
        w_d = Weights(
            w1_all + w2_all,
            z_then_plane(0, 0, hidden, cut) + plane_then_z(8, cut, 0, hidden - cut),
            block,
            hidden,
        )
    out_low, g_rows, g_low, d_down_bias, d_scale, d_logit, w_down = down_stage(
        w_d, mv.at, last_at, spot, acts, after_attn, row(down_bias), mine, cot, owned_rows, pics, pairs,
        log_scale, logit_bias, caption_total,
    )

    split = count // 2
    out_near = _flip(out_low, "mp", 1)
    down_give, down_keep = down_grad(g_low, acts)
    down_give, down_keep, g_low, out_near = fence(down_give, down_keep, g_low, out_near)
    down_got = mv.to_core(down_give)
    out_a = _flip(out_low[:split], "mp", 2)
    up_give, up_bias_a, d_h_two = up_grad(g_low, h_two, slopes, w_down, w_up, 1)
    down_got, up_give, d_h_two, out_a = fence(down_got, up_give, d_h_two, out_a)
    up_got = mv.to_core(up_give)
    out_cross_a = _flip(out_a, "mp", 1)
    if mv.near:
        sent = plane_parts(mv, down_keep, down_got)
        sent, d_h_two = fence(sent, d_h_two)
        down_held = mv.plane_sides(sent)
    up_keep, up_bias_b, d_h_two = up_grad(g_low, h_two, slopes, w_down, w_up, 0, d_h_two)
    vec = ((1, width), F32)
    d_after, d_attended, o_grad, d_gain_two, d_shift_two, d_o_bias = run(
        _middle_kernel,
        "middle",
        [((count, width), F32), rows_low, square, vec, vec, vec],
        [d_h_two, g_rows, after_attn, row(gain_two), attended, w_o],
    )
    parts = [attend_back(queries, keys, vals, d_attended, fq, fk, 0)]
    if mv.near:
        down_held, up_got, up_keep, parts, out_cross_a = fence(
            down_held, up_got, up_keep, parts, out_cross_a
        )
        down_sent = z_parts(mv, down_held)
        sent = plane_parts(mv, up_keep, up_got)
        down_sent, sent, d_attended = fence(down_sent, sent, d_attended)
        up_held = mv.plane_sides(sent)
        down_pieces = [down_sent[0]] + [_flip(down_sent[j], "dp", 2 * j) for j in (1, 2)]
    for c in range(1, quads):
        parts.append(attend_back(queries, keys, vals, d_attended, fq, fk, c))
    if mv.near:
        parts, up_held, down_pieces = fence(parts, up_held, down_pieces)
        sent = z_parts(mv, up_held)
        sent, parts = fence(sent, parts)
        up_pieces = [sent[0]] + mv.z_sides(sent)
        down_pieces.append(_flip(down_sent[3], "dp", 6))
    flat = [p[i] for i in range(3) for p in parts]
    d_tokens, summed = run(
        functools.partial(_input_kernel, quads, shard),
        "input",
        [rows_low, ((24, hidden), F32)],
        [
            *flat, w_q, w_k, w_v, d_after, x_rows, row(gain_one), mv.at, up_bias_a, up_bias_b,
            d_o_bias, d_down_bias, d_gain_two, d_shift_two, d_scale, d_logit,
        ],
        "v" * (3 * quads + 6) + "s" + "v" * 8,
    )
    if mv.near:
        d_tokens, flat, summed, up_pieces, down_pieces, out_low = fence(
            d_tokens, flat, summed, up_pieces, down_pieces, out_low
        )
        summed = summed + _flip(summed, "mp", 1)
    out_b = _flip(out_low[split:], "mp", 2)
    attn_give, attn_keep = run(
        functools.partial(_attn_grad_kernel, quads, shard),
        "attn_grad",
        [((2, width, hidden), BF16)] * 2,
        [*flat, h_one, o_grad],
    )
    attn_give, attn_keep, summed, out_b, d_tokens = fence(
        attn_give, attn_keep, summed, out_b, d_tokens
    )
    attn_got = mv.to_core(attn_give)
    grad_near = _flip(d_tokens, "mp", 1)
    if mv.near:
        summed = mv.plane_all(summed)
        attn_got, grad_near, summed = fence(attn_got, grad_near, summed)
        cut = 2 * QUAD
        own_a, sent_a = x_parts(mv, attn_keep, attn_got, 0, cut)
        sent = z_first_parts(mv, attn_keep, attn_got, cut, hidden)
        sent_a, sent, d_tokens, out_b = fence(sent_a, sent, d_tokens, out_b)
        side_a = _flip(sent_a, "dp", 1)
        pieces_b = [sent[0]] + mv.z_sides(sent)
    far_a = _flip(d_tokens[:split], "mp", 2)
    out_cross_b = _flip(out_b, "mp", 1)

    def low_sum(pieces):
        return sum(v.astype(F32) for v in pieces)

    if mv.near:
        side_a, pieces_b, far_a, out_cross_b = fence(side_a, pieces_b, far_a, out_cross_b)
        sent = z_pair_parts(mv, own_a, side_a)
        own_b, sent_b = x_last_parts(mv, pieces_b)
        sent, sent_b, d_tokens, out_cross_b = fence(sent, sent_b, d_tokens, out_cross_b)
        pieces_a = [sent[0]] + mv.z_sides(sent)
        side_b = _flip(sent_b, "dp", 1)
    far_b = _flip(d_tokens[split:], "mp", 2)
    grad_cross_a = _flip(far_a, "mp", 1)
    layer_out = spread(
        mv.at, keep_head, [out_low, out_near, out_a, out_b, out_cross_a, out_cross_b], piece, BF16
    )
    if mv.near:
        pieces_a, side_b, far_b, grad_cross_a, summed = fence(
            pieces_a, side_b, far_b, grad_cross_a, summed
        )
        summed = mv.z_all((summed[0] + summed[1]) + (summed[2] + summed[3]))
        summed = (summed[0] + summed[1]) + (summed[2] + summed[3])
        grad_down = low_sum(down_pieces).T
        grad_up = low_sum(up_pieces)
        sum_a, sum_b = low_sum(pieces_a), low_sum([own_b, side_b])
        both = jnp.concatenate([sum_a, sum_b], axis=2)
        grad_attn = both[0] + _flip(both[1].astype(BF16), "mp", 2).astype(F32)
    else:
        summed = lax.psum(summed, ("dp", "mp"))
        grad_down = mv.scatter_far(down_keep, down_got).T
        grad_up = mv.scatter_far(up_keep, up_got)
        grad_attn = mv.scatter_far(attn_keep, attn_got)
    grad_cross_b = _flip(far_b, "mp", 1)
    grad_tokens = spread(
        mv.at, keep_head, [d_tokens, grad_near, far_a, far_b, grad_cross_a, grad_cross_b], piece, F32
    )
    def mine_of(first):
        return lax.dynamic_index_in_dim(summed, first + at, 0, keepdims=False)

    out_vectors = [mine_of(0)[:shard], mine_of(4)[:shard], summed[12], mine_of(8)]
    out_vectors += [summed[i] for i in range(13, 18)] + [summed[18, :1], summed[19, :1]]

    return (
        layer_out,
        grad_tokens,
        grad_attn[:, :shard],
        grad_attn[:, shard : 2 * shard],
        grad_attn[:, 2 * shard : 3 * shard],
        grad_attn[:, 3 * shard :].T,
        grad_up,
        grad_down,
        *out_vectors,
    )


def solution(mesh):
    rows, weight, weight_t = P("dp", None), P("dp", "mp"), P("mp", "dp")
    placed = (rows,) * 7 + (weight,) * 3 + (weight_t, weight, weight_t) + (P(),) * 11
    return jax.shard_map(
        body,
        mesh=mesh,
        in_specs=placed,
        out_specs=(rows,) * 2
        + (weight,) * 3
        + (weight_t, weight, weight_t)
        + (P("mp"), P("mp"), P(), P("mp"))
        + (P(),) * 7,
        check_vma=False,
    )
```

```python
import functools

import jax
import jax.numpy as jnp
from jax import lax
from jax.experimental import pallas as pl
from jax.experimental.pallas import tpu as pltpu
from jax.sharding import PartitionSpec as P

HEAD_DIM = 64
HALO = 64
QUAD = 4 * HEAD_DIM
CHUNK = 208
EPSILON = 1e-06
MASKED = -1000000000.0
PRECISE = lax.Precision.HIGHEST
F32 = jnp.float32
BF16 = jnp.bfloat16
VMEM = pltpu.VMEM
SMEM = pltpu.SMEM
GROUPS = 4
LIMIT = dict(plane_parts=10, qkv=62, attend=62, attend_back=40, up=62, down=62, down_grad=16, up_grad=24, middle=20, input=62, attn_grad=62, z_parts=6, spread=16)


def _nt(a, b):
    return lax.dot_general(a, b, (((1,), (1,)), ((), ())), preferred_element_type=F32)


def _tn(a, b):
    return lax.dot_general(a, b, (((0,), (0,)), ((), ())), preferred_element_type=F32)


def _nn(a, b, precision=None):
    return lax.dot_general(
        a, b, (((1,), (0,)), ((), ())), precision=precision, preferred_element_type=F32
    )


def norm_parts(values):
    center = values - jnp.mean(values, axis=-1, keepdims=True)
    factor = lax.rsqrt(jnp.mean(center * center, axis=-1, keepdims=True) + EPSILON)
    return (center * factor, factor)


def norm_back(grad_rows, normed, factor, gain_vec):
    shaped = grad_rows * gain_vec
    first_mean = jnp.mean(shaped, axis=-1, keepdims=True)
    second_mean = jnp.mean(shaped * normed, axis=-1, keepdims=True)
    return factor * (shaped - first_mean - normed * second_mean)


def gelu_parts(u):
    k = 0.7978845608028654
    sq = u * u
    t = jnp.tanh(k * (u + 0.044715 * (sq * u)))
    half = 0.5 * (1.0 + t)
    slope = half + 0.5 * u * (1.0 - t * t) * (k * (1.0 + 3.0 * 0.044715 * sq))
    return u * half, slope


def col_sum(a):
    return jnp.sum(a, axis=0, keepdims=True)


def staged(kernel, spaces, n_out, *refs):
    n_in = len(spaces)
    moved = [i for i, c in enumerate(spaces) if c == "v"]
    ins, outs = list(refs[:n_in]), refs[n_in : n_in + n_out]
    rest = refs[n_in + n_out :]
    in_bufs, out_bufs = rest[: len(moved)], rest[len(moved) : len(moved) + n_out]
    sem = rest[len(moved) + n_out]
    copies = [
        pltpu.make_async_copy(ins[i], buf, sem.at[n]) for n, (i, buf) in enumerate(zip(moved, in_bufs))
    ]
    for c in copies:
        c.start()
    for c in copies:
        c.wait()
    for i, buf in zip(moved, in_bufs):
        ins[i] = buf
    kernel(*ins, *out_bufs, *rest[len(moved) + n_out + 1 :])
    copies = [
        pltpu.make_async_copy(buf, ref, sem.at[len(moved) + n])
        for n, (buf, ref) in enumerate(zip(out_bufs, outs))
    ]
    for c in copies:
        c.start()
    for c in copies:
        c.wait()


def run(kernel, name, outs, ins, spaces=None, scratch=()):
    spaces = spaces or "v" * len(ins)
    moved = [a for a, c in zip(ins, spaces) if c == "v"]
    hbm, smem = pl.BlockSpec(memory_space=pltpu.HBM), pl.BlockSpec(memory_space=SMEM)
    return pl.pallas_call(
        functools.partial(staged, kernel, spaces, len(outs)),
        out_shape=tuple(jax.ShapeDtypeStruct(s, d) for s, d in outs),
        in_specs=[smem if c == "s" else hbm for c in spaces],
        out_specs=tuple(hbm for _ in outs),
        scratch_shapes=[VMEM(a.shape, a.dtype) for a in moved]
        + [VMEM(s, d) for s, d in outs]
        + [pltpu.SemaphoreType.DMA((len(moved) + len(outs),))]
        + list(scratch),
        compiler_params=pltpu.CompilerParams(vmem_limit_bytes=LIMIT[name] << 20),
        name=name,
    )(*ins)


def copies_of(plan, rows, at_ref, refs, buf, sem):
    z, x = at_ref[0], at_ref[1]
    out = [[] for _ in range(GROUPS)]
    for n, (src, first, zrel, dx, group, col, cut, wide) in enumerate(plan):
        slot = pl.multiple_of(((z ^ zrel) * 2 + (x ^ dx)) * rows, rows)
        out[group].append(
            pltpu.make_async_copy(
                refs[src].at[(*first, pl.ds(0, rows), pl.ds(cut, wide))],
                buf.at[group, pl.ds(slot, rows), pl.ds(col, wide)],
                sem.at[n],
            )
        )
    return out


def whole_copies(ref, buf, sem):
    return [[pltpu.make_async_copy(ref.at[g], buf.at[g], sem.at[g])] for g in range(GROUPS)]


class Weights:
    def __init__(self, arrays, plan, rows, cols):
        self.arrays, self.plan, self.rows, self.cols = arrays, plan, rows, cols

    def scratch(self, width):
        count = GROUPS if self.plan is None else len(self.plan)
        return [VMEM((GROUPS, width, self.cols), BF16), pltpu.SemaphoreType.DMA((count,))]

    def copies(self, at_ref, refs, buf, sem):
        if self.plan is None:
            return whole_copies(refs[0], buf, sem)
        return copies_of(self.plan, self.rows, at_ref, refs, buf, sem)


def _head_masks(rows):
    lane = lax.broadcasted_iota(jnp.int32, (rows, QUAD), 1) // HEAD_DIM
    return [lane == h for h in range(4)]


def _stack_heads(block, masks):
    zero = jnp.zeros_like(block)
    return jnp.concatenate([jnp.where(m, block, zero) for m in masks], axis=0)


def _pick_heads(stacked, masks):
    rows = stacked.shape[0] // 4
    out = stacked[:rows]
    for h in range(1, 4):
        out = jnp.where(masks[h], stacked[h * rows : (h + 1) * rows], out)
    return out


def _probs(k_win, q_stack, allowed):
    scores = jnp.where(allowed, _nt(k_win, q_stack), MASKED)
    top = jnp.max(scores, axis=0, keepdims=True)
    e = jnp.exp(scores - top)
    return e * (1.0 / jnp.sum(e, axis=0, keepdims=True))


def _blocks(total):
    for b in range(total // HALO):
        first = min(max(b - 1, 0) * HALO, total - 3 * HALO)
        yield b, slice(b * HALO, (b + 1) * HALO), slice(first, first + 3 * HALO)


def _qkv_kernel(ws, width, shard, *refs):
    at_ref, x_ref, table_ref = refs[:3]
    pieces = refs[3 : 3 + len(ws.arrays)]
    h_ref, q_ref, k_ref, v_ref, wq_ref, wk_ref, wv_ref, wo_ref, buf, sem = refs[
        3 + len(ws.arrays) :
    ]
    copies = ws.copies(at_ref, pieces, buf, sem)
    for group in copies:
        for c in group:
            c.start()
    normed = norm_parts(x_ref[...].astype(F32))[0]
    h_ref[...] = (normed * table_ref[4:5, :] + table_ref[5:6, :]).astype(BF16)
    h = h_ref[...]
    for g in range(GROUPS):
        for c in copies[g]:
            c.wait()
        cols = slice(g * shard, (g + 1) * shard)
        r = _nn(h, buf[g])
        own = at_ref[2] ^ g
        q_bias, v_bias = (
            sum(
                jnp.where(own == j, table_ref[i : i + 1, j * shard : (j + 1) * shard], 0.0)
                for j in range(GROUPS)
            )
            for i in range(2)
        )
        q_ref[:, cols] = ((r[:, :shard] + q_bias) * HEAD_DIM ** (-0.5)).astype(BF16)
        k_ref[:, cols] = r[:, shard : 2 * shard].astype(BF16)
        v_ref[:, cols] = (r[:, 2 * shard : 3 * shard] + v_bias).astype(BF16)
        for i, ref in enumerate((wq_ref, wk_ref, wv_ref, wo_ref)):
            ref[:, cols] = buf[g, :, i * shard : (i + 1) * shard]


def _attend_kernel(
    q_ref, k_ref, v_ref, ids_ref, own_ref, wo_ref, x_ref, table_ref,
    o_ref, after_ref, h_ref,
):
    masks = _head_masks(HALO)
    for b, rows, window in _blocks(q_ref.shape[0]):
        allowed = ids_ref[window, :] == own_ref[b]
        for c in range(q_ref.shape[1] // QUAD):
            cols = slice(c * QUAD, (c + 1) * QUAD)
            q_stack = _stack_heads(q_ref[rows, cols], masks)
            p = _probs(k_ref[window, cols], q_stack, allowed).astype(BF16)
            o_ref[rows, cols] = _pick_heads(_tn(p, v_ref[window, cols]), masks).astype(BF16)
    after_ref[...] = x_ref[...].astype(F32) + _nt(o_ref[...], wo_ref[...]) + table_ref[2:3, :]
    normed = norm_parts(after_ref[...])[0]
    h_ref[...] = (normed * table_ref[6:7, :] + table_ref[7:8, :]).astype(BF16)


def _attend_back_kernel(
    q_ref, k_ref, v_ref, do_ref, ids_ref, own_ref, dq_ref, dk_ref, dv_ref, dk_acc, dv_acc
):
    masks = _head_masks(HALO)
    dk_acc[...] = jnp.zeros_like(dk_acc)
    dv_acc[...] = jnp.zeros_like(dv_acc)
    for b, rows, window in _blocks(q_ref.shape[0]):
        allowed = ids_ref[window, :] == own_ref[b]
        q_stack = _stack_heads(q_ref[rows, :], masks)
        do_stack = _stack_heads(do_ref[rows, :], masks)
        k_win = k_ref[window, :]
        p = _probs(k_win, q_stack, allowed)
        dp = _nt(v_ref[window, :], do_stack)
        ds = (p * (dp - jnp.sum(p * dp, axis=0, keepdims=True))).astype(BF16)
        dv_acc[window, :] += _nn(p.astype(BF16), do_stack)
        dk_acc[window, :] += _nn(ds, q_stack)
        dq_ref[rows, :] = _pick_heads(_tn(ds, k_win), masks).astype(BF16)
    dk_ref[...] = dk_acc[...].astype(BF16)
    dv_ref[...] = dv_acc[...].astype(BF16)


def _attend_back_columns(c, *refs):
    fq_ref, fk_ref = refs[4:6]
    outs, bufs, sem = refs[6:9], refs[9:13], refs[13]
    copies = [
        pltpu.make_async_copy(ref.at[:, pl.ds(c * QUAD, QUAD)], buf, sem.at[n])
        for n, (ref, buf) in enumerate(zip(refs[:4], bufs))
    ]
    for copy in copies:
        copy.start()
    for copy in copies:
        copy.wait()
    _attend_back_kernel(*bufs, fq_ref, fk_ref, *outs, *refs[14:])


def attend_back(q, k, v, do, fq, fk, c):
    rows = q.shape[0]
    return run(
        functools.partial(_attend_back_columns, c),
        "attend_back",
        [((rows, QUAD), BF16)] * 3,
        [q, k, v, do, fq, fk],
        "aaaavv",
        scratch=[VMEM((rows, QUAD), BF16)] * 4
        + [pltpu.SemaphoreType.DMA((4,))]
        + [VMEM((rows, QUAD), F32)] * 2,
    )


def _up_kernel(ws, *refs):
    at_ref, h_ref, b_ref = refs[:3]
    pieces = refs[3 : 3 + len(ws.arrays)]
    act_ref, slope_ref, w_ref, buf, sem = refs[3 + len(ws.arrays) :]
    g = pl.program_id(0)
    copies = ws.copies(at_ref, pieces, buf, sem)

    @pl.when(g == 0)
    def _():
        for group in copies:
            for c in group:
                c.start()

    for i in range(GROUPS):

        @pl.when(g == i)
        def _(i=i):
            for c in copies[i]:
                c.wait()

    w_ref[0] = buf[g]
    bias = b_ref[pl.ds(8 + (at_ref[2] ^ g), 1), :]
    for i in range(h_ref.shape[0] // CHUNK):
        rows = slice(i * CHUNK, (i + 1) * CHUNK)
        value, slope = gelu_parts(_nn(h_ref[rows, :], buf[g]) + bias)
        act_ref[0, rows, :] = value.astype(BF16)
        slope_ref[0, rows, :] = slope.astype(BF16)


def at_group(*shape):
    zeros = (0,) * (len(shape) - 1)
    return pl.BlockSpec((1,) + shape[1:], lambda g: (g,) + zeros)


def fixed(*shape):
    zeros = (0,) * len(shape)
    return pl.BlockSpec(shape, lambda g: zeros, pipeline_mode=pl.Buffered(1))


def up_stage(ws, at, h, bias):
    rows, width = h.shape
    hidden = ws.cols
    act = jax.ShapeDtypeStruct((GROUPS, rows, hidden), BF16)
    return pl.pallas_call(
        functools.partial(_up_kernel, ws),
        grid=(GROUPS,),
        out_shape=(act, act, jax.ShapeDtypeStruct((GROUPS, width, hidden), BF16)),
        in_specs=[pl.BlockSpec(memory_space=SMEM), fixed(rows, width), fixed(*bias.shape)]
        + [pl.BlockSpec(memory_space=pltpu.HBM)] * len(ws.arrays),
        out_specs=(
            at_group(GROUPS, rows, hidden),
            at_group(GROUPS, rows, hidden),
            at_group(GROUPS, width, hidden),
        ),
        scratch_shapes=ws.scratch(width),
        compiler_params=pltpu.CompilerParams(vmem_limit_bytes=LIMIT["up"] << 20),
        name="up",
    )(at, h, bias, *ws.arrays)


def _down_kernel(ws, total, images, *refs):
    (
        at_ref, last_ref, act_ref, after_ref, bias_ref, mine_ref, cot_ref, owned_ref, pairs_ref,
        scale_ref, logit_ref,
    ) = refs[:11]
    image_refs, refs = refs[11 : 11 + images], refs[11 + images :]
    pieces = refs[: len(ws.arrays)]
    out_ref, g_ref, low_ref, dbias_ref, dscale_ref, dlogit_ref, w_ref, buf, sem, acc, text_buf, image_buf, image_sem = refs[
        len(ws.arrays) :
    ]
    g = pl.program_id(0)
    copies = ws.copies(at_ref, pieces, buf, sem)
    if images == 1:
        pics = [pltpu.make_async_copy(image_refs[0], image_buf, image_sem.at[0])]
    else:
        many = image_refs[0].shape[1] - ws.rows
        pics = [
            pltpu.make_async_copy(
                image_refs[dx].at[zrel, pl.ds(ws.rows, many), pl.ds(0, image_buf.shape[1])],
                image_buf.at[
                    pl.ds(
                        pl.multiple_of(((at_ref[0] ^ zrel) * 2 + (at_ref[1] ^ dx)) * many, many),
                        many,
                    )
                ],
                image_sem.at[2 * zrel + dx],
            )
            for zrel in range(4)
            for dx in range(2)
        ]

    @pl.when(g == 0)
    def _():
        for group in copies:
            for c in group:
                c.start()
        for c in pics:
            c.start()
        acc[...] = after_ref[...] + bias_ref[3:4, :]

    for i in range(GROUPS):

        @pl.when(g == i)
        def _(i=i):
            for c in copies[i]:
                c.wait()

    w_ref[0] = buf[g]
    acc[...] += _nt(act_ref[0], buf[g])

    @pl.when(g == GROUPS - 1)
    def _():
        out_ref[...] = acc[...].astype(BF16)
        caps = text_buf.shape[0]
        for c in range(caps):
            text_buf[c : c + 1, :] = acc[pl.ds(last_ref[c], 1), :]
        mine = mine_ref[...]
        pooled = text_buf[...]
        text_scale = lax.rsqrt(jnp.sum(pooled * pooled, axis=1, keepdims=True) + EPSILON)
        text = pooled * text_scale
        for c in pics:
            c.wait()
        image = image_buf[...].astype(F32)
        image = image * lax.rsqrt(jnp.sum(image * image, axis=1, keepdims=True) + EPSILON)
        scale = jnp.exp(scale_ref[...])
        dots = lax.dot_general(
            text, image, (((1,), (1,)), ((), ())), precision=PRECISE, preferred_element_type=F32
        )
        sign = 2.0 * pairs_ref[...].astype(F32) - 1.0
        logits = scale * dots + logit_ref[...]
        d_logits = (-1.0 / total) * mine * sign / (1.0 + jnp.exp(sign * logits))
        dlogit_ref[...] = jnp.sum(d_logits, keepdims=True)
        dscale_ref[...] = jnp.sum(d_logits * (scale * dots), keepdims=True)
        d_text = scale * _nn(d_logits, image, PRECISE)
        d_pooled = text_scale * (d_text - text * jnp.sum(d_text * text, axis=1, keepdims=True))
        g_ref[...] = cot_ref[...].astype(F32) * owned_ref[...]
        text_buf[...] = d_pooled
        for c in range(caps):
            g_ref[pl.ds(last_ref[c], 1), :] += text_buf[c : c + 1, :]
        rows = g_ref[...]
        low_ref[...] = rows.astype(BF16)
        dbias_ref[...] = col_sum(rows)


def down_stage(ws, at, last_at, act, after, bias, mine, cot, owned, images, pairs, scale, logit, total):
    rows, width = after.shape
    hidden = ws.cols
    caps = mine.shape[0]
    one = jax.ShapeDtypeStruct((1, 1), F32)
    return pl.pallas_call(
        functools.partial(_down_kernel, ws, total, len(images)),
        grid=(GROUPS,),
        out_shape=(
            jax.ShapeDtypeStruct((rows, width), BF16),
            jax.ShapeDtypeStruct((rows, width), F32),
            jax.ShapeDtypeStruct((rows, width), BF16),
            jax.ShapeDtypeStruct((1, width), F32),
            one,
            one,
            jax.ShapeDtypeStruct((GROUPS, width, hidden), BF16),
        ),
        in_specs=[
            pl.BlockSpec(memory_space=SMEM),
            pl.BlockSpec(memory_space=SMEM),
            at_group(GROUPS, rows, hidden),
            fixed(rows, width),
            fixed(*bias.shape),
            fixed(caps, 1),
            fixed(rows, width),
            fixed(rows, 1),
            fixed(*pairs.shape),
            fixed(1, 1),
            fixed(1, 1),
        ]
        + [pl.BlockSpec(memory_space=pltpu.HBM)] * (len(images) + len(ws.arrays)),
        out_specs=(
            fixed(rows, width),
            fixed(rows, width),
            fixed(rows, width),
            fixed(1, width),
            fixed(1, 1),
            fixed(1, 1),
            at_group(GROUPS, width, hidden),
        ),
        scratch_shapes=ws.scratch(width) + [VMEM((rows, width), F32), VMEM((caps, width), F32), VMEM((pairs.shape[1], width), BF16), pltpu.SemaphoreType.DMA((8,))],
        compiler_params=pltpu.CompilerParams(vmem_limit_bytes=LIMIT["down"] << 20),
        name="down",
    )(
        at, last_at, act, after, bias, mine, cot, owned, pairs, scale.reshape(1, 1),
        logit.reshape(1, 1), *images, *ws.arrays,
    )


def _down_grad_kernel(low_ref, act_ref, give_ref, keep_ref):
    i = pl.program_id(0)
    grad = _tn(low_ref[...], act_ref[0]).astype(BF16)

    @pl.when(i < 2)
    def _():
        give_ref[0] = grad

    @pl.when(i >= 2)
    def _():
        keep_ref[0] = grad


def down_grad(low, act):
    rows, width = low.shape
    hidden = act.shape[2]
    out = jax.ShapeDtypeStruct((2, width, hidden), BF16)
    return pl.pallas_call(
        _down_grad_kernel,
        grid=(GROUPS,),
        out_shape=(out, out),
        in_specs=[
            fixed(rows, width),
            pl.BlockSpec((1, rows, hidden), lambda i: ((2 * i + 1) % 5, 0, 0)),
        ],
        out_specs=(
            pl.BlockSpec((1, width, hidden), lambda i: (jnp.minimum(i, 1), 0, 0)),
            pl.BlockSpec((1, width, hidden), lambda i: (jnp.maximum(i - 2, 0), 0, 0)),
        ),
        compiler_params=pltpu.CompilerParams(vmem_limit_bytes=LIMIT["down_grad"] << 20),
        name="down_grad",
    )(low, act)


def _up_grad_kernel(has_sum, low_ref, h_ref, slope_ref, wd_ref, wu_ref, *refs):
    i = pl.program_id(0)
    grad_ref, bias_ref, dh_ref, d_pre = refs[-4:]

    @pl.when(i == 0)
    def _():
        dh_ref[...] = refs[0][...] if has_sum else jnp.zeros_like(dh_ref)

    d_act = _nn(low_ref[...], wd_ref[0])
    d_pre[...] = (d_act * slope_ref[0].astype(F32)).astype(BF16)
    bias_ref[0] = col_sum(d_pre[...].astype(F32))
    grad_ref[0] = _tn(h_ref[...], d_pre[...]).astype(BF16)
    dh_ref[...] += _nt(d_pre[...], wu_ref[0])


def up_grad(low, h, slope, w_d, w_u, first, so_far=None):
    rows, width = low.shape
    hidden = slope.shape[2]

    def pair(a, b):
        return pl.BlockSpec((1, a, b), lambda i: (2 * i + first, 0, 0))

    extra = [] if so_far is None else [so_far]
    return pl.pallas_call(
        functools.partial(_up_grad_kernel, so_far is not None),
        grid=(2,),
        out_shape=(
            jax.ShapeDtypeStruct((2, width, hidden), BF16),
            jax.ShapeDtypeStruct((2, 1, hidden), F32),
            jax.ShapeDtypeStruct((rows, width), F32),
        ),
        in_specs=[
            fixed(rows, width),
            fixed(rows, width),
            pair(rows, hidden),
            pair(width, hidden),
            pair(width, hidden),
        ]
        + [fixed(rows, width)] * len(extra),
        out_specs=(
            at_group(2, width, hidden),
            at_group(2, 1, hidden),
            fixed(rows, width),
        ),
        scratch_shapes=[VMEM((rows, hidden), BF16)],
        compiler_params=pltpu.CompilerParams(vmem_limit_bytes=LIMIT["up_grad"] << 20),
        name="up_grad",
    )(low, h, slope, w_d, w_u, *extra)


def _middle_kernel(
    dh_ref, g_ref, after_ref, gain_ref, att_ref, wo_ref,
    after_grad_ref, datt_ref, ograd_ref, dgain_ref, dshift_ref, dob_ref,
):
    normed, factor = norm_parts(after_ref[...])
    dh = dh_ref[...]
    dgain_ref[...] = col_sum(dh * normed)
    dshift_ref[...] = col_sum(dh)
    d_after = g_ref[...] + norm_back(dh, normed, factor, gain_ref[6:7, :])
    after_grad_ref[...] = d_after
    dob_ref[...] = col_sum(d_after)
    low = d_after.astype(BF16)
    datt_ref[...] = _nn(low, wo_ref[...]).astype(BF16)
    ograd_ref[...] = _tn(low, att_ref[...]).astype(BF16)


def _input_kernel(quads, shard, *refs):
    dq, dk, dv = refs[:quads], refs[quads : 2 * quads], refs[2 * quads : 3 * quads]
    (
        wq_ref, wk_ref, wv_ref, after_grad_ref, x_ref, gain_ref, at_ref, up_a_ref, up_b_ref,
        ob_ref, db_ref, gain_two_ref, shift_two_ref, scale_ref, logit_ref,
    ) = refs[3 * quads : 3 * quads + 15]
    out_ref, vec_ref = refs[3 * quads + 15 :]
    vec_ref[...] = jnp.zeros_like(vec_ref)
    q_part = rest = None
    sums = ([], [])
    for c in range(quads):
        cols = slice(c * QUAD, (c + 1) * QUAD)
        terms = [_nt(d[c][...], w[:, cols]) for d, w in ((dq, wq_ref), (dk, wk_ref), (dv, wv_ref))]
        q_part = terms[0] if q_part is None else q_part + terms[0]
        both = terms[1] + terms[2]
        rest = both if rest is None else rest + both
        sums[0].append(col_sum(dq[c][...].astype(F32)) * HEAD_DIM ** (-0.5))
        sums[1].append(col_sum(dv[c][...].astype(F32)))
    me = at_ref[2]
    for i in range(2):
        whole = jnp.concatenate(sums[i], axis=1)
        for g in range(GROUPS):
            vec_ref[pl.ds(4 * i + (me ^ g), 1), :shard] = whole[:, g * shard : (g + 1) * shard]
    for g in range(GROUPS):
        ref = up_b_ref if g % 2 == 0 else up_a_ref
        vec_ref[pl.ds(8 + (me ^ g), 1), :] = ref[g // 2]
    dh = q_part * HEAD_DIM ** (-0.5) + rest
    normed, factor = norm_parts(x_ref[...].astype(F32))
    rows = [ob_ref[...], db_ref[...], col_sum(dh * normed), col_sum(dh)]
    rows += [gain_two_ref[...], shift_two_ref[...]]
    for i, v in enumerate(rows):
        vec_ref[12 + i : 13 + i, :] = v
    vec_ref[18:19, :1] = scale_ref[...]
    vec_ref[19:20, :1] = logit_ref[...]
    out_ref[...] = (after_grad_ref[...] + norm_back(dh, normed, factor, gain_ref[4:5, :])).astype(BF16)


def _attn_grad_kernel(quads, shard, *refs):
    h_ref, o_ref = refs[3 * quads : 3 * quads + 2]
    give_ref, keep_ref = refs[3 * quads + 2 :]
    place = {1: (give_ref, 0), 3: (give_ref, 1), 0: (keep_ref, 0), 2: (keep_ref, 1)}
    h = h_ref[...]
    for i in range(3):
        for c in range(quads):
            grad = _tn(h, refs[i * quads + c][...])
            if i == 0:
                grad = grad * HEAD_DIM ** (-0.5)
            grad = grad.astype(BF16)
            lo = c * QUAD
            while lo < (c + 1) * QUAD:
                g = lo // shard
                hi = min((g + 1) * shard, (c + 1) * QUAD)
                ref, slot = place[g]
                start = i * shard + lo - g * shard
                ref[slot, :, start : start + hi - lo] = grad[:, lo - c * QUAD : hi - c * QUAD]
                lo = hi
    for g in range(GROUPS):
        ref, slot = place[g]
        ref[slot, :, 3 * shard :] = o_ref[:, g * shard : (g + 1) * shard]


def _add(*vals):
    total = vals[0].astype(F32)
    for v in vals[1:]:
        total = total + v.astype(F32)
    return total.astype(BF16)


def _plane_kernel(at_ref, keep_ref, got_ref, *outs):
    for y in range(2):
        for dx in range(2):
            x = at_ref[1] ^ dx
            for z in range(keep_ref.shape[1]):
                outs[2 * y + dx][z] = _add(keep_ref[y, z, x], got_ref[y, z, x])


def _x_kernel(lo, hi, at_ref, keep_ref, got_ref, own_ref, give_ref):
    for dx, ref in enumerate((own_ref, give_ref)):
        x = at_ref[1] ^ dx
        for y in range(2):
            for z in range(keep_ref.shape[1]):
                ref[y, z] = _add(keep_ref[y, z, x, :, lo:hi], got_ref[y, z, x, :, lo:hi])


def _z_first_kernel(lo, hi, at_ref, keep_ref, got_ref, *outs):
    for j, ref in enumerate(outs):
        z = at_ref[0] ^ j
        for y in range(2):
            for x in range(2):
                ref[y, x] = _add(keep_ref[y, z, x, :, lo:hi], got_ref[y, z, x, :, lo:hi])


def by_block(mv, a):
    return a.reshape(2, mv.nz, 2, a.shape[1] // mv.n, a.shape[2])


def plane_parts(mv, keep, got):
    keep, got = by_block(mv, keep), by_block(mv, got)
    out = ((mv.nz,) + keep.shape[3:], BF16)
    return run(_plane_kernel, "plane_parts", [out] * 4, [mv.at, keep, got], "svv")


def x_parts(mv, keep, got, lo, hi):
    keep, got = by_block(mv, keep), by_block(mv, got)
    out = ((2, mv.nz, keep.shape[3], hi - lo), BF16)
    kernel = functools.partial(_x_kernel, lo, hi)
    return run(kernel, "plane_parts", [out] * 2, [mv.at, keep, got], "svv")


def z_first_parts(mv, keep, got, lo, hi):
    keep, got = by_block(mv, keep), by_block(mv, got)
    out = ((2, 2, keep.shape[3], hi - lo), BF16)
    kernel = functools.partial(_z_first_kernel, lo, hi)
    return run(kernel, "plane_parts", [out] * 4, [mv.at, keep, got], "svv")


def _z_kernel(count, at_ref, *refs):
    ins, outs = refs[:count], refs[count:]
    for j in range(4):
        b = at_ref[0] ^ j
        outs[j][...] = _add(*[r[b] for r in ins])


def _z_pair_kernel(at_ref, a_ref, b_ref, *outs):
    for j in range(4):
        b = at_ref[0] ^ j
        for y in range(2):
            outs[j][y] = _add(a_ref[y, b], b_ref[y, b])


def z_parts(mv, held):
    out = (held[0].shape[1:], BF16)
    kernel = functools.partial(_z_kernel, len(held))
    return run(kernel, "z_parts", [out] * 4, [mv.at, *held], "s" + "v" * len(held))


def z_pair_parts(mv, own, got):
    out = ((2,) + own.shape[2:], BF16)
    return run(_z_pair_kernel, "z_parts", [out] * 4, [mv.at, own, got], "svv")


def _x_last_kernel(at_ref, a_ref, b_ref, c_ref, d_ref, own_ref, give_ref):
    for dx, ref in enumerate((own_ref, give_ref)):
        x = at_ref[1] ^ dx
        for y in range(2):
            ref[y] = _add(a_ref[y, x], b_ref[y, x], c_ref[y, x], d_ref[y, x])


def x_last_parts(mv, held):
    out = ((2,) + held[0].shape[2:], BF16)
    return run(_x_last_kernel, "z_parts", [out] * 2, [mv.at, *held], "svvvv")


def _spread_kernel(piece, at_ref, keep_ref, *refs):
    out_ref = refs[-1]
    wins = [(refs[0],), (refs[1],), (refs[2], refs[3]), (refs[4], refs[5])]
    j = pl.program_id(0)
    here = j ^ at_ref[2]
    before = (j - 1) ^ at_ref[2]
    for i in range(4):

        @pl.when(here == i)
        def _(i=i):
            done = 0
            for ref in wins[i]:
                rows = min(ref.shape[0], piece - done)
                out_ref[done : done + rows, :] = ref[:rows, :].astype(out_ref.dtype)
                done += rows

    for i in range(4):

        @pl.when((before == i) & (j > 0))
        def _(i=i):
            ref = wins[i][-1]
            tail = ref[ref.shape[0] - HALO :, :].astype(out_ref.dtype)
            out_ref[:HALO, :] = jnp.where(keep_ref[0] > 0, out_ref[:HALO, :], tail)


def spread(at, keep, windows, piece, dtype):
    cols = windows[0].shape[1]
    return pl.pallas_call(
        functools.partial(_spread_kernel, piece),
        grid=(GROUPS,),
        out_shape=jax.ShapeDtypeStruct((GROUPS * piece, cols), dtype),
        in_specs=[pl.BlockSpec(memory_space=SMEM), at_group(GROUPS, HALO, 1)]
        + [fixed(*w.shape) for w in windows],
        out_specs=pl.BlockSpec((piece, cols), lambda j: (j, 0)),
        compiler_params=pltpu.CompilerParams(vmem_limit_bytes=LIMIT["spread"] << 20),
        name="spread",
    )(at, keep, *windows)


def _flip(a, axis, bit):
    n = lax.axis_size(axis)
    return lax.ppermute(a, axis, [(i, i ^ bit) for i in range(n)])


def fence(*trees):
    return lax.optimization_barrier(trees)


def add_low(a, b):
    return (a.astype(F32) + b.astype(F32)).astype(BF16)


class Moves:
    def __init__(self):
        self.n = lax.axis_size("dp")
        self.nz = self.n // 2
        at = lax.axis_index("dp")
        self.at = jnp.stack([at // 2, at % 2, lax.axis_index("mp")]).astype(jnp.int32)
        self.near = self.n == 8

    def z_all(self, a):
        return [a] + [_flip(a, "dp", 2 * j) for j in range(1, 4)]

    def cross_flip(self, a):
        return lax.ppermute(
            a,
            ("dp", "mp"),
            [(4 * d + m, 4 * (d ^ 1) + (m ^ 2)) for d in range(self.n) for m in range(4)],
        )

    def plane_all(self, a):
        return [a, _flip(a, "dp", 1), _flip(a, "mp", 2), self.cross_flip(a)]

    def core_all(self, parts):
        return [_flip(a, "mp", 1) for a in parts]

    def gather_far(self, a):
        mine = lax.all_gather(a, "dp", axis=0, tiled=True)
        far = _flip(mine, "mp", 2)
        whole = jnp.stack([mine, _flip(mine, "mp", 1), far, _flip(far, "mp", 1)])
        return Weights([whole], None, a.shape[0], a.shape[1])

    def to_core(self, give):
        return _flip(give, "mp", 1)

    def scatter_far(self, keep, got):
        both = add_low(keep, got)
        mine = add_low(both[0], _flip(both[1], "mp", 2))
        return lax.psum_scatter(mine, "dp", scatter_dimension=0, tiled=True).astype(F32)

    def plane_sides(self, parts):
        return [
            parts[0], _flip(parts[1], "dp", 1), _flip(parts[2], "mp", 2), self.cross_flip(parts[3]),
        ]

    def z_sides(self, parts):
        return [_flip(parts[j], "dp", 2 * j) for j in range(1, 4)]


PLANE = [(dx, dy) for dy in range(2) for dx in range(2)]


def z_then_plane(first, col, cut, wide):
    return [
        (first + 4 * core + i, (zrel,), zrel, dx, core + 2 * dy, col, cut, wide)
        for core in range(2)
        for i, (dx, dy) in enumerate(PLANE)
        for zrel in range(4)
    ]


def plane_then_z(first, col, cut, wide):
    return [
        (first + 4 * core + zrel, (i,), zrel, dx, core + 2 * dy, col, cut, wide)
        for core in range(2)
        for zrel in range(4)
        for i, (dx, dy) in enumerate(PLANE)
    ]


def body(
    tokens,
    out_cot,
    seg_ids,
    valid_mask,
    last_pos,
    pairs,
    images,
    q_weight,
    k_weight,
    v_weight,
    o_weight,
    up_weight,
    down_weight,
    q_bias,
    v_bias,
    o_bias,
    up_bias,
    down_bias,
    gain_one,
    shift_one,
    gain_two,
    shift_two,
    log_scale,
    logit_bias,
):
    mv = Moves()
    assert lax.axis_size("mp") == GROUPS
    row_count, seq_len = seg_ids.shape
    token_count, width = tokens.shape
    piece = token_count // GROUPS
    caption_total = pairs.shape[0] * mv.n
    at = lax.axis_index("mp")
    shard = q_weight.shape[1]
    hidden = up_weight.shape[1]
    block = q_weight.shape[0]
    quads = width // QUAD

    own_a = jnp.concatenate([q_weight, k_weight, v_weight, o_weight.T], axis=1)
    down_t = down_weight.T
    cut = QUAD
    if mv.near:
        a_z = mv.z_all(own_a)
        own_1 = jnp.concatenate([up_weight, down_t[:, :cut]], axis=1)
        own_1 = jnp.concatenate([own_1, jnp.pad(images, ((0, 0), (0, cut)))], axis=0)
        w2_plane = mv.plane_all(down_t[:, cut:])
        a_z, own_1, w2_plane = fence(a_z, own_1, w2_plane)
        a_here = jnp.stack(a_z)
        a_here, tokens, out_cot, seg_ids, valid_mask, last_pos, q_bias = fence(
            a_here, tokens, out_cot, seg_ids, valid_mask, last_pos, q_bias
        )
        a_plane = mv.plane_all(a_here)
        w1_z = mv.z_all(own_1)

    start = at * piece
    tail = jnp.minimum(start + piece, token_count - HALO)

    def window(a):
        return jnp.concatenate(
            [
                lax.dynamic_slice_in_dim(a, start, piece),
                lax.dynamic_slice_in_dim(a, tail, HALO),
            ],
            axis=0,
        )

    flat_at = jnp.arange(token_count, dtype=jnp.int32)
    caption_id = jnp.where(
        valid_mask.reshape(-1) > 0,
        (flat_at // seq_len) * (last_pos.shape[1] * 2) + seg_ids.reshape(-1),
        (1 << 20) + flat_at,
    )
    inside = at < GROUPS - 1
    ids = window(caption_id)
    tail_ids = jnp.where(inside, ids[piece:], -2 - jnp.arange(HALO, dtype=jnp.int32))
    ids = jnp.concatenate([ids[:piece], tail_ids])
    before = jnp.where(
        at > 0, lax.dynamic_index_in_dim(caption_id, jnp.maximum(start - 1, 0), keepdims=False), -1
    )
    owned = jnp.concatenate([ids[:piece] != before, (tail_ids == ids[piece - 1]) & inside])
    by_piece = caption_id.reshape(GROUPS, piece)
    last_before = jnp.concatenate([jnp.full((1,), -1, jnp.int32), by_piece[:-1, -1]])
    keep_head = (by_piece[:, :HALO] != last_before[:, None]).astype(F32)[:, :, None]
    count = piece + HALO
    places = start + jnp.arange(count, dtype=jnp.int32)
    fq = ids[:, None]
    blocks = count // HALO
    fk = jnp.concatenate([ids.reshape(blocks, HALO)] * 4, axis=1)[:, None, :]

    flat_last = (
        last_pos + seq_len * jnp.arange(row_count, dtype=jnp.int32)[:, None]
    ).reshape(-1)
    last_at = jnp.clip(flat_last - start, 0, count - 1)
    mine = jnp.any((flat_last[:, None] == places[None, :]) & owned[None, :], axis=1)
    mine = mine.astype(F32)[:, None]
    x_rows = window(tokens)
    cot = window(out_cot)
    owned_rows = owned.astype(F32)[:, None]

    table = jnp.concatenate(
        [q_bias, v_bias, o_bias, down_bias, gain_one, shift_one, gain_two, shift_two, up_bias]
    ).reshape(-1, width)
    if mv.near:
        small = (x_rows, cot, fq, fk, last_at, mine, owned_rows, keep_head, table)
        a_plane, w1_z, w2_plane, small = fence(a_plane, w1_z, w2_plane, small)
        x_rows, cot, fq, fk, last_at, mine, owned_rows, keep_head, table = small
        a_core = [mv.to_core(v) for v in a_plane]
        w_a = Weights(a_plane + a_core, z_then_plane(0, 0, 0, hidden), block, hidden)
        w1_here, w2_here = jnp.stack(w1_z), jnp.stack(w2_plane)
        w1_x, w1_y = _flip(w1_here, "dp", 1), _flip(w1_here, "mp", 2)
        w2_near = [_flip(w2_here, "dp", 2), _flip(w2_here, "dp", 4)]
    else:
        w_a, w_u, w_d = (mv.gather_far(v) for v in (own_a, up_weight, down_t))
        pics = [lax.all_gather(images, "dp", axis=0, tiled=True)]

    rows_low = ((count, width), BF16)
    square = ((width, width), BF16)
    h_one, queries, keys, vals, w_q, w_k, w_v, w_o = run(
        functools.partial(_qkv_kernel, w_a, width, shard),
        "qkv",
        [rows_low] * 4 + [square] * 4,
        [mv.at, x_rows, table, *w_a.arrays],
        "svv" + "a" * len(w_a.arrays),
        scratch=w_a.scratch(width),
    )
    if mv.near:
        queries, keys, vals, w1_here, w2_here, w1_x, w1_y, w2_near = fence(
            queries, keys, vals, w1_here, w2_here, w1_x, w1_y, w2_near
        )
        w1_cross, w2_last = mv.cross_flip(w1_here), _flip(w2_here, "dp", 6)
        w1_core = [mv.to_core(v) for v in (w1_here, w1_x, w1_y)]
    attended, after_attn, h_two = run(
        _attend_kernel,
        "attend",
        [rows_low, ((count, width), F32), rows_low],
        [queries, keys, vals, fq, fk, w_o, x_rows, table],
    )
    if mv.near:
        h_two, w1_cross, w2_last, w1_core = fence(h_two, w1_cross, w2_last, w1_core)
        pics = [w1_here, w1_x]
        w1_all = [w1_here, w1_x, w1_y, w1_cross, *w1_core, mv.to_core(w1_cross)]
        w_u = Weights(w1_all, z_then_plane(0, 0, 0, hidden), block, hidden)
        w2_all = [w2_here, *w2_near, w2_last]
        w2_all = w2_all + [mv.to_core(v) for v in w2_all]
    acts, slopes, w_up = up_stage(w_u, mv.at, h_two, table)
    if mv.near:
        w2_all, acts = fence(w2_all, acts)
        w_d = Weights(
            w1_all + w2_all,
            z_then_plane(0, 0, hidden, cut) + plane_then_z(8, cut, 0, hidden - cut),
            block,
            hidden,
        )
    out_low, g_rows, g_low, d_down_bias, d_scale, d_logit, w_down = down_stage(
        w_d, mv.at, last_at, acts, after_attn, table, mine, cot, owned_rows, pics, pairs,
        log_scale, logit_bias, caption_total,
    )

    split = count // 2
    out_near = _flip(out_low, "mp", 1)
    down_give, down_keep = down_grad(g_low, acts)
    down_give, down_keep, g_low, out_near = fence(down_give, down_keep, g_low, out_near)
    down_got = mv.to_core(down_give)
    out_a = _flip(out_low[:split], "mp", 2)
    up_give, up_bias_a, d_h_two = up_grad(g_low, h_two, slopes, w_down, w_up, 1)
    down_got, up_give, d_h_two, out_a = fence(down_got, up_give, d_h_two, out_a)
    up_got = mv.to_core(up_give)
    out_cross_a = _flip(out_a, "mp", 1)
    if mv.near:
        sent = plane_parts(mv, down_keep, down_got)
        sent, d_h_two = fence(sent, d_h_two)
        down_held = mv.plane_sides(sent)
    up_keep, up_bias_b, d_h_two = up_grad(g_low, h_two, slopes, w_down, w_up, 0, d_h_two)
    vec = ((1, width), F32)
    d_after, d_attended, o_grad, d_gain_two, d_shift_two, d_o_bias = run(
        _middle_kernel,
        "middle",
        [((count, width), F32), rows_low, square, vec, vec, vec],
        [d_h_two, g_rows, after_attn, table, attended, w_o],
    )
    parts = [attend_back(queries, keys, vals, d_attended, fq, fk, 0)]
    if mv.near:
        down_held, up_got, up_keep, parts, out_cross_a = fence(
            down_held, up_got, up_keep, parts, out_cross_a
        )
        down_sent = z_parts(mv, down_held)
        sent = plane_parts(mv, up_keep, up_got)
        down_sent, sent, d_attended = fence(down_sent, sent, d_attended)
        up_held = mv.plane_sides(sent)
        down_pieces = [down_sent[0]] + [_flip(down_sent[j], "dp", 2 * j) for j in (1, 2)]
    for c in range(1, quads):
        parts.append(attend_back(queries, keys, vals, d_attended, fq, fk, c))
    if mv.near:
        parts, up_held, down_pieces = fence(parts, up_held, down_pieces)
        sent = z_parts(mv, up_held)
        sent, parts = fence(sent, parts)
        up_pieces = [sent[0]] + mv.z_sides(sent)
        down_pieces.append(_flip(down_sent[3], "dp", 6))
    flat = [p[i] for i in range(3) for p in parts]
    d_tokens, summed = run(
        functools.partial(_input_kernel, quads, shard),
        "input",
        [rows_low, ((24, hidden), F32)],
        [
            *flat, w_q, w_k, w_v, d_after, x_rows, table, mv.at, up_bias_a, up_bias_b,
            d_o_bias, d_down_bias, d_gain_two, d_shift_two, d_scale, d_logit,
        ],
        "v" * (3 * quads + 6) + "s" + "v" * 8,
    )
    if mv.near:
        d_tokens, flat, summed, up_pieces, down_pieces, out_low = fence(
            d_tokens, flat, summed, up_pieces, down_pieces, out_low
        )
        summed = summed + _flip(summed, "mp", 1)
    out_b = _flip(out_low[split:], "mp", 2)
    attn_give, attn_keep = run(
        functools.partial(_attn_grad_kernel, quads, shard),
        "attn_grad",
        [((2, width, hidden), BF16)] * 2,
        [*flat, h_one, o_grad],
    )
    attn_give, attn_keep, summed, out_b, d_tokens = fence(
        attn_give, attn_keep, summed, out_b, d_tokens
    )
    attn_got = mv.to_core(attn_give)
    grad_near = _flip(d_tokens, "mp", 1)
    if mv.near:
        summed = mv.plane_all(summed)
        attn_got, grad_near, summed = fence(attn_got, grad_near, summed)
        cut = 2 * QUAD
        own_a, sent_a = x_parts(mv, attn_keep, attn_got, 0, cut)
        sent = z_first_parts(mv, attn_keep, attn_got, cut, hidden)
        sent_a, sent, d_tokens, out_b = fence(sent_a, sent, d_tokens, out_b)
        side_a = _flip(sent_a, "dp", 1)
        pieces_b = [sent[0]] + mv.z_sides(sent)
    far_a = _flip(d_tokens[:split], "mp", 2)
    out_cross_b = _flip(out_b, "mp", 1)

    def low_sum(pieces):
        return sum(v.astype(F32) for v in pieces)

    if mv.near:
        side_a, pieces_b, far_a, out_cross_b = fence(side_a, pieces_b, far_a, out_cross_b)
        sent = z_pair_parts(mv, own_a, side_a)
        own_b, sent_b = x_last_parts(mv, pieces_b)
        sent, sent_b, d_tokens, out_cross_b = fence(sent, sent_b, d_tokens, out_cross_b)
        pieces_a = [sent[0]] + mv.z_sides(sent)
        side_b = _flip(sent_b, "dp", 1)
    far_b = _flip(d_tokens[split:], "mp", 2)
    grad_cross_a = _flip(far_a, "mp", 1)
    layer_out = spread(
        mv.at, keep_head, [out_low, out_near, out_a, out_b, out_cross_a, out_cross_b], piece, BF16
    )
    if mv.near:
        pieces_a, side_b, far_b, grad_cross_a, summed, layer_out = fence(
            pieces_a, side_b, far_b, grad_cross_a, summed, layer_out
        )
        summed = mv.z_all((summed[0] + summed[1]) + (summed[2] + summed[3]))
        sum_a, sum_b = low_sum(pieces_a), low_sum([own_b, side_b])
        both = jnp.concatenate([sum_a, sum_b], axis=2)
        attn_far = _flip(both[1].astype(BF16), "mp", 2)
    else:
        summed = lax.psum(summed, ("dp", "mp"))
        grad_down = mv.scatter_far(down_keep, down_got).T
        grad_up = mv.scatter_far(up_keep, up_got)
        grad_attn = mv.scatter_far(attn_keep, attn_got)
    grad_cross_b = _flip(far_b, "mp", 1)
    grad_tokens = spread(
        mv.at, keep_head, [d_tokens, grad_near, far_a, far_b, grad_cross_a, grad_cross_b], piece, F32
    )
    if mv.near:
        grad_tokens, summed, attn_far = fence(grad_tokens, summed, attn_far)
        summed = (summed[0] + summed[1]) + (summed[2] + summed[3])
        grad_down = low_sum(down_pieces).T
        grad_up = low_sum(up_pieces)
        grad_attn = both[0] + attn_far.astype(F32)

    def mine_of(first):
        return lax.dynamic_index_in_dim(summed, first + at, 0, keepdims=False)

    out_vectors = [mine_of(0)[:shard], mine_of(4)[:shard], summed[12], mine_of(8)]
    out_vectors += [summed[i] for i in range(13, 18)] + [summed[18, :1], summed[19, :1]]

    return (
        layer_out,
        grad_tokens,
        grad_attn[:, :shard],
        grad_attn[:, shard : 2 * shard],
        grad_attn[:, 2 * shard : 3 * shard],
        grad_attn[:, 3 * shard :].T,
        grad_up,
        grad_down,
        *out_vectors,
    )


def solution(mesh):
    rows, weight, weight_t = P("dp", None), P("dp", "mp"), P("mp", "dp")
    placed = (rows,) * 7 + (weight,) * 3 + (weight_t, weight, weight_t) + (P(),) * 11
    return jax.shard_map(
        body,
        mesh=mesh,
        in_specs=placed,
        out_specs=(rows,) * 2
        + (weight,) * 3
        + (weight_t, weight, weight_t)
        + (P("mp"), P("mp"), P(), P("mp"))
        + (P(),) * 7,
        check_vma=False,
    )
```

```python
import functools

import jax
import jax.numpy as jnp
from jax import lax
from jax.experimental import pallas as pl
from jax.experimental.pallas import tpu as pltpu
from jax.sharding import PartitionSpec as P

HEAD_DIM = 64
HALO = 64
QUAD = 4 * HEAD_DIM
CHUNK = 208
EPSILON = 1e-06
MASKED = -1000000000.0
PRECISE = lax.Precision.HIGHEST
F32 = jnp.float32
BF16 = jnp.bfloat16
VMEM = pltpu.VMEM
SMEM = pltpu.SMEM
GROUPS = 4
LIMIT = dict(plane_parts=10, qkv=62, attend=62, attend_back=30, up=40, down=48, down_grad=16, up_grad=24, middle=20, input=30, attn_grad=40, z_parts=6, spread=16)


def _nt(a, b):
    return lax.dot_general(a, b, (((1,), (1,)), ((), ())), preferred_element_type=F32)


def _tn(a, b):
    return lax.dot_general(a, b, (((0,), (0,)), ((), ())), preferred_element_type=F32)


def _nn(a, b, precision=None):
    return lax.dot_general(
        a, b, (((1,), (0,)), ((), ())), precision=precision, preferred_element_type=F32
    )


def norm_parts(values):
    center = values - jnp.mean(values, axis=-1, keepdims=True)
    factor = lax.rsqrt(jnp.mean(center * center, axis=-1, keepdims=True) + EPSILON)
    return (center * factor, factor)


def norm_back(grad_rows, normed, factor, gain_vec):
    shaped = grad_rows * gain_vec
    first_mean = jnp.mean(shaped, axis=-1, keepdims=True)
    second_mean = jnp.mean(shaped * normed, axis=-1, keepdims=True)
    return factor * (shaped - first_mean - normed * second_mean)


def gelu_parts(u):
    k = 0.7978845608028654
    sq = u * u
    t = jnp.tanh(k * (u + 0.044715 * (sq * u)))
    half = 0.5 * (1.0 + t)
    slope = half + 0.5 * u * (1.0 - t * t) * (k * (1.0 + 3.0 * 0.044715 * sq))
    return u * half, slope


def col_sum(a):
    return jnp.sum(a, axis=0, keepdims=True)


def staged(kernel, spaces, n_out, early, *refs):
    n_in = len(spaces)
    moved = [i for i, c in enumerate(spaces) if c == "v"]
    ins, outs = list(refs[:n_in]), refs[n_in : n_in + n_out]
    rest = refs[n_in + n_out :]
    in_bufs, out_bufs = rest[: len(moved)], rest[len(moved) : len(moved) + n_out]
    sem = rest[len(moved) + n_out]
    rest = rest[len(moved) + n_out + 1 :]
    copies = [
        pltpu.make_async_copy(ins[i], buf, sem.at[n]) for n, (i, buf) in enumerate(zip(moved, in_bufs))
    ]
    for c in copies:
        c.start()
    own = [] if early is None else [early(*ins, *rest)]
    for c in copies:
        c.wait()
    for i, buf in zip(moved, in_bufs):
        ins[i] = buf
    kernel(*own, *ins, *out_bufs, *rest)
    copies = [
        pltpu.make_async_copy(buf, ref, sem.at[len(moved) + n])
        for n, (buf, ref) in enumerate(zip(out_bufs, outs))
    ]
    for c in copies:
        c.start()
    for c in copies:
        c.wait()


def run(kernel, name, outs, ins, spaces=None, scratch=(), early=None):
    spaces = spaces or "v" * len(ins)
    moved = [a for a, c in zip(ins, spaces) if c == "v"]
    hbm, smem = pl.BlockSpec(memory_space=pltpu.HBM), pl.BlockSpec(memory_space=SMEM)
    return pl.pallas_call(
        functools.partial(staged, kernel, spaces, len(outs), early),
        out_shape=tuple(jax.ShapeDtypeStruct(s, d) for s, d in outs),
        in_specs=[smem if c == "s" else hbm for c in spaces],
        out_specs=tuple(hbm for _ in outs),
        scratch_shapes=[VMEM(a.shape, a.dtype) for a in moved]
        + [VMEM(s, d) for s, d in outs]
        + [pltpu.SemaphoreType.DMA((len(moved) + len(outs),))]
        + list(scratch),
        compiler_params=pltpu.CompilerParams(vmem_limit_bytes=LIMIT[name] << 20),
        name=name,
    )(*ins)


def copies_of(plan, rows, at_ref, refs, buf, sem):
    z, x = at_ref[0], at_ref[1]
    out = [[] for _ in range(GROUPS)]
    for n, (src, first, zrel, dx, group, col, cut, wide) in enumerate(plan):
        slot = pl.multiple_of(((z ^ zrel) * 2 + (x ^ dx)) * rows, rows)
        out[group].append(
            pltpu.make_async_copy(
                refs[src].at[(*first, pl.ds(0, rows), pl.ds(cut, wide))],
                buf.at[group, pl.ds(slot, rows), pl.ds(col, wide)],
                sem.at[n],
            )
        )
    return out


def whole_copies(ref, buf, sem):
    return [[pltpu.make_async_copy(ref.at[g], buf.at[g], sem.at[g])] for g in range(GROUPS)]


class Weights:
    def __init__(self, arrays, plan, rows, cols):
        self.arrays, self.plan, self.rows, self.cols = arrays, plan, rows, cols

    def scratch(self, width):
        count = GROUPS if self.plan is None else len(self.plan)
        return [VMEM((GROUPS, width, self.cols), BF16), pltpu.SemaphoreType.DMA((count,))]

    def copies(self, at_ref, refs, buf, sem):
        if self.plan is None:
            return whole_copies(refs[0], buf, sem)
        return copies_of(self.plan, self.rows, at_ref, refs, buf, sem)


def _head_masks(rows):
    lane = lax.broadcasted_iota(jnp.int32, (rows, QUAD), 1) // HEAD_DIM
    return [lane == h for h in range(4)]


def _stack_heads(block, masks):
    zero = jnp.zeros_like(block)
    return jnp.concatenate([jnp.where(m, block, zero) for m in masks], axis=0)


def _pick_heads(stacked, masks):
    rows = stacked.shape[0] // 4
    out = stacked[:rows]
    for h in range(1, 4):
        out = jnp.where(masks[h], stacked[h * rows : (h + 1) * rows], out)
    return out


def _probs(k_win, q_stack, allowed):
    scores = jnp.where(allowed, _nt(k_win, q_stack), MASKED)
    top = jnp.max(scores, axis=0, keepdims=True)
    e = jnp.exp(scores - top)
    return e * (1.0 / jnp.sum(e, axis=0, keepdims=True))


def _blocks(total):
    for b in range(total // HALO):
        first = min(max(b - 1, 0) * HALO, total - 3 * HALO)
        yield b, slice(b * HALO, (b + 1) * HALO), slice(first, first + 3 * HALO)


def _qkv_early(ws, at_ref, x_ref, table_ref, *refs):
    copies = ws.copies(at_ref, refs[: len(ws.arrays)], *refs[len(ws.arrays) :])
    for group in copies:
        for c in group:
            c.start()
    return copies


def _qkv_kernel(ws, width, shard, copies, *refs):
    at_ref, x_ref, table_ref = refs[:3]
    h_ref, q_ref, k_ref, v_ref, wq_ref, wk_ref, wv_ref, wo_ref, buf, sem = refs[
        3 + len(ws.arrays) :
    ]
    normed = norm_parts(x_ref[...].astype(F32))[0]
    h_ref[...] = (normed * table_ref[4:5, :] + table_ref[5:6, :]).astype(BF16)
    h = h_ref[...]
    for g in range(GROUPS):
        for c in copies[g]:
            c.wait()
        cols = slice(g * shard, (g + 1) * shard)
        r = _nn(h, buf[g])
        own = at_ref[2] ^ g
        q_bias, v_bias = (
            sum(
                jnp.where(own == j, table_ref[i : i + 1, j * shard : (j + 1) * shard], 0.0)
                for j in range(GROUPS)
            )
            for i in range(2)
        )
        q_ref[:, cols] = ((r[:, :shard] + q_bias) * HEAD_DIM ** (-0.5)).astype(BF16)
        k_ref[:, cols] = r[:, shard : 2 * shard].astype(BF16)
        v_ref[:, cols] = (r[:, 2 * shard : 3 * shard] + v_bias).astype(BF16)
        for i, ref in enumerate((wq_ref, wk_ref, wv_ref, wo_ref)):
            ref[:, cols] = buf[g, :, i * shard : (i + 1) * shard]


def _attend_kernel(
    q_ref, k_ref, v_ref, ids_ref, own_ref, wo_ref, x_ref, table_ref,
    o_ref, after_ref, h_ref,
):
    masks = _head_masks(HALO)
    for b, rows, window in _blocks(q_ref.shape[0]):
        allowed = ids_ref[window, :] == own_ref[b]
        for c in range(q_ref.shape[1] // QUAD):
            cols = slice(c * QUAD, (c + 1) * QUAD)
            q_stack = _stack_heads(q_ref[rows, cols], masks)
            p = _probs(k_ref[window, cols], q_stack, allowed).astype(BF16)
            o_ref[rows, cols] = _pick_heads(_tn(p, v_ref[window, cols]), masks).astype(BF16)
    after_ref[...] = x_ref[...].astype(F32) + _nt(o_ref[...], wo_ref[...]) + table_ref[2:3, :]
    normed = norm_parts(after_ref[...])[0]
    h_ref[...] = (normed * table_ref[6:7, :] + table_ref[7:8, :]).astype(BF16)


def _attend_back_kernel(
    q_ref, k_ref, v_ref, do_ref, ids_ref, own_ref, dq_ref, dk_ref, dv_ref, dk_acc, dv_acc
):
    masks = _head_masks(HALO)
    dk_acc[...] = jnp.zeros_like(dk_acc)
    dv_acc[...] = jnp.zeros_like(dv_acc)
    for b, rows, window in _blocks(q_ref.shape[0]):
        allowed = ids_ref[window, :] == own_ref[b]
        q_stack = _stack_heads(q_ref[rows, :], masks)
        do_stack = _stack_heads(do_ref[rows, :], masks)
        k_win = k_ref[window, :]
        p = _probs(k_win, q_stack, allowed)
        dp = _nt(v_ref[window, :], do_stack)
        ds = (p * (dp - jnp.sum(p * dp, axis=0, keepdims=True))).astype(BF16)
        dv_acc[window, :] += _nn(p.astype(BF16), do_stack)
        dk_acc[window, :] += _nn(ds, q_stack)
        dq_ref[rows, :] = _pick_heads(_tn(ds, k_win), masks).astype(BF16)
    dk_ref[...] = dk_acc[...].astype(BF16)
    dv_ref[...] = dv_acc[...].astype(BF16)


def _columns_early(c, *refs):
    copies = [
        pltpu.make_async_copy(ref.at[:, pl.ds(c * QUAD, QUAD)], buf, refs[10].at[n])
        for n, (ref, buf) in enumerate(zip(refs[:4], refs[6:10]))
    ]
    for copy in copies:
        copy.start()
    return copies


def _attend_back_columns(copies, *refs):
    for copy in copies:
        copy.wait()
    _attend_back_kernel(*refs[9:13], *refs[4:6], *refs[6:9], *refs[14:])


def attend_back(q, k, v, do, fq, fk, c):
    rows = q.shape[0]
    return run(
        _attend_back_columns,
        "attend_back",
        [((rows, QUAD), BF16)] * 3,
        [q, k, v, do, fq, fk],
        "aaaavv",
        scratch=[VMEM((rows, QUAD), BF16)] * 4
        + [pltpu.SemaphoreType.DMA((4,))]
        + [VMEM((rows, QUAD), F32)] * 2,
        early=functools.partial(_columns_early, c),
    )


def _up_kernel(ws, *refs):
    at_ref, h_ref, b_ref = refs[:3]
    pieces = refs[3 : 3 + len(ws.arrays)]
    act_ref, slope_ref, w_ref, buf, sem = refs[3 + len(ws.arrays) :]
    g = pl.program_id(0)
    copies = ws.copies(at_ref, pieces, buf, sem)

    @pl.when(g == 0)
    def _():
        for group in copies:
            for c in group:
                c.start()

    for i in range(GROUPS):

        @pl.when(g == i)
        def _(i=i):
            for c in copies[i]:
                c.wait()

    w_ref[0] = buf[g]
    bias = b_ref[pl.ds(8 + (at_ref[2] ^ g), 1), :]
    for i in range(h_ref.shape[0] // CHUNK):
        rows = slice(i * CHUNK, (i + 1) * CHUNK)
        value, slope = gelu_parts(_nn(h_ref[rows, :], buf[g]) + bias)
        act_ref[0, rows, :] = value.astype(BF16)
        slope_ref[0, rows, :] = slope.astype(BF16)


def at_group(*shape):
    zeros = (0,) * (len(shape) - 1)
    return pl.BlockSpec((1,) + shape[1:], lambda g: (g,) + zeros)


def fixed(*shape):
    zeros = (0,) * len(shape)
    return pl.BlockSpec(shape, lambda g: zeros, pipeline_mode=pl.Buffered(1))


def up_stage(ws, at, h, bias):
    rows, width = h.shape
    hidden = ws.cols
    act = jax.ShapeDtypeStruct((GROUPS, rows, hidden), BF16)
    return pl.pallas_call(
        functools.partial(_up_kernel, ws),
        grid=(GROUPS,),
        out_shape=(act, act, jax.ShapeDtypeStruct((GROUPS, width, hidden), BF16)),
        in_specs=[pl.BlockSpec(memory_space=SMEM), fixed(rows, width), fixed(*bias.shape)]
        + [pl.BlockSpec(memory_space=pltpu.HBM)] * len(ws.arrays),
        out_specs=(
            at_group(GROUPS, rows, hidden),
            at_group(GROUPS, rows, hidden),
            at_group(GROUPS, width, hidden),
        ),
        scratch_shapes=ws.scratch(width),
        compiler_params=pltpu.CompilerParams(vmem_limit_bytes=LIMIT["up"] << 20),
        name="up",
    )(at, h, bias, *ws.arrays)


def _down_kernel(ws, total, images, *refs):
    (
        at_ref, last_ref, act_ref, after_ref, bias_ref, mine_ref, cot_ref, owned_ref, pairs_ref,
        scale_ref, logit_ref,
    ) = refs[:11]
    image_refs, refs = refs[11 : 11 + images], refs[11 + images :]
    pieces = refs[: len(ws.arrays)]
    out_ref, g_ref, low_ref, dbias_ref, dscale_ref, dlogit_ref, w_ref, give_ref, keep_ref, buf, sem, acc, text_buf, image_buf, image_sem = refs[
        len(ws.arrays) :
    ]
    g = pl.program_id(0)
    copies = ws.copies(at_ref, pieces, buf, sem)
    if images == 1:
        pics = [pltpu.make_async_copy(image_refs[0], image_buf, image_sem.at[0])]
    else:
        many = image_refs[0].shape[1] - ws.rows
        pics = [
            pltpu.make_async_copy(
                image_refs[dx].at[zrel, pl.ds(ws.rows, many), pl.ds(0, image_buf.shape[1])],
                image_buf.at[
                    pl.ds(
                        pl.multiple_of(((at_ref[0] ^ zrel) * 2 + (at_ref[1] ^ dx)) * many, many),
                        many,
                    )
                ],
                image_sem.at[2 * zrel + dx],
            )
            for zrel in range(4)
            for dx in range(2)
        ]

    @pl.when(g == 0)
    def _():
        for group in copies:
            for c in group:
                c.start()
        for c in pics:
            c.start()
        acc[...] = after_ref[...] + bias_ref[3:4, :]

    for i in range(GROUPS):

        @pl.when(g == i)
        def _(i=i):
            for c in copies[i]:
                c.wait()

    @pl.when(g < GROUPS)
    def _():
        w_ref[0] = buf[g]
        acc[...] += _nt(act_ref[0], buf[g])

    @pl.when(g == GROUPS - 1)
    def _():
        out_ref[...] = acc[...].astype(BF16)
        caps = text_buf.shape[0]
        for c in range(caps):
            text_buf[c : c + 1, :] = acc[pl.ds(last_ref[c], 1), :]
        mine = mine_ref[...]
        pooled = text_buf[...]
        text_scale = lax.rsqrt(jnp.sum(pooled * pooled, axis=1, keepdims=True) + EPSILON)
        text = pooled * text_scale
        for c in pics:
            c.wait()
        image = image_buf[...].astype(F32)
        image = image * lax.rsqrt(jnp.sum(image * image, axis=1, keepdims=True) + EPSILON)
        scale = jnp.exp(scale_ref[...])
        dots = lax.dot_general(
            text, image, (((1,), (1,)), ((), ())), precision=PRECISE, preferred_element_type=F32
        )
        sign = 2.0 * pairs_ref[...].astype(F32) - 1.0
        logits = scale * dots + logit_ref[...]
        d_logits = (-1.0 / total) * mine * sign / (1.0 + jnp.exp(sign * logits))
        dlogit_ref[...] = jnp.sum(d_logits, keepdims=True)
        dscale_ref[...] = jnp.sum(d_logits * (scale * dots), keepdims=True)
        d_text = scale * _nn(d_logits, image, PRECISE)
        d_pooled = text_scale * (d_text - text * jnp.sum(d_text * text, axis=1, keepdims=True))
        g_ref[...] = cot_ref[...].astype(F32) * owned_ref[...]
        text_buf[...] = d_pooled
        for c in range(caps):
            g_ref[pl.ds(last_ref[c], 1), :] += text_buf[c : c + 1, :]
        rows = g_ref[...]
        low_ref[...] = rows.astype(BF16)
        dbias_ref[...] = col_sum(rows)

    @pl.when((g >= GROUPS) & (g < GROUPS + 2))
    def _():
        give_ref[0] = _tn(low_ref[...], act_ref[0]).astype(BF16)

    @pl.when(g >= GROUPS + 2)
    def _():
        keep_ref[0] = _tn(low_ref[...], act_ref[0]).astype(BF16)


def down_stage(ws, at, last_at, act, after, bias, mine, cot, owned, images, pairs, scale, logit, total):
    rows, width = after.shape
    hidden = ws.cols
    caps = mine.shape[0]
    one = jax.ShapeDtypeStruct((1, 1), F32)
    pair = jax.ShapeDtypeStruct((2, width, hidden), BF16)

    def visit(i):
        return jnp.where(i < GROUPS, i, (2 * (i - GROUPS) + 1) % 5)

    return pl.pallas_call(
        functools.partial(_down_kernel, ws, total, len(images)),
        grid=(2 * GROUPS,),
        out_shape=(
            jax.ShapeDtypeStruct((rows, width), BF16),
            jax.ShapeDtypeStruct((rows, width), F32),
            jax.ShapeDtypeStruct((rows, width), BF16),
            jax.ShapeDtypeStruct((1, width), F32),
            one,
            one,
            jax.ShapeDtypeStruct((GROUPS, width, hidden), BF16),
            pair,
            pair,
        ),
        in_specs=[
            pl.BlockSpec(memory_space=SMEM),
            pl.BlockSpec(memory_space=SMEM),
            pl.BlockSpec((1, rows, hidden), lambda i: (visit(i), 0, 0)),
            fixed(rows, width),
            fixed(*bias.shape),
            fixed(caps, 1),
            fixed(rows, width),
            fixed(rows, 1),
            fixed(*pairs.shape),
            fixed(1, 1),
            fixed(1, 1),
        ]
        + [pl.BlockSpec(memory_space=pltpu.HBM)] * (len(images) + len(ws.arrays)),
        out_specs=(
            fixed(rows, width),
            fixed(rows, width),
            fixed(rows, width),
            fixed(1, width),
            fixed(1, 1),
            fixed(1, 1),
            pl.BlockSpec((1, width, hidden), lambda i: (jnp.minimum(i, GROUPS - 1), 0, 0)),
            pl.BlockSpec((1, width, hidden), lambda i: (jnp.clip(i - GROUPS, 0, 1), 0, 0)),
            pl.BlockSpec((1, width, hidden), lambda i: (jnp.clip(i - GROUPS - 2, 0, 1), 0, 0)),
        ),
        scratch_shapes=ws.scratch(width) + [VMEM((rows, width), F32), VMEM((caps, width), F32), VMEM((pairs.shape[1], width), BF16), pltpu.SemaphoreType.DMA((8,))],
        compiler_params=pltpu.CompilerParams(vmem_limit_bytes=LIMIT["down"] << 20),
        name="down",
    )(
        at, last_at, act, after, bias, mine, cot, owned, pairs, scale.reshape(1, 1),
        logit.reshape(1, 1), *images, *ws.arrays,
    )


def _up_grad_kernel(has_sum, low_ref, h_ref, slope_ref, wd_ref, wu_ref, *refs):
    i = pl.program_id(0)
    grad_ref, bias_ref, dh_ref, d_pre = refs[-4:]

    @pl.when(i == 0)
    def _():
        dh_ref[...] = refs[0][...] if has_sum else jnp.zeros_like(dh_ref)

    d_act = _nn(low_ref[...], wd_ref[0])
    d_pre[...] = (d_act * slope_ref[0].astype(F32)).astype(BF16)
    bias_ref[0] = col_sum(d_pre[...].astype(F32))
    grad_ref[0] = _tn(h_ref[...], d_pre[...]).astype(BF16)
    dh_ref[...] += _nt(d_pre[...], wu_ref[0])


def up_grad(low, h, slope, w_d, w_u, first, so_far=None):
    rows, width = low.shape
    hidden = slope.shape[2]

    def pair(a, b):
        return pl.BlockSpec((1, a, b), lambda i: (2 * i + first, 0, 0))

    extra = [] if so_far is None else [so_far]
    return pl.pallas_call(
        functools.partial(_up_grad_kernel, so_far is not None),
        grid=(2,),
        out_shape=(
            jax.ShapeDtypeStruct((2, width, hidden), BF16),
            jax.ShapeDtypeStruct((2, 1, hidden), F32),
            jax.ShapeDtypeStruct((rows, width), F32),
        ),
        in_specs=[
            fixed(rows, width),
            fixed(rows, width),
            pair(rows, hidden),
            pair(width, hidden),
            pair(width, hidden),
        ]
        + [fixed(rows, width)] * len(extra),
        out_specs=(
            at_group(2, width, hidden),
            at_group(2, 1, hidden),
            fixed(rows, width),
        ),
        scratch_shapes=[VMEM((rows, hidden), BF16)],
        compiler_params=pltpu.CompilerParams(vmem_limit_bytes=LIMIT["up_grad"] << 20),
        name="up_grad",
    )(low, h, slope, w_d, w_u, *extra)


def _middle_kernel(
    dh_ref, g_ref, after_ref, gain_ref, att_ref, wo_ref,
    after_grad_ref, datt_ref, ograd_ref, dgain_ref, dshift_ref, dob_ref,
):
    normed, factor = norm_parts(after_ref[...])
    dh = dh_ref[...]
    dgain_ref[...] = col_sum(dh * normed)
    dshift_ref[...] = col_sum(dh)
    d_after = g_ref[...] + norm_back(dh, normed, factor, gain_ref[6:7, :])
    after_grad_ref[...] = d_after
    dob_ref[...] = col_sum(d_after)
    low = d_after.astype(BF16)
    datt_ref[...] = _nn(low, wo_ref[...]).astype(BF16)
    ograd_ref[...] = _tn(low, att_ref[...]).astype(BF16)


def _input_early(quads, *refs):
    d_buf, w_buf, sem = refs[-3:]
    width = quads * QUAD
    copies = [
        pltpu.make_async_copy(refs[n], d_buf.at[:, pl.ds(n * QUAD, QUAD)], sem.at[n])
        for n in range(3 * quads)
    ]
    copies += [
        pltpu.make_async_copy(
            refs[3 * quads + n], w_buf.at[:, pl.ds(n * width, width)], sem.at[3 * quads + n]
        )
        for n in range(3)
    ]
    for c in copies:
        c.start()
    return copies


def _input_kernel(quads, shard, copies, *refs):
    (
        after_grad_ref, x_ref, table_ref, at_ref, up_a_ref, up_b_ref,
        ob_ref, db_ref, gain_two_ref, shift_two_ref, scale_ref, logit_ref,
    ) = refs[3 * quads + 3 : 3 * quads + 15]
    out_ref, vec_ref, d_buf, w_buf, sem = refs[3 * quads + 15 :]
    width = quads * QUAD
    normed, factor = norm_parts(x_ref[...].astype(F32))
    for c in copies:
        c.wait()
    d_buf[:, :width] = d_buf[:, :width] * HEAD_DIM ** (-0.5)
    dh = _nt(d_buf[...], w_buf[...])
    vec_ref[...] = jnp.zeros_like(vec_ref)
    me = at_ref[2]
    for i, first in enumerate((0, 2 * width)):
        whole = col_sum(d_buf[:, first : first + width].astype(F32))
        for g in range(GROUPS):
            vec_ref[pl.ds(4 * i + (me ^ g), 1), :shard] = whole[:, g * shard : (g + 1) * shard]
    for g in range(GROUPS):
        ref = up_b_ref if g % 2 == 0 else up_a_ref
        vec_ref[pl.ds(8 + (me ^ g), 1), :] = ref[g // 2]
    rows = [ob_ref[...], db_ref[...], col_sum(dh * normed), col_sum(dh)]
    rows += [gain_two_ref[...], shift_two_ref[...]]
    for i, v in enumerate(rows):
        vec_ref[12 + i : 13 + i, :] = v
    vec_ref[18:19, :1] = scale_ref[...]
    vec_ref[19:20, :1] = logit_ref[...]
    out_ref[...] = (after_grad_ref[...] + norm_back(dh, normed, factor, table_ref[4:5, :])).astype(
        BF16
    )


def _attn_grad_kernel(quads, shard, *refs):
    h_ref, o_ref = refs[3 * quads : 3 * quads + 2]
    give_ref, keep_ref = refs[3 * quads + 2 :]
    place = {1: (give_ref, 0), 3: (give_ref, 1), 0: (keep_ref, 0), 2: (keep_ref, 1)}
    h = h_ref[...]
    for i in range(3):
        for c in range(quads):
            grad = _tn(h, refs[i * quads + c][...])
            if i == 0:
                grad = grad * HEAD_DIM ** (-0.5)
            grad = grad.astype(BF16)
            lo = c * QUAD
            while lo < (c + 1) * QUAD:
                g = lo // shard
                hi = min((g + 1) * shard, (c + 1) * QUAD)
                ref, slot = place[g]
                start = i * shard + lo - g * shard
                ref[slot, :, start : start + hi - lo] = grad[:, lo - c * QUAD : hi - c * QUAD]
                lo = hi
    for g in range(GROUPS):
        ref, slot = place[g]
        ref[slot, :, 3 * shard :] = o_ref[:, g * shard : (g + 1) * shard]


def _add(*vals):
    total = vals[0].astype(F32)
    for v in vals[1:]:
        total = total + v.astype(F32)
    return total.astype(BF16)


def _plane_kernel(at_ref, keep_ref, got_ref, *outs):
    for y in range(2):
        for dx in range(2):
            x = at_ref[1] ^ dx
            for z in range(keep_ref.shape[1]):
                outs[2 * y + dx][z] = _add(keep_ref[y, z, x], got_ref[y, z, x])


def _x_kernel(lo, hi, at_ref, keep_ref, got_ref, own_ref, give_ref):
    for dx, ref in enumerate((own_ref, give_ref)):
        x = at_ref[1] ^ dx
        for y in range(2):
            for z in range(keep_ref.shape[1]):
                ref[y, z] = _add(keep_ref[y, z, x, :, lo:hi], got_ref[y, z, x, :, lo:hi])


def _z_first_kernel(lo, hi, at_ref, keep_ref, got_ref, *outs):
    for j, ref in enumerate(outs):
        z = at_ref[0] ^ j
        for y in range(2):
            for x in range(2):
                ref[y, x] = _add(keep_ref[y, z, x, :, lo:hi], got_ref[y, z, x, :, lo:hi])


def by_block(mv, a):
    return a.reshape(2, mv.nz, 2, a.shape[1] // mv.n, a.shape[2])


def plane_parts(mv, keep, got):
    keep, got = by_block(mv, keep), by_block(mv, got)
    out = ((mv.nz,) + keep.shape[3:], BF16)
    return run(_plane_kernel, "plane_parts", [out] * 4, [mv.at, keep, got], "svv")


def x_parts(mv, keep, got, lo, hi):
    keep, got = by_block(mv, keep), by_block(mv, got)
    out = ((2, mv.nz, keep.shape[3], hi - lo), BF16)
    kernel = functools.partial(_x_kernel, lo, hi)
    return run(kernel, "plane_parts", [out] * 2, [mv.at, keep, got], "svv")


def z_first_parts(mv, keep, got, lo, hi):
    keep, got = by_block(mv, keep), by_block(mv, got)
    out = ((2, 2, keep.shape[3], hi - lo), BF16)
    kernel = functools.partial(_z_first_kernel, lo, hi)
    return run(kernel, "plane_parts", [out] * 4, [mv.at, keep, got], "svv")


def _z_kernel(count, at_ref, *refs):
    ins, outs = refs[:count], refs[count:]
    for j in range(4):
        b = at_ref[0] ^ j
        outs[j][...] = _add(*[r[b] for r in ins])


def _z_pair_kernel(at_ref, a_ref, b_ref, *outs):
    for j in range(4):
        b = at_ref[0] ^ j
        for y in range(2):
            outs[j][y] = _add(a_ref[y, b], b_ref[y, b])


def z_parts(mv, held):
    out = (held[0].shape[1:], BF16)
    kernel = functools.partial(_z_kernel, len(held))
    return run(kernel, "z_parts", [out] * 4, [mv.at, *held], "s" + "v" * len(held))


def z_pair_parts(mv, own, got):
    out = ((2,) + own.shape[2:], BF16)
    return run(_z_pair_kernel, "z_parts", [out] * 4, [mv.at, own, got], "svv")


def _x_last_kernel(at_ref, a_ref, b_ref, c_ref, d_ref, own_ref, give_ref):
    for dx, ref in enumerate((own_ref, give_ref)):
        x = at_ref[1] ^ dx
        for y in range(2):
            ref[y] = _add(a_ref[y, x], b_ref[y, x], c_ref[y, x], d_ref[y, x])


def x_last_parts(mv, held):
    out = ((2,) + held[0].shape[2:], BF16)
    return run(_x_last_kernel, "z_parts", [out] * 2, [mv.at, *held], "svvvv")


def _spread_kernel(piece, at_ref, keep_ref, *refs):
    out_ref = refs[-1]
    wins = [(refs[0],), (refs[1],), (refs[2], refs[3]), (refs[4], refs[5])]
    j = pl.program_id(0)
    here = j ^ at_ref[2]
    before = (j - 1) ^ at_ref[2]
    for i in range(4):

        @pl.when(here == i)
        def _(i=i):
            done = 0
            for ref in wins[i]:
                rows = min(ref.shape[0], piece - done)
                out_ref[done : done + rows, :] = ref[:rows, :].astype(out_ref.dtype)
                done += rows

    for i in range(4):

        @pl.when((before == i) & (j > 0))
        def _(i=i):
            ref = wins[i][-1]
            tail = ref[ref.shape[0] - HALO :, :].astype(out_ref.dtype)
            out_ref[:HALO, :] = jnp.where(keep_ref[0] > 0, out_ref[:HALO, :], tail)


def spread(at, keep, windows, piece, dtype):
    cols = windows[0].shape[1]
    return pl.pallas_call(
        functools.partial(_spread_kernel, piece),
        grid=(GROUPS,),
        out_shape=jax.ShapeDtypeStruct((GROUPS * piece, cols), dtype),
        in_specs=[pl.BlockSpec(memory_space=SMEM), at_group(GROUPS, HALO, 1)]
        + [fixed(*w.shape) for w in windows],
        out_specs=pl.BlockSpec((piece, cols), lambda j: (j, 0)),
        compiler_params=pltpu.CompilerParams(vmem_limit_bytes=LIMIT["spread"] << 20),
        name="spread",
    )(at, keep, *windows)


def _flip(a, axis, bit):
    n = lax.axis_size(axis)
    return lax.ppermute(a, axis, [(i, i ^ bit) for i in range(n)])


def fence(*trees):
    return lax.optimization_barrier(trees)


def add_low(a, b):
    return (a.astype(F32) + b.astype(F32)).astype(BF16)


class Moves:
    def __init__(self):
        self.n = lax.axis_size("dp")
        self.nz = self.n // 2
        at = lax.axis_index("dp")
        self.at = jnp.stack([at // 2, at % 2, lax.axis_index("mp")]).astype(jnp.int32)
        self.near = self.n == 8

    def z_all(self, a):
        return [a] + [_flip(a, "dp", 2 * j) for j in range(1, 4)]

    def cross_flip(self, a):
        return lax.ppermute(
            a,
            ("dp", "mp"),
            [(4 * d + m, 4 * (d ^ 1) + (m ^ 2)) for d in range(self.n) for m in range(4)],
        )

    def plane_all(self, a):
        return [a, _flip(a, "dp", 1), _flip(a, "mp", 2), self.cross_flip(a)]

    def core_all(self, parts):
        return [_flip(a, "mp", 1) for a in parts]

    def gather_far(self, a):
        mine = lax.all_gather(a, "dp", axis=0, tiled=True)
        far = _flip(mine, "mp", 2)
        whole = jnp.stack([mine, _flip(mine, "mp", 1), far, _flip(far, "mp", 1)])
        return Weights([whole], None, a.shape[0], a.shape[1])

    def to_core(self, give):
        return _flip(give, "mp", 1)

    def scatter_far(self, keep, got):
        both = add_low(keep, got)
        mine = add_low(both[0], _flip(both[1], "mp", 2))
        return lax.psum_scatter(mine, "dp", scatter_dimension=0, tiled=True).astype(F32)

    def plane_sides(self, parts):
        return [
            parts[0], _flip(parts[1], "dp", 1), _flip(parts[2], "mp", 2), self.cross_flip(parts[3]),
        ]

    def z_sides(self, parts):
        return [_flip(parts[j], "dp", 2 * j) for j in range(1, 4)]


PLANE = [(dx, dy) for dy in range(2) for dx in range(2)]


def z_then_plane(first, col, cut, wide):
    return [
        (first + 4 * core + i, (zrel,), zrel, dx, core + 2 * dy, col, cut, wide)
        for core in range(2)
        for i, (dx, dy) in enumerate(PLANE)
        for zrel in range(4)
    ]


def plane_then_z(first, col, cut, wide):
    return [
        (first + 4 * core + zrel, (i,), zrel, dx, core + 2 * dy, col, cut, wide)
        for core in range(2)
        for zrel in range(4)
        for i, (dx, dy) in enumerate(PLANE)
    ]


def body(
    tokens,
    out_cot,
    seg_ids,
    valid_mask,
    last_pos,
    pairs,
    images,
    q_weight,
    k_weight,
    v_weight,
    o_weight,
    up_weight,
    down_weight,
    q_bias,
    v_bias,
    o_bias,
    up_bias,
    down_bias,
    gain_one,
    shift_one,
    gain_two,
    shift_two,
    log_scale,
    logit_bias,
):
    mv = Moves()
    assert lax.axis_size("mp") == GROUPS
    row_count, seq_len = seg_ids.shape
    token_count, width = tokens.shape
    piece = token_count // GROUPS
    caption_total = pairs.shape[0] * mv.n
    at = lax.axis_index("mp")
    shard = q_weight.shape[1]
    hidden = up_weight.shape[1]
    block = q_weight.shape[0]
    quads = width // QUAD

    own_a = jnp.concatenate([q_weight, k_weight, v_weight, o_weight.T], axis=1)
    down_t = down_weight.T
    cut = QUAD
    if mv.near:
        a_z = mv.z_all(own_a)
        a_z[1], up_weight, down_t, images = fence(a_z[1], up_weight, down_t, images)
        own_1 = jnp.concatenate([up_weight, down_t[:, :cut]], axis=1)
        own_1 = jnp.concatenate([own_1, jnp.pad(images, ((0, 0), (0, cut)))], axis=0)
        w2_plane = mv.plane_all(down_t[:, cut:])
        a_z, own_1, w2_plane = fence(a_z, own_1, w2_plane)
        a_here = jnp.stack(a_z)
        a_here, tokens, out_cot, seg_ids, valid_mask, last_pos, q_bias = fence(
            a_here, tokens, out_cot, seg_ids, valid_mask, last_pos, q_bias
        )
        a_plane = mv.plane_all(a_here)
        w1_z = mv.z_all(own_1)

    start = at * piece
    tail = jnp.minimum(start + piece, token_count - HALO)

    def window(a):
        return jnp.concatenate(
            [
                lax.dynamic_slice_in_dim(a, start, piece),
                lax.dynamic_slice_in_dim(a, tail, HALO),
            ],
            axis=0,
        )

    flat_at = jnp.arange(token_count, dtype=jnp.int32)
    caption_id = jnp.where(
        valid_mask.reshape(-1) > 0,
        (flat_at // seq_len) * (last_pos.shape[1] * 2) + seg_ids.reshape(-1),
        (1 << 20) + flat_at,
    )
    inside = at < GROUPS - 1
    ids = window(caption_id)
    tail_ids = jnp.where(inside, ids[piece:], -2 - jnp.arange(HALO, dtype=jnp.int32))
    ids = jnp.concatenate([ids[:piece], tail_ids])
    before = jnp.where(
        at > 0, lax.dynamic_index_in_dim(caption_id, jnp.maximum(start - 1, 0), keepdims=False), -1
    )
    owned = jnp.concatenate([ids[:piece] != before, (tail_ids == ids[piece - 1]) & inside])
    by_piece = caption_id.reshape(GROUPS, piece)
    last_before = jnp.concatenate([jnp.full((1,), -1, jnp.int32), by_piece[:-1, -1]])
    keep_head = (by_piece[:, :HALO] != last_before[:, None]).astype(F32)[:, :, None]
    count = piece + HALO
    places = start + jnp.arange(count, dtype=jnp.int32)
    fq = ids[:, None]
    blocks = count // HALO
    fk = jnp.concatenate([ids.reshape(blocks, HALO)] * 4, axis=1)[:, None, :]

    flat_last = (
        last_pos + seq_len * jnp.arange(row_count, dtype=jnp.int32)[:, None]
    ).reshape(-1)
    last_at = jnp.clip(flat_last - start, 0, count - 1)
    mine = jnp.any((flat_last[:, None] == places[None, :]) & owned[None, :], axis=1)
    mine = mine.astype(F32)[:, None]
    x_rows = window(tokens)
    cot = window(out_cot)
    owned_rows = owned.astype(F32)[:, None]

    table = jnp.concatenate(
        [q_bias, v_bias, o_bias, down_bias, gain_one, shift_one, gain_two, shift_two, up_bias]
    ).reshape(-1, width)
    if mv.near:
        small = (x_rows, cot, fq, fk, last_at, mine, owned_rows, keep_head, table)
        a_plane, w1_z, w2_plane, small = fence(a_plane, w1_z, w2_plane, small)
        x_rows, cot, fq, fk, last_at, mine, owned_rows, keep_head, table = small
        a_core = [mv.to_core(v) for v in a_plane]
        w_a = Weights(a_plane + a_core, z_then_plane(0, 0, 0, hidden), block, hidden)
        w1_here, w2_here = jnp.stack(w1_z), jnp.stack(w2_plane)
        w1_x, w1_y = _flip(w1_here, "dp", 1), _flip(w1_here, "mp", 2)
        w2_near = [_flip(w2_here, "dp", 2), _flip(w2_here, "dp", 4)]
    else:
        w_a, w_u, w_d = (mv.gather_far(v) for v in (own_a, up_weight, down_t))
        pics = [lax.all_gather(images, "dp", axis=0, tiled=True)]

    rows_low = ((count, width), BF16)
    square = ((width, width), BF16)
    h_one, queries, keys, vals, w_q, w_k, w_v, w_o = run(
        functools.partial(_qkv_kernel, w_a, width, shard),
        "qkv",
        [rows_low] * 4 + [square] * 4,
        [mv.at, x_rows, table, *w_a.arrays],
        "svv" + "a" * len(w_a.arrays),
        scratch=w_a.scratch(width),
        early=functools.partial(_qkv_early, w_a),
    )
    if mv.near:
        queries, keys, vals, w1_here, w2_here, w1_x, w1_y, w2_near = fence(
            queries, keys, vals, w1_here, w2_here, w1_x, w1_y, w2_near
        )
        w1_cross, w2_last = mv.cross_flip(w1_here), _flip(w2_here, "dp", 6)
        w1_core = [mv.to_core(v) for v in (w1_here, w1_x, w1_y)]
    attended, after_attn, h_two = run(
        _attend_kernel,
        "attend",
        [rows_low, ((count, width), F32), rows_low],
        [queries, keys, vals, fq, fk, w_o, x_rows, table],
    )
    if mv.near:
        h_two, w1_cross, w2_last, w1_core = fence(h_two, w1_cross, w2_last, w1_core)
        pics = [w1_here, w1_x]
        w1_all = [w1_here, w1_x, w1_y, w1_cross, *w1_core, mv.to_core(w1_cross)]
        w_u = Weights(w1_all, z_then_plane(0, 0, 0, hidden), block, hidden)
        w2_all = [w2_here, *w2_near, w2_last]
        w2_all = w2_all + [mv.to_core(v) for v in w2_all]
    acts, slopes, w_up = up_stage(w_u, mv.at, h_two, table)
    if mv.near:
        w2_all, acts = fence(w2_all, acts)
        w_d = Weights(
            w1_all + w2_all,
            z_then_plane(0, 0, hidden, cut) + plane_then_z(8, cut, 0, hidden - cut),
            block,
            hidden,
        )
    out_low, g_rows, g_low, d_down_bias, d_scale, d_logit, w_down, down_give, down_keep = down_stage(
        w_d, mv.at, last_at, acts, after_attn, table, mine, cot, owned_rows, pics, pairs,
        log_scale, logit_bias, caption_total,
    )

    split = count // 2
    down_got = mv.to_core(down_give)
    out_a = _flip(out_low[:split], "mp", 2)
    up_give, up_bias_a, d_h_two = up_grad(g_low, h_two, slopes, w_down, w_up, 1)
    down_got, up_give, d_h_two, out_a = fence(down_got, up_give, d_h_two, out_a)
    up_got = mv.to_core(up_give)
    out_cross_a, out_near = _flip(out_a, "mp", 1), _flip(out_low, "mp", 1)
    if mv.near:
        sent = plane_parts(mv, down_keep, down_got)
        sent, d_h_two = fence(sent, d_h_two)
        down_held = mv.plane_sides(sent)
    up_keep, up_bias_b, d_h_two = up_grad(g_low, h_two, slopes, w_down, w_up, 0, d_h_two)
    vec = ((1, width), F32)
    d_after, d_attended, o_grad, d_gain_two, d_shift_two, d_o_bias = run(
        _middle_kernel,
        "middle",
        [((count, width), F32), rows_low, square, vec, vec, vec],
        [d_h_two, g_rows, after_attn, table, attended, w_o],
    )
    parts = [attend_back(queries, keys, vals, d_attended, fq, fk, 0)]
    if mv.near:
        sent = plane_parts(mv, up_keep, up_got)
        down_held, sent, parts, out_cross_a, out_near = fence(
            down_held, sent, parts, out_cross_a, out_near
        )
        down_sent = z_parts(mv, down_held)
        down_sent, sent, d_attended = fence(down_sent, sent, d_attended)
        up_held = mv.plane_sides(sent)
        down_pieces = [down_sent[0]] + [_flip(down_sent[j], "dp", 2 * j) for j in (1, 2)]
    for c in range(1, quads):
        parts.append(attend_back(queries, keys, vals, d_attended, fq, fk, c))
    if mv.near:
        parts, up_held, down_pieces = fence(parts, up_held, down_pieces)
        sent = z_parts(mv, up_held)
        sent, parts = fence(sent, parts)
        up_pieces = [sent[0]] + mv.z_sides(sent)
        down_pieces.append(_flip(down_sent[3], "dp", 6))
    flat = [p[i] for i in range(3) for p in parts]
    d_tokens, summed = run(
        functools.partial(_input_kernel, quads, shard),
        "input",
        [rows_low, ((24, hidden), F32)],
        [
            *flat, w_q, w_k, w_v, d_after, x_rows, table, mv.at, up_bias_a, up_bias_b,
            d_o_bias, d_down_bias, d_gain_two, d_shift_two, d_scale, d_logit,
        ],
        "a" * (3 * quads + 3) + "vvvs" + "v" * 8,
        scratch=[
            VMEM((count, 3 * width), BF16),
            VMEM((width, 3 * width), BF16),
            pltpu.SemaphoreType.DMA((3 * quads + 3,)),
        ],
        early=functools.partial(_input_early, quads),
    )
    if mv.near:
        d_tokens, flat, summed, up_pieces, down_pieces, out_low = fence(
            d_tokens, flat, summed, up_pieces, down_pieces, out_low
        )
        summed = summed + _flip(summed, "mp", 1)
    out_b = _flip(out_low[split:], "mp", 2)
    attn_give, attn_keep = run(
        functools.partial(_attn_grad_kernel, quads, shard),
        "attn_grad",
        [((2, width, hidden), BF16)] * 2,
        [*flat, h_one, o_grad],
    )
    attn_give, attn_keep, summed, out_b, d_tokens = fence(
        attn_give, attn_keep, summed, out_b, d_tokens
    )
    attn_got = mv.to_core(attn_give)
    grad_near = _flip(d_tokens, "mp", 1)
    if mv.near:
        summed = mv.plane_all(summed)
        attn_got, grad_near, summed = fence(attn_got, grad_near, summed)
        cut = 2 * QUAD
        own_a, sent_a = x_parts(mv, attn_keep, attn_got, 0, cut)
        sent = z_first_parts(mv, attn_keep, attn_got, cut, hidden)
        sent_a, sent, d_tokens, out_b = fence(sent_a, sent, d_tokens, out_b)
        side_a = _flip(sent_a, "dp", 1)
        pieces_b = [sent[0]] + mv.z_sides(sent)
    far_a = _flip(d_tokens[:split], "mp", 2)
    out_cross_b = _flip(out_b, "mp", 1)

    def low_sum(pieces):
        return sum(v.astype(F32) for v in pieces)

    if mv.near:
        side_a, pieces_b, far_a, out_cross_b = fence(side_a, pieces_b, far_a, out_cross_b)
        sent = z_pair_parts(mv, own_a, side_a)
        own_b, sent_b = x_last_parts(mv, pieces_b)
        sent, sent_b, d_tokens, out_cross_b = fence(sent, sent_b, d_tokens, out_cross_b)
        pieces_a = [sent[0]] + mv.z_sides(sent)
        side_b = _flip(sent_b, "dp", 1)
    far_b = _flip(d_tokens[split:], "mp", 2)
    grad_cross_a = _flip(far_a, "mp", 1)
    layer_out = spread(
        mv.at, keep_head, [out_low, out_near, out_a, out_b, out_cross_a, out_cross_b], piece, BF16
    )
    if mv.near:
        pieces_a, side_b, far_b, grad_cross_a, summed, layer_out = fence(
            pieces_a, side_b, far_b, grad_cross_a, summed, layer_out
        )
        summed = mv.z_all((summed[0] + summed[1]) + (summed[2] + summed[3]))
        sum_a, sum_b = low_sum(pieces_a), low_sum([own_b, side_b])
        both = jnp.concatenate([sum_a, sum_b], axis=2)
        attn_far = _flip(both[1].astype(BF16), "mp", 2)
    else:
        summed = lax.psum(summed, ("dp", "mp"))
        grad_down = mv.scatter_far(down_keep, down_got).T
        grad_up = mv.scatter_far(up_keep, up_got)
        grad_attn = mv.scatter_far(attn_keep, attn_got)
    grad_cross_b = _flip(far_b, "mp", 1)
    grad_tokens = spread(
        mv.at, keep_head, [d_tokens, grad_near, far_a, far_b, grad_cross_a, grad_cross_b], piece, F32
    )
    if mv.near:
        grad_tokens, summed, attn_far = fence(grad_tokens, summed, attn_far)
        summed = (summed[0] + summed[1]) + (summed[2] + summed[3])
        grad_down = low_sum(down_pieces).T
        grad_up = low_sum(up_pieces)
        grad_attn = both[0] + attn_far.astype(F32)

    def mine_of(first):
        return lax.dynamic_index_in_dim(summed, first + at, 0, keepdims=False)

    out_vectors = [mine_of(0)[:shard], mine_of(4)[:shard], summed[12], mine_of(8)]
    out_vectors += [summed[i] for i in range(13, 18)] + [summed[18, :1], summed[19, :1]]

    return (
        layer_out,
        grad_tokens,
        grad_attn[:, :shard],
        grad_attn[:, shard : 2 * shard],
        grad_attn[:, 2 * shard : 3 * shard],
        grad_attn[:, 3 * shard :].T,
        grad_up,
        grad_down,
        *out_vectors,
    )


def solution(mesh):
    rows, weight, weight_t = P("dp", None), P("dp", "mp"), P("mp", "dp")
    placed = (rows,) * 7 + (weight,) * 3 + (weight_t, weight, weight_t) + (P(),) * 11
    return jax.shard_map(
        body,
        mesh=mesh,
        in_specs=placed,
        out_specs=(rows,) * 2
        + (weight,) * 3
        + (weight_t, weight, weight_t)
        + (P("mp"), P("mp"), P(), P("mp"))
        + (P(),) * 7,
        check_vma=False,
    )
```

```python
import functools

import jax
import jax.numpy as jnp
from jax import lax
from jax.experimental import pallas as pl
from jax.experimental.pallas import tpu as pltpu
from jax.sharding import PartitionSpec as P

HEAD_DIM = 64
HALO = 64
QUAD = 4 * HEAD_DIM
CHUNK = 208
EPSILON = 1e-06
MASKED = -1000000000.0
PRECISE = lax.Precision.HIGHEST
F32 = jnp.float32
BF16 = jnp.bfloat16
VMEM = pltpu.VMEM
SMEM = pltpu.SMEM
GROUPS = 4
LIMIT = dict(plane_parts=10, qkv=62, attend=62, attend_back=30, up=40, down=48, down_grad=16, up_grad=24, middle=20, input=30, attn_grad=40, z_parts=6, spread=16)


def _nt(a, b):
    return lax.dot_general(a, b, (((1,), (1,)), ((), ())), preferred_element_type=F32)


def _tn(a, b):
    return lax.dot_general(a, b, (((0,), (0,)), ((), ())), preferred_element_type=F32)


def _nn(a, b, precision=None):
    return lax.dot_general(
        a, b, (((1,), (0,)), ((), ())), precision=precision, preferred_element_type=F32
    )


def norm_parts(values):
    center = values - jnp.mean(values, axis=-1, keepdims=True)
    factor = lax.rsqrt(jnp.mean(center * center, axis=-1, keepdims=True) + EPSILON)
    return (center * factor, factor)


def norm_back(grad_rows, normed, factor, gain_vec):
    shaped = grad_rows * gain_vec
    first_mean = jnp.mean(shaped, axis=-1, keepdims=True)
    second_mean = jnp.mean(shaped * normed, axis=-1, keepdims=True)
    return factor * (shaped - first_mean - normed * second_mean)


def gelu_parts(u):
    k = 0.7978845608028654
    sq = u * u
    t = jnp.tanh(k * (u + 0.044715 * (sq * u)))
    half = 0.5 * (1.0 + t)
    slope = half + 0.5 * u * (1.0 - t * t) * (k * (1.0 + 3.0 * 0.044715 * sq))
    return u * half, slope


def col_sum(a):
    return jnp.sum(a, axis=0, keepdims=True)


def staged(kernel, spaces, n_out, early, *refs):
    n_in = len(spaces)
    moved = [i for i, c in enumerate(spaces) if c == "v"]
    ins, outs = list(refs[:n_in]), refs[n_in : n_in + n_out]
    rest = refs[n_in + n_out :]
    in_bufs, out_bufs = rest[: len(moved)], rest[len(moved) : len(moved) + n_out]
    sem = rest[len(moved) + n_out]
    rest = rest[len(moved) + n_out + 1 :]
    copies = [
        pltpu.make_async_copy(ins[i], buf, sem.at[n]) for n, (i, buf) in enumerate(zip(moved, in_bufs))
    ]
    for c in copies:
        c.start()
    own = [] if early is None else [early(*ins, *rest)]
    for c in copies:
        c.wait()
    for i, buf in zip(moved, in_bufs):
        ins[i] = buf
    kernel(*own, *ins, *out_bufs, *rest)
    copies = [
        pltpu.make_async_copy(buf, ref, sem.at[len(moved) + n])
        for n, (buf, ref) in enumerate(zip(out_bufs, outs))
    ]
    for c in copies:
        c.start()
    for c in copies:
        c.wait()


def run(kernel, name, outs, ins, spaces=None, scratch=(), early=None):
    spaces = spaces or "v" * len(ins)
    moved = [a for a, c in zip(ins, spaces) if c == "v"]
    hbm, smem = pl.BlockSpec(memory_space=pltpu.HBM), pl.BlockSpec(memory_space=SMEM)
    return pl.pallas_call(
        functools.partial(staged, kernel, spaces, len(outs), early),
        out_shape=tuple(jax.ShapeDtypeStruct(s, d) for s, d in outs),
        in_specs=[smem if c == "s" else hbm for c in spaces],
        out_specs=tuple(hbm for _ in outs),
        scratch_shapes=[VMEM(a.shape, a.dtype) for a in moved]
        + [VMEM(s, d) for s, d in outs]
        + [pltpu.SemaphoreType.DMA((len(moved) + len(outs),))]
        + list(scratch),
        compiler_params=pltpu.CompilerParams(vmem_limit_bytes=LIMIT[name] << 20),
        name=name,
    )(*ins)


def copies_of(plan, rows, at_ref, refs, buf, sem):
    z, x = at_ref[0], at_ref[1]
    out = [[] for _ in range(GROUPS)]
    for n, (src, first, zrel, dx, group, col, cut, wide) in enumerate(plan):
        slot = pl.multiple_of(((z ^ zrel) * 2 + (x ^ dx)) * rows, rows)
        out[group].append(
            pltpu.make_async_copy(
                refs[src].at[(*first, pl.ds(0, rows), pl.ds(cut, wide))],
                buf.at[group, pl.ds(slot, rows), pl.ds(col, wide)],
                sem.at[n],
            )
        )
    return out


def whole_copies(ref, buf, sem):
    return [[pltpu.make_async_copy(ref.at[g], buf.at[g], sem.at[g])] for g in range(GROUPS)]


class Weights:
    def __init__(self, arrays, plan, rows, cols):
        self.arrays, self.plan, self.rows, self.cols = arrays, plan, rows, cols

    def scratch(self, width):
        count = GROUPS if self.plan is None else len(self.plan)
        return [VMEM((GROUPS, width, self.cols), BF16), pltpu.SemaphoreType.DMA((count,))]

    def copies(self, at_ref, refs, buf, sem):
        if self.plan is None:
            return whole_copies(refs[0], buf, sem)
        return copies_of(self.plan, self.rows, at_ref, refs, buf, sem)


def _head_masks(rows):
    lane = lax.broadcasted_iota(jnp.int32, (rows, QUAD), 1) // HEAD_DIM
    return [lane == h for h in range(4)]


def _stack_heads(block, masks):
    zero = jnp.zeros_like(block)
    return jnp.concatenate([jnp.where(m, block, zero) for m in masks], axis=0)


def _pick_heads(stacked, masks):
    rows = stacked.shape[0] // 4
    out = stacked[:rows]
    for h in range(1, 4):
        out = jnp.where(masks[h], stacked[h * rows : (h + 1) * rows], out)
    return out


def _probs(k_win, q_stack, allowed):
    scores = jnp.where(allowed, _nt(k_win, q_stack), MASKED)
    top = jnp.max(scores, axis=0, keepdims=True)
    e = jnp.exp(scores - top)
    return e * (1.0 / jnp.sum(e, axis=0, keepdims=True))


def _blocks(total):
    for b in range(total // HALO):
        first = min(max(b - 1, 0) * HALO, total - 3 * HALO)
        yield b, slice(b * HALO, (b + 1) * HALO), slice(first, first + 3 * HALO)


def _qkv_early(ws, at_ref, x_ref, table_ref, *refs):
    copies = ws.copies(at_ref, refs[: len(ws.arrays)], *refs[len(ws.arrays) :])
    for group in copies:
        for c in group:
            c.start()
    return copies


def _qkv_kernel(ws, width, shard, copies, *refs):
    at_ref, x_ref, table_ref = refs[:3]
    h_ref, q_ref, k_ref, v_ref, wq_ref, wk_ref, wv_ref, wo_ref, buf, sem = refs[
        3 + len(ws.arrays) :
    ]
    normed = norm_parts(x_ref[...].astype(F32))[0]
    h_ref[...] = (normed * table_ref[4:5, :] + table_ref[5:6, :]).astype(BF16)
    h = h_ref[...]
    for g in range(GROUPS):
        for c in copies[g]:
            c.wait()
        cols = slice(g * shard, (g + 1) * shard)
        r = _nn(h, buf[g])
        own = at_ref[2] ^ g
        q_bias, v_bias = (
            sum(
                jnp.where(own == j, table_ref[i : i + 1, j * shard : (j + 1) * shard], 0.0)
                for j in range(GROUPS)
            )
            for i in range(2)
        )
        q_ref[:, cols] = ((r[:, :shard] + q_bias) * HEAD_DIM ** (-0.5)).astype(BF16)
        k_ref[:, cols] = r[:, shard : 2 * shard].astype(BF16)
        v_ref[:, cols] = (r[:, 2 * shard : 3 * shard] + v_bias).astype(BF16)
        for i, ref in enumerate((wq_ref, wk_ref, wv_ref, wo_ref)):
            ref[:, cols] = buf[g, :, i * shard : (i + 1) * shard]


def _attend_kernel(
    q_ref, k_ref, v_ref, ids_ref, own_ref, wo_ref, x_ref, table_ref,
    o_ref, after_ref, h_ref,
):
    masks = _head_masks(HALO)
    for b, rows, window in _blocks(q_ref.shape[0]):
        allowed = ids_ref[window, :] == own_ref[b]
        for c in range(q_ref.shape[1] // QUAD):
            cols = slice(c * QUAD, (c + 1) * QUAD)
            q_stack = _stack_heads(q_ref[rows, cols], masks)
            p = _probs(k_ref[window, cols], q_stack, allowed).astype(BF16)
            o_ref[rows, cols] = _pick_heads(_tn(p, v_ref[window, cols]), masks).astype(BF16)
    after_ref[...] = x_ref[...].astype(F32) + _nt(o_ref[...], wo_ref[...]) + table_ref[2:3, :]
    normed = norm_parts(after_ref[...])[0]
    h_ref[...] = (normed * table_ref[6:7, :] + table_ref[7:8, :]).astype(BF16)


def _attend_back_kernel(
    q_ref, k_ref, v_ref, do_ref, ids_ref, own_ref, dq_ref, dk_ref, dv_ref, dk_acc, dv_acc
):
    masks = _head_masks(HALO)
    dk_acc[...] = jnp.zeros_like(dk_acc)
    dv_acc[...] = jnp.zeros_like(dv_acc)
    for b, rows, window in _blocks(q_ref.shape[0]):
        allowed = ids_ref[window, :] == own_ref[b]
        q_stack = _stack_heads(q_ref[rows, :], masks)
        do_stack = _stack_heads(do_ref[rows, :], masks)
        k_win = k_ref[window, :]
        p = _probs(k_win, q_stack, allowed)
        dp = _nt(v_ref[window, :], do_stack)
        ds = (p * (dp - jnp.sum(p * dp, axis=0, keepdims=True))).astype(BF16)
        dv_acc[window, :] += _nn(p.astype(BF16), do_stack)
        dk_acc[window, :] += _nn(ds, q_stack)
        dq_ref[rows, :] = _pick_heads(_tn(ds, k_win), masks).astype(BF16)
    dk_ref[...] = dk_acc[...].astype(BF16)
    dv_ref[...] = dv_acc[...].astype(BF16)


def _columns_early(c, *refs):
    copies = [
        pltpu.make_async_copy(ref.at[:, pl.ds(c * QUAD, QUAD)], buf, refs[10].at[n])
        for n, (ref, buf) in enumerate(zip(refs[:4], refs[6:10]))
    ]
    for copy in copies:
        copy.start()
    return copies


def _attend_back_columns(copies, *refs):
    for copy in copies:
        copy.wait()
    _attend_back_kernel(*refs[9:13], *refs[4:6], *refs[6:9], *refs[14:])


def attend_back(q, k, v, do, fq, fk, c):
    rows = q.shape[0]
    return run(
        _attend_back_columns,
        "attend_back",
        [((rows, QUAD), BF16)] * 3,
        [q, k, v, do, fq, fk],
        "aaaavv",
        scratch=[VMEM((rows, QUAD), BF16)] * 4
        + [pltpu.SemaphoreType.DMA((4,))]
        + [VMEM((rows, QUAD), F32)] * 2,
        early=functools.partial(_columns_early, c),
    )


def _up_kernel(ws, *refs):
    at_ref, h_ref, b_ref = refs[:3]
    pieces = refs[3 : 3 + len(ws.arrays)]
    act_ref, slope_ref, w_ref, buf, sem = refs[3 + len(ws.arrays) :]
    g = pl.program_id(0)
    copies = ws.copies(at_ref, pieces, buf, sem)

    @pl.when(g == 0)
    def _():
        for group in copies:
            for c in group:
                c.start()

    for i in range(GROUPS):

        @pl.when(g == i)
        def _(i=i):
            for c in copies[i]:
                c.wait()

    w_ref[0] = buf[g]
    bias = b_ref[pl.ds(8 + (at_ref[2] ^ g), 1), :]
    for i in range(h_ref.shape[0] // CHUNK):
        rows = slice(i * CHUNK, (i + 1) * CHUNK)
        value, slope = gelu_parts(_nn(h_ref[rows, :], buf[g]) + bias)
        act_ref[0, rows, :] = value.astype(BF16)
        slope_ref[0, rows, :] = slope.astype(BF16)


def at_group(*shape):
    zeros = (0,) * (len(shape) - 1)
    return pl.BlockSpec((1,) + shape[1:], lambda g: (g,) + zeros)


def fixed(*shape):
    zeros = (0,) * len(shape)
    return pl.BlockSpec(shape, lambda g: zeros, pipeline_mode=pl.Buffered(1))


def up_stage(ws, at, h, bias):
    rows, width = h.shape
    hidden = ws.cols
    act = jax.ShapeDtypeStruct((GROUPS, rows, hidden), BF16)
    return pl.pallas_call(
        functools.partial(_up_kernel, ws),
        grid=(GROUPS,),
        out_shape=(act, act, jax.ShapeDtypeStruct((GROUPS, width, hidden), BF16)),
        in_specs=[pl.BlockSpec(memory_space=SMEM), fixed(rows, width), fixed(*bias.shape)]
        + [pl.BlockSpec(memory_space=pltpu.HBM)] * len(ws.arrays),
        out_specs=(
            at_group(GROUPS, rows, hidden),
            at_group(GROUPS, rows, hidden),
            at_group(GROUPS, width, hidden),
        ),
        scratch_shapes=ws.scratch(width),
        compiler_params=pltpu.CompilerParams(vmem_limit_bytes=LIMIT["up"] << 20),
        name="up",
    )(at, h, bias, *ws.arrays)


def _down_kernel(ws, total, images, *refs):
    (
        at_ref, last_ref, act_ref, after_ref, bias_ref, mine_ref, cot_ref, owned_ref, pairs_ref,
        scale_ref, logit_ref,
    ) = refs[:11]
    image_refs, refs = refs[11 : 11 + images], refs[11 + images :]
    pieces = refs[: len(ws.arrays)]
    out_ref, g_ref, low_ref, dbias_ref, dscale_ref, dlogit_ref, w_ref, give_ref, keep_ref, buf, sem, acc, text_buf, image_buf, image_sem = refs[
        len(ws.arrays) :
    ]
    g = pl.program_id(0)
    copies = ws.copies(at_ref, pieces, buf, sem)
    if images == 1:
        pics = [pltpu.make_async_copy(image_refs[0], image_buf, image_sem.at[0])]
    else:
        many = image_refs[0].shape[1] - ws.rows
        pics = [
            pltpu.make_async_copy(
                image_refs[dx].at[zrel, pl.ds(ws.rows, many), pl.ds(0, image_buf.shape[1])],
                image_buf.at[
                    pl.ds(
                        pl.multiple_of(((at_ref[0] ^ zrel) * 2 + (at_ref[1] ^ dx)) * many, many),
                        many,
                    )
                ],
                image_sem.at[2 * zrel + dx],
            )
            for zrel in range(4)
            for dx in range(2)
        ]

    @pl.when(g == 0)
    def _():
        for group in copies:
            for c in group:
                c.start()
        for c in pics:
            c.start()
        acc[...] = after_ref[...] + bias_ref[3:4, :]

    for i in range(GROUPS):

        @pl.when(g == i)
        def _(i=i):
            for c in copies[i]:
                c.wait()

    @pl.when(g < GROUPS)
    def _():
        w_ref[0] = buf[g]
        acc[...] += _nt(act_ref[0], buf[g])

    @pl.when(g == GROUPS - 1)
    def _():
        out_ref[...] = acc[...].astype(BF16)
        caps = text_buf.shape[0]
        for c in range(caps):
            text_buf[c : c + 1, :] = acc[pl.ds(last_ref[c], 1), :]
        mine = mine_ref[...]
        pooled = text_buf[...]
        text_scale = lax.rsqrt(jnp.sum(pooled * pooled, axis=1, keepdims=True) + EPSILON)
        text = pooled * text_scale
        for c in pics:
            c.wait()
        image = image_buf[...].astype(F32)
        image = image * lax.rsqrt(jnp.sum(image * image, axis=1, keepdims=True) + EPSILON)
        scale = jnp.exp(scale_ref[...])
        dots = lax.dot_general(
            text, image, (((1,), (1,)), ((), ())), precision=PRECISE, preferred_element_type=F32
        )
        sign = 2.0 * pairs_ref[...].astype(F32) - 1.0
        logits = scale * dots + logit_ref[...]
        d_logits = (-1.0 / total) * mine * sign / (1.0 + jnp.exp(sign * logits))
        dlogit_ref[...] = jnp.sum(d_logits, keepdims=True)
        dscale_ref[...] = jnp.sum(d_logits * (scale * dots), keepdims=True)
        d_text = scale * _nn(d_logits, image, PRECISE)
        d_pooled = text_scale * (d_text - text * jnp.sum(d_text * text, axis=1, keepdims=True))
        g_ref[...] = cot_ref[...].astype(F32) * owned_ref[...]
        text_buf[...] = d_pooled
        for c in range(caps):
            g_ref[pl.ds(last_ref[c], 1), :] += text_buf[c : c + 1, :]
        rows = g_ref[...]
        low_ref[...] = rows.astype(BF16)
        dbias_ref[...] = col_sum(rows)

    @pl.when((g >= GROUPS) & (g < GROUPS + 2))
    def _():
        give_ref[0] = _tn(low_ref[...], act_ref[0]).astype(BF16)

    @pl.when(g >= GROUPS + 2)
    def _():
        keep_ref[0] = _tn(low_ref[...], act_ref[0]).astype(BF16)


def down_stage(ws, at, last_at, act, after, bias, mine, cot, owned, images, pairs, scale, logit, total):
    rows, width = after.shape
    hidden = ws.cols
    caps = mine.shape[0]
    one = jax.ShapeDtypeStruct((1, 1), F32)
    pair = jax.ShapeDtypeStruct((2, width, hidden), BF16)

    def visit(i):
        return jnp.where(i < GROUPS, i, (2 * (i - GROUPS) + 1) % 5)

    return pl.pallas_call(
        functools.partial(_down_kernel, ws, total, len(images)),
        grid=(2 * GROUPS,),
        out_shape=(
            jax.ShapeDtypeStruct((rows, width), BF16),
            jax.ShapeDtypeStruct((rows, width), F32),
            jax.ShapeDtypeStruct((rows, width), BF16),
            jax.ShapeDtypeStruct((1, width), F32),
            one,
            one,
            jax.ShapeDtypeStruct((GROUPS, width, hidden), BF16),
            pair,
            pair,
        ),
        in_specs=[
            pl.BlockSpec(memory_space=SMEM),
            pl.BlockSpec(memory_space=SMEM),
            pl.BlockSpec((1, rows, hidden), lambda i: (visit(i), 0, 0)),
            fixed(rows, width),
            fixed(*bias.shape),
            fixed(caps, 1),
            fixed(rows, width),
            fixed(rows, 1),
            fixed(*pairs.shape),
            fixed(1, 1),
            fixed(1, 1),
        ]
        + [pl.BlockSpec(memory_space=pltpu.HBM)] * (len(images) + len(ws.arrays)),
        out_specs=(
            fixed(rows, width),
            fixed(rows, width),
            fixed(rows, width),
            fixed(1, width),
            fixed(1, 1),
            fixed(1, 1),
            pl.BlockSpec((1, width, hidden), lambda i: (jnp.minimum(i, GROUPS - 1), 0, 0)),
            pl.BlockSpec((1, width, hidden), lambda i: (jnp.clip(i - GROUPS, 0, 1), 0, 0)),
            pl.BlockSpec((1, width, hidden), lambda i: (jnp.clip(i - GROUPS - 2, 0, 1), 0, 0)),
        ),
        scratch_shapes=ws.scratch(width) + [VMEM((rows, width), F32), VMEM((caps, width), F32), VMEM((pairs.shape[1], width), BF16), pltpu.SemaphoreType.DMA((8,))],
        compiler_params=pltpu.CompilerParams(vmem_limit_bytes=LIMIT["down"] << 20),
        name="down",
    )(
        at, last_at, act, after, bias, mine, cot, owned, pairs, scale.reshape(1, 1),
        logit.reshape(1, 1), *images, *ws.arrays,
    )


def _up_grad_kernel(has_sum, low_ref, h_ref, slope_ref, wd_ref, wu_ref, *refs):
    i = pl.program_id(0)
    grad_ref, bias_ref, dh_ref, d_pre = refs[-4:]

    @pl.when(i == 0)
    def _():
        dh_ref[...] = refs[0][...] if has_sum else jnp.zeros_like(dh_ref)

    d_act = _nn(low_ref[...], wd_ref[0])
    d_pre[...] = (d_act * slope_ref[0].astype(F32)).astype(BF16)
    bias_ref[0] = col_sum(d_pre[...].astype(F32))
    grad_ref[0] = _tn(h_ref[...], d_pre[...]).astype(BF16)
    dh_ref[...] += _nt(d_pre[...], wu_ref[0])


def up_grad(low, h, slope, w_d, w_u, first, so_far=None):
    rows, width = low.shape
    hidden = slope.shape[2]

    def pair(a, b):
        return pl.BlockSpec((1, a, b), lambda i: (2 * i + first, 0, 0))

    extra = [] if so_far is None else [so_far]
    return pl.pallas_call(
        functools.partial(_up_grad_kernel, so_far is not None),
        grid=(2,),
        out_shape=(
            jax.ShapeDtypeStruct((2, width, hidden), BF16),
            jax.ShapeDtypeStruct((2, 1, hidden), F32),
            jax.ShapeDtypeStruct((rows, width), F32),
        ),
        in_specs=[
            fixed(rows, width),
            fixed(rows, width),
            pair(rows, hidden),
            pair(width, hidden),
            pair(width, hidden),
        ]
        + [fixed(rows, width)] * len(extra),
        out_specs=(
            at_group(2, width, hidden),
            at_group(2, 1, hidden),
            fixed(rows, width),
        ),
        scratch_shapes=[VMEM((rows, hidden), BF16)],
        compiler_params=pltpu.CompilerParams(vmem_limit_bytes=LIMIT["up_grad"] << 20),
        name="up_grad",
    )(low, h, slope, w_d, w_u, *extra)


def _middle_kernel(
    dh_ref, g_ref, after_ref, gain_ref, att_ref, wo_ref,
    after_grad_ref, datt_ref, ograd_ref, dgain_ref, dshift_ref, dob_ref,
):
    normed, factor = norm_parts(after_ref[...])
    dh = dh_ref[...]
    dgain_ref[...] = col_sum(dh * normed)
    dshift_ref[...] = col_sum(dh)
    d_after = g_ref[...] + norm_back(dh, normed, factor, gain_ref[6:7, :])
    after_grad_ref[...] = d_after
    dob_ref[...] = col_sum(d_after)
    low = d_after.astype(BF16)
    datt_ref[...] = _nn(low, wo_ref[...]).astype(BF16)
    ograd_ref[...] = _tn(low, att_ref[...]).astype(BF16)


def _input_early(quads, *refs):
    d_buf, w_buf, sem = refs[-3:]
    width = quads * QUAD
    copies = [
        pltpu.make_async_copy(refs[n], d_buf.at[:, pl.ds(n * QUAD, QUAD)], sem.at[n])
        for n in range(3 * quads)
    ]
    copies += [
        pltpu.make_async_copy(
            refs[3 * quads + n], w_buf.at[:, pl.ds(n * width, width)], sem.at[3 * quads + n]
        )
        for n in range(3)
    ]
    for c in copies:
        c.start()
    return copies


def _input_kernel(quads, shard, copies, *refs):
    (
        after_grad_ref, x_ref, table_ref, at_ref, up_a_ref, up_b_ref,
        ob_ref, db_ref, gain_two_ref, shift_two_ref, scale_ref, logit_ref,
    ) = refs[3 * quads + 3 : 3 * quads + 15]
    out_ref, vec_ref, d_buf, w_buf, sem = refs[3 * quads + 15 :]
    width = quads * QUAD
    normed, factor = norm_parts(x_ref[...].astype(F32))
    for c in copies:
        c.wait()
    d_buf[:, :width] = d_buf[:, :width] * HEAD_DIM ** (-0.5)
    dh = _nt(d_buf[...], w_buf[...])
    vec_ref[...] = jnp.zeros_like(vec_ref)
    me = at_ref[2]
    for i, first in enumerate((0, 2 * width)):
        whole = col_sum(d_buf[:, first : first + width].astype(F32))
        for g in range(GROUPS):
            vec_ref[pl.ds(4 * i + (me ^ g), 1), :shard] = whole[:, g * shard : (g + 1) * shard]
    for g in range(GROUPS):
        ref = up_b_ref if g % 2 == 0 else up_a_ref
        vec_ref[pl.ds(8 + (me ^ g), 1), :] = ref[g // 2]
    rows = [ob_ref[...], db_ref[...], col_sum(dh * normed), col_sum(dh)]
    rows += [gain_two_ref[...], shift_two_ref[...]]
    for i, v in enumerate(rows):
        vec_ref[12 + i : 13 + i, :] = v
    vec_ref[18:19, :1] = scale_ref[...]
    vec_ref[19:20, :1] = logit_ref[...]
    out_ref[...] = (after_grad_ref[...] + norm_back(dh, normed, factor, table_ref[4:5, :])).astype(
        BF16
    )


def _attn_grad_kernel(quads, shard, *refs):
    h_ref, o_ref = refs[3 * quads : 3 * quads + 2]
    give_ref, keep_ref = refs[3 * quads + 2 :]
    place = {1: (give_ref, 0), 3: (give_ref, 1), 0: (keep_ref, 0), 2: (keep_ref, 1)}
    h = h_ref[...]
    for i in range(3):
        for c in range(quads):
            grad = _tn(h, refs[i * quads + c][...])
            if i == 0:
                grad = grad * HEAD_DIM ** (-0.5)
            grad = grad.astype(BF16)
            lo = c * QUAD
            while lo < (c + 1) * QUAD:
                g = lo // shard
                hi = min((g + 1) * shard, (c + 1) * QUAD)
                ref, slot = place[g]
                start = i * shard + lo - g * shard
                ref[slot, :, start : start + hi - lo] = grad[:, lo - c * QUAD : hi - c * QUAD]
                lo = hi
    for g in range(GROUPS):
        ref, slot = place[g]
        ref[slot, :, 3 * shard :] = o_ref[:, g * shard : (g + 1) * shard]


def _add(*vals):
    total = vals[0].astype(F32)
    for v in vals[1:]:
        total = total + v.astype(F32)
    return total.astype(BF16)


def _plane_kernel(at_ref, keep_ref, got_ref, *outs):
    for y in range(2):
        for dx in range(2):
            x = at_ref[1] ^ dx
            for z in range(keep_ref.shape[1]):
                outs[2 * y + dx][z] = _add(keep_ref[y, z, x], got_ref[y, z, x])


def _split_kernel(cut, at_ref, keep_ref, got_ref, own_ref, give_ref, *outs):
    cols = keep_ref.shape[4]
    for dx, ref in enumerate((own_ref, give_ref)):
        x = at_ref[1] ^ dx
        for y in range(2):
            for z in range(keep_ref.shape[1]):
                ref[y, z] = _add(keep_ref[y, z, x, :, :cut], got_ref[y, z, x, :, :cut])
    for j, ref in enumerate(outs):
        z = at_ref[0] ^ j
        for y in range(2):
            for x in range(2):
                ref[y, x] = _add(keep_ref[y, z, x, :, cut:], got_ref[y, z, x, :, cut:])


def by_block(mv, a):
    return a.reshape(2, mv.nz, 2, a.shape[1] // mv.n, a.shape[2])


def plane_parts(mv, keep, got):
    keep, got = by_block(mv, keep), by_block(mv, got)
    out = ((mv.nz,) + keep.shape[3:], BF16)
    return run(_plane_kernel, "plane_parts", [out] * 4, [mv.at, keep, got], "svv")


def split_parts(mv, keep, got, cut):
    keep, got = by_block(mv, keep), by_block(mv, got)
    rows, cols = keep.shape[3:]
    outs = [((2, mv.nz, rows, cut), BF16)] * 2 + [((2, 2, rows, cols - cut), BF16)] * 4
    kernel = functools.partial(_split_kernel, cut)
    return run(kernel, "plane_parts", outs, [mv.at, keep, got], "svv")


def _z_kernel(count, at_ref, *refs):
    ins, outs = refs[:count], refs[count:]
    for j in range(4):
        b = at_ref[0] ^ j
        outs[j][...] = _add(*[r[b] for r in ins])


def z_parts(mv, held):
    out = (held[0].shape[1:], BF16)
    kernel = functools.partial(_z_kernel, len(held))
    return run(kernel, "z_parts", [out] * 4, [mv.at, *held], "s" + "v" * len(held))


def _join_kernel(at_ref, a_ref, b_ref, *refs):
    ins, outs, (own_ref, give_ref) = refs[:4], refs[4:8], refs[8:]
    for j in range(4):
        b = at_ref[0] ^ j
        for y in range(2):
            outs[j][y] = _add(a_ref[y, b], b_ref[y, b])
    for dx, ref in enumerate((own_ref, give_ref)):
        x = at_ref[1] ^ dx
        for y in range(2):
            ref[y] = _add(*[r[y, x] for r in ins])


def join_parts(mv, own, got, held):
    outs = [((2,) + own.shape[2:], BF16)] * 4 + [((2,) + held[0].shape[2:], BF16)] * 2
    return run(_join_kernel, "z_parts", outs, [mv.at, own, got, *held], "s" + "v" * 6)


def _spread_kernel(piece, at_ref, keep_ref, *refs):
    out_ref = refs[-1]
    wins = [(refs[0],), (refs[1],), (refs[2], refs[3]), (refs[4], refs[5])]
    j = pl.program_id(0)
    here = j ^ at_ref[2]
    before = (j - 1) ^ at_ref[2]
    for i in range(4):

        @pl.when(here == i)
        def _(i=i):
            done = 0
            for ref in wins[i]:
                rows = min(ref.shape[0], piece - done)
                out_ref[done : done + rows, :] = ref[:rows, :].astype(out_ref.dtype)
                done += rows

    for i in range(4):

        @pl.when((before == i) & (j > 0))
        def _(i=i):
            ref = wins[i][-1]
            tail = ref[ref.shape[0] - HALO :, :].astype(out_ref.dtype)
            out_ref[:HALO, :] = jnp.where(keep_ref[0] > 0, out_ref[:HALO, :], tail)


def spread(at, keep, windows, piece, dtype):
    cols = windows[0].shape[1]
    return pl.pallas_call(
        functools.partial(_spread_kernel, piece),
        grid=(GROUPS,),
        out_shape=jax.ShapeDtypeStruct((GROUPS * piece, cols), dtype),
        in_specs=[pl.BlockSpec(memory_space=SMEM), at_group(GROUPS, HALO, 1)]
        + [fixed(*w.shape) for w in windows],
        out_specs=pl.BlockSpec((piece, cols), lambda j: (j, 0)),
        compiler_params=pltpu.CompilerParams(vmem_limit_bytes=LIMIT["spread"] << 20),
        name="spread",
    )(at, keep, *windows)


def _spread_first_kernel(piece, at_ref, own_ref, near_ref, far_ref, out_ref, *rest):
    bufs, sem = rest[:3], rest[3]
    copies = []
    for i, ref in enumerate((own_ref, near_ref, far_ref)):
        rows = min(ref.shape[0], piece)
        bufs[i][...] = ref[:rows, :].astype(F32)
        start = pl.multiple_of((at_ref[2] ^ i) * piece, piece)
        copies.append(pltpu.make_async_copy(bufs[i], out_ref.at[pl.ds(start, rows)], sem.at[i]))
        copies[-1].start()
    for c in copies:
        c.wait()


def spread_first(at, own, near, far, piece):
    rows, cols = own.shape
    wins = (own, near, far)
    return pl.pallas_call(
        functools.partial(_spread_first_kernel, piece),
        out_shape=jax.ShapeDtypeStruct((GROUPS * piece, cols), F32),
        in_specs=[pl.BlockSpec(memory_space=SMEM)] + [pl.BlockSpec(memory_space=VMEM)] * 3,
        out_specs=pl.BlockSpec(memory_space=pltpu.HBM),
        scratch_shapes=[VMEM((min(w.shape[0], piece), cols), F32) for w in wins]
        + [pltpu.SemaphoreType.DMA((3,))],
        compiler_params=pltpu.CompilerParams(vmem_limit_bytes=LIMIT["spread"] << 20),
        name="spread",
    )(at, *wins)


def _spread_last_kernel(piece, at_ref, keep_ref, *refs):
    heads, tails, parts = refs[:4], refs[4:8], refs[8:11]
    out_ref, bufs, head_bufs, sem = refs[12], refs[13:16], refs[16], refs[17]
    copies = []
    for n, (ref, side, first) in enumerate(zip(parts, (2, 3, 3), (1, 0, 1))):
        rows = bufs[n].shape[0]
        bufs[n][...] = ref[:rows, :].astype(F32)
        start = (at_ref[2] ^ side) * piece + first * (piece - rows)
        copies.append(
            pltpu.make_async_copy(
                bufs[n], out_ref.at[pl.ds(pl.multiple_of(start, HALO // 2), rows)], sem.at[n]
            )
        )
        copies[-1].start()
    for c in copies:
        c.wait()
    copies = []
    for j in range(1, GROUPS):
        for i in range(4):

            @pl.when((at_ref[2] ^ j) == i)
            def _(i=i, j=j):
                head_bufs[j - 1] = heads[i][...].astype(F32)

        for i in range(4):

            @pl.when((at_ref[2] ^ (j - 1)) == i)
            def _(i=i, j=j):
                head_bufs[j - 1] = jnp.where(
                    keep_ref[j] > 0, head_bufs[j - 1], tails[i][...].astype(F32)
                )

        copies.append(
            pltpu.make_async_copy(
                head_bufs.at[j - 1], out_ref.at[pl.ds(j * piece, HALO)], sem.at[2 + j]
            )
        )
        copies[-1].start()
    for c in copies:
        c.wait()


def spread_last(at, keep, firsts, lasts, so_far, piece):
    cols = so_far.shape[1]
    split = firsts[2].shape[0]
    heads = [f[:HALO] for f in firsts]
    tails = [t[t.shape[0] - HALO :] for t in lasts]
    vmem = pl.BlockSpec(memory_space=VMEM)
    return pl.pallas_call(
        functools.partial(_spread_last_kernel, piece),
        out_shape=jax.ShapeDtypeStruct(so_far.shape, F32),
        in_specs=[pl.BlockSpec(memory_space=SMEM)]
        + [vmem] * 12
        + [pl.BlockSpec(memory_space=pltpu.HBM)],
        out_specs=pl.BlockSpec(memory_space=pltpu.HBM),
        scratch_shapes=[VMEM((rows, cols), F32) for rows in (piece - split, split, piece - split)]
        + [VMEM((3, HALO, cols), F32), pltpu.SemaphoreType.DMA((6,))],
        input_output_aliases={13: 0},
        compiler_params=pltpu.CompilerParams(vmem_limit_bytes=LIMIT["spread"] << 20),
        name="spread",
    )(at, keep, *heads, *tails, lasts[2], firsts[3], lasts[3], so_far)


def _flip(a, axis, bit):
    n = lax.axis_size(axis)
    return lax.ppermute(a, axis, [(i, i ^ bit) for i in range(n)])


def fence(*trees):
    return lax.optimization_barrier(trees)


def add_low(a, b):
    return (a.astype(F32) + b.astype(F32)).astype(BF16)


class Moves:
    def __init__(self):
        self.n = lax.axis_size("dp")
        self.nz = self.n // 2
        at = lax.axis_index("dp")
        self.at = jnp.stack([at // 2, at % 2, lax.axis_index("mp")]).astype(jnp.int32)
        self.near = self.n == 8

    def z_all(self, a):
        return [a] + [_flip(a, "dp", 2 * j) for j in range(1, 4)]

    def cross_flip(self, a):
        return lax.ppermute(
            a,
            ("dp", "mp"),
            [(4 * d + m, 4 * (d ^ 1) + (m ^ 2)) for d in range(self.n) for m in range(4)],
        )

    def plane_all(self, a):
        return [a, _flip(a, "dp", 1), _flip(a, "mp", 2), self.cross_flip(a)]

    def core_all(self, parts):
        return [_flip(a, "mp", 1) for a in parts]

    def gather_far(self, a):
        mine = lax.all_gather(a, "dp", axis=0, tiled=True)
        far = _flip(mine, "mp", 2)
        whole = jnp.stack([mine, _flip(mine, "mp", 1), far, _flip(far, "mp", 1)])
        return Weights([whole], None, a.shape[0], a.shape[1])

    def to_core(self, give):
        return _flip(give, "mp", 1)

    def scatter_far(self, keep, got):
        both = add_low(keep, got)
        mine = add_low(both[0], _flip(both[1], "mp", 2))
        return lax.psum_scatter(mine, "dp", scatter_dimension=0, tiled=True).astype(F32)

    def plane_sides(self, parts):
        return [
            parts[0], _flip(parts[1], "dp", 1), _flip(parts[2], "mp", 2), self.cross_flip(parts[3]),
        ]

    def z_sides(self, parts):
        return [_flip(parts[j], "dp", 2 * j) for j in range(1, 4)]


PLANE = [(dx, dy) for dy in range(2) for dx in range(2)]


def z_then_plane(first, col, cut, wide):
    return [
        (first + 4 * core + i, (zrel,), zrel, dx, core + 2 * dy, col, cut, wide)
        for core in range(2)
        for i, (dx, dy) in enumerate(PLANE)
        for zrel in range(4)
    ]


def plane_then_z(first, col, cut, wide):
    return [
        (first + 4 * core + zrel, (i,), zrel, dx, core + 2 * dy, col, cut, wide)
        for core in range(2)
        for zrel in range(4)
        for i, (dx, dy) in enumerate(PLANE)
    ]


def body(
    tokens,
    out_cot,
    seg_ids,
    valid_mask,
    last_pos,
    pairs,
    images,
    q_weight,
    k_weight,
    v_weight,
    o_weight,
    up_weight,
    down_weight,
    q_bias,
    v_bias,
    o_bias,
    up_bias,
    down_bias,
    gain_one,
    shift_one,
    gain_two,
    shift_two,
    log_scale,
    logit_bias,
):
    mv = Moves()
    assert lax.axis_size("mp") == GROUPS
    row_count, seq_len = seg_ids.shape
    token_count, width = tokens.shape
    piece = token_count // GROUPS
    caption_total = pairs.shape[0] * mv.n
    at = lax.axis_index("mp")
    shard = q_weight.shape[1]
    hidden = up_weight.shape[1]
    block = q_weight.shape[0]
    quads = width // QUAD

    own_a = jnp.concatenate([q_weight, k_weight, v_weight, o_weight.T], axis=1)
    down_t = down_weight.T
    cut = QUAD
    if mv.near:
        a_z = mv.z_all(own_a)
        a_z[1], up_weight, down_t, images = fence(a_z[1], up_weight, down_t, images)
        own_1 = jnp.concatenate([up_weight, down_t[:, :cut]], axis=1)
        own_1 = jnp.concatenate([own_1, jnp.pad(images, ((0, 0), (0, cut)))], axis=0)
        w2_plane = mv.plane_all(down_t[:, cut:])
        a_z, own_1, w2_plane = fence(a_z, own_1, w2_plane)
        a_here = jnp.stack(a_z)
        a_here, tokens, out_cot, seg_ids, valid_mask, last_pos, q_bias = fence(
            a_here, tokens, out_cot, seg_ids, valid_mask, last_pos, q_bias
        )
        a_plane = mv.plane_all(a_here)
        w1_z = mv.z_all(own_1)

    start = at * piece
    tail = jnp.minimum(start + piece, token_count - HALO)

    def window(a):
        return jnp.concatenate(
            [
                lax.dynamic_slice_in_dim(a, start, piece),
                lax.dynamic_slice_in_dim(a, tail, HALO),
            ],
            axis=0,
        )

    flat_at = jnp.arange(token_count, dtype=jnp.int32)
    caption_id = jnp.where(
        valid_mask.reshape(-1) > 0,
        (flat_at // seq_len) * (last_pos.shape[1] * 2) + seg_ids.reshape(-1),
        (1 << 20) + flat_at,
    )
    inside = at < GROUPS - 1
    ids = window(caption_id)
    tail_ids = jnp.where(inside, ids[piece:], -2 - jnp.arange(HALO, dtype=jnp.int32))
    ids = jnp.concatenate([ids[:piece], tail_ids])
    before = jnp.where(
        at > 0, lax.dynamic_index_in_dim(caption_id, jnp.maximum(start - 1, 0), keepdims=False), -1
    )
    owned = jnp.concatenate([ids[:piece] != before, (tail_ids == ids[piece - 1]) & inside])
    by_piece = caption_id.reshape(GROUPS, piece)
    last_before = jnp.concatenate([jnp.full((1,), -1, jnp.int32), by_piece[:-1, -1]])
    keep_head = (by_piece[:, :HALO] != last_before[:, None]).astype(F32)[:, :, None]
    count = piece + HALO
    places = start + jnp.arange(count, dtype=jnp.int32)
    fq = ids[:, None]
    blocks = count // HALO
    fk = jnp.concatenate([ids.reshape(blocks, HALO)] * 4, axis=1)[:, None, :]

    flat_last = (
        last_pos + seq_len * jnp.arange(row_count, dtype=jnp.int32)[:, None]
    ).reshape(-1)
    last_at = jnp.clip(flat_last - start, 0, count - 1)
    mine = jnp.any((flat_last[:, None] == places[None, :]) & owned[None, :], axis=1)
    mine = mine.astype(F32)[:, None]
    x_rows = window(tokens)
    cot = window(out_cot)
    owned_rows = owned.astype(F32)[:, None]

    table = jnp.concatenate(
        [q_bias, v_bias, o_bias, down_bias, gain_one, shift_one, gain_two, shift_two, up_bias]
    ).reshape(-1, width)
    if mv.near:
        small = (x_rows, cot, fq, fk, last_at, mine, owned_rows, keep_head, table)
        a_plane, w1_z, w2_plane, small = fence(a_plane, w1_z, w2_plane, small)
        x_rows, cot, fq, fk, last_at, mine, owned_rows, keep_head, table = small
        a_core = [mv.to_core(v) for v in a_plane]
        w_a = Weights(a_plane + a_core, z_then_plane(0, 0, 0, hidden), block, hidden)
        w1_here, w2_here = jnp.stack(w1_z), jnp.stack(w2_plane)
        w1_x, w1_y = _flip(w1_here, "dp", 1), _flip(w1_here, "mp", 2)
        w2_near = [_flip(w2_here, "dp", 2), _flip(w2_here, "dp", 4)]
    else:
        w_a, w_u, w_d = (mv.gather_far(v) for v in (own_a, up_weight, down_t))
        pics = [lax.all_gather(images, "dp", axis=0, tiled=True)]

    rows_low = ((count, width), BF16)
    square = ((width, width), BF16)
    h_one, queries, keys, vals, w_q, w_k, w_v, w_o = run(
        functools.partial(_qkv_kernel, w_a, width, shard),
        "qkv",
        [rows_low] * 4 + [square] * 4,
        [mv.at, x_rows, table, *w_a.arrays],
        "svv" + "a" * len(w_a.arrays),
        scratch=w_a.scratch(width),
        early=functools.partial(_qkv_early, w_a),
    )
    if mv.near:
        queries, keys, vals, w1_here, w2_here, w1_x, w1_y, w2_near = fence(
            queries, keys, vals, w1_here, w2_here, w1_x, w1_y, w2_near
        )
        w1_cross, w2_last = mv.cross_flip(w1_here), _flip(w2_here, "dp", 6)
        w1_core = [mv.to_core(v) for v in (w1_here, w1_x, w1_y)]
    attended, after_attn, h_two = run(
        _attend_kernel,
        "attend",
        [rows_low, ((count, width), F32), rows_low],
        [queries, keys, vals, fq, fk, w_o, x_rows, table],
    )
    if mv.near:
        h_two, w1_cross, w2_last, w1_core = fence(h_two, w1_cross, w2_last, w1_core)
        pics = [w1_here, w1_x]
        w1_all = [w1_here, w1_x, w1_y, w1_cross, *w1_core, mv.to_core(w1_cross)]
        w_u = Weights(w1_all, z_then_plane(0, 0, 0, hidden), block, hidden)
        w2_all = [w2_here, *w2_near, w2_last]
        w2_all = w2_all + [mv.to_core(v) for v in w2_all]
    acts, slopes, w_up = up_stage(w_u, mv.at, h_two, table)
    if mv.near:
        w2_all, acts = fence(w2_all, acts)
        w_d = Weights(
            w1_all + w2_all,
            z_then_plane(0, 0, hidden, cut) + plane_then_z(8, cut, 0, hidden - cut),
            block,
            hidden,
        )
    out_low, g_rows, g_low, d_down_bias, d_scale, d_logit, w_down, down_give, down_keep = down_stage(
        w_d, mv.at, last_at, acts, after_attn, table, mine, cot, owned_rows, pics, pairs,
        log_scale, logit_bias, caption_total,
    )

    split = count // 2
    down_got = mv.to_core(down_give)
    out_a, out_near = _flip(out_low[:split], "mp", 2), _flip(out_low, "mp", 1)
    up_give, up_bias_a, d_h_two = up_grad(g_low, h_two, slopes, w_down, w_up, 1)
    down_got, up_give, d_h_two, out_a, out_near = fence(
        down_got, up_give, d_h_two, out_a, out_near
    )
    up_got = mv.to_core(up_give)
    out_cross_a = _flip(out_a, "mp", 1)
    if mv.near:
        sent = plane_parts(mv, down_keep, down_got)
        sent, d_h_two = fence(sent, d_h_two)
        down_held = mv.plane_sides(sent)
    up_keep, up_bias_b, d_h_two = up_grad(g_low, h_two, slopes, w_down, w_up, 0, d_h_two)
    vec = ((1, width), F32)
    d_after, d_attended, o_grad, d_gain_two, d_shift_two, d_o_bias = run(
        _middle_kernel,
        "middle",
        [((count, width), F32), rows_low, square, vec, vec, vec],
        [d_h_two, g_rows, after_attn, table, attended, w_o],
    )
    parts = [attend_back(queries, keys, vals, d_attended, fq, fk, 0)]
    if mv.near:
        sent = plane_parts(mv, up_keep, up_got)
        down_held, sent, parts, out_cross_a = fence(
            down_held, sent, parts, out_cross_a
        )
        down_sent = z_parts(mv, down_held)
        down_sent, sent, d_attended = fence(down_sent, sent, d_attended)
        up_held = mv.plane_sides(sent)
        down_pieces = [down_sent[0]] + [_flip(down_sent[j], "dp", 2 * j) for j in (1, 2)]
    for c in range(1, quads):
        parts.append(attend_back(queries, keys, vals, d_attended, fq, fk, c))
    if mv.near:
        parts, up_held, down_pieces = fence(parts, up_held, down_pieces)
        sent = z_parts(mv, up_held)
        sent, parts = fence(sent, parts)
        up_pieces = [sent[0]] + mv.z_sides(sent)
        down_pieces.append(_flip(down_sent[3], "dp", 6))
    flat = [p[i] for i in range(3) for p in parts]
    out_b = _flip(out_low[split:], "mp", 2)
    d_tokens, summed = run(
        functools.partial(_input_kernel, quads, shard),
        "input",
        [rows_low, ((24, hidden), F32)],
        [
            *flat, w_q, w_k, w_v, d_after, x_rows, table, mv.at, up_bias_a, up_bias_b,
            d_o_bias, d_down_bias, d_gain_two, d_shift_two, d_scale, d_logit,
        ],
        "a" * (3 * quads + 3) + "vvvs" + "v" * 8,
        scratch=[
            VMEM((count, 3 * width), BF16),
            VMEM((width, 3 * width), BF16),
            pltpu.SemaphoreType.DMA((3 * quads + 3,)),
        ],
        early=functools.partial(_input_early, quads),
    )
    if mv.near:
        d_tokens, flat, summed, up_pieces, down_pieces, out_b = fence(
            d_tokens, flat, summed, up_pieces, down_pieces, out_b
        )
        summed = summed + _flip(summed, "mp", 1)
    out_cross_b = _flip(out_b, "mp", 1)
    attn_give, attn_keep = run(
        functools.partial(_attn_grad_kernel, quads, shard),
        "attn_grad",
        [((2, width, hidden), BF16)] * 2,
        [*flat, h_one, o_grad],
    )
    attn_give, attn_keep, summed, out_cross_b, d_tokens = fence(
        attn_give, attn_keep, summed, out_cross_b, d_tokens
    )
    attn_got = mv.to_core(attn_give)
    grad_near = _flip(d_tokens, "mp", 1)
    if mv.near:
        summed = mv.plane_all(summed)
        attn_got, grad_near, summed = fence(attn_got, grad_near, summed)
        cut = 2 * QUAD
        own_a, sent_a, *sent = split_parts(mv, attn_keep, attn_got, cut)
        sent_a, sent, d_tokens = fence(sent_a, sent, d_tokens)
        side_a = _flip(sent_a, "dp", 1)
        pieces_b = [sent[0]] + mv.z_sides(sent)
    far_a = _flip(d_tokens[:split], "mp", 2)

    def low_sum(pieces):
        return sum(v.astype(F32) for v in pieces)

    if mv.near:
        side_a, pieces_b, far_a, out_cross_b = fence(side_a, pieces_b, far_a, out_cross_b)
        *sent, own_b, sent_b = join_parts(mv, own_a, side_a, pieces_b)
        sent, sent_b, d_tokens, out_cross_b = fence(sent, sent_b, d_tokens, out_cross_b)
        pieces_a = [sent[0]] + mv.z_sides(sent)
        side_b = _flip(sent_b, "dp", 1)
    far_b = _flip(d_tokens[split:], "mp", 2)
    grad_first = spread_first(mv.at, d_tokens, grad_near, far_a, piece)
    layer_out = spread(
        mv.at, keep_head, [out_low, out_near, out_a, out_b, out_cross_a, out_cross_b], piece, BF16
    )
    if mv.near:
        pieces_a, side_b, far_a, far_b, summed, layer_out, grad_first = fence(
            pieces_a, side_b, far_a, far_b, summed, layer_out, grad_first
        )
    if mv.near:
        summed = mv.z_all((summed[0] + summed[1]) + (summed[2] + summed[3]))
        sum_a, sum_b = low_sum(pieces_a), low_sum([own_b, side_b])
        both = jnp.concatenate([sum_a, sum_b], axis=2)
        attn_far = _flip(both[1].astype(BF16), "mp", 2)
    else:
        summed = lax.psum(summed, ("dp", "mp"))
        grad_down = mv.scatter_far(down_keep, down_got).T
        grad_up = mv.scatter_far(up_keep, up_got)
        grad_attn = mv.scatter_far(attn_keep, attn_got)
    grad_cross_a, grad_cross_b = _flip(far_a, "mp", 1), _flip(far_b, "mp", 1)
    grad_tokens = spread_last(
        mv.at, keep_head, [d_tokens, grad_near, far_a, grad_cross_a],
        [d_tokens, grad_near, far_b, grad_cross_b], grad_first, piece,
    )
    if mv.near:
        grad_tokens, summed, attn_far = fence(grad_tokens, summed, attn_far)
        summed = (summed[0] + summed[1]) + (summed[2] + summed[3])
        grad_down = low_sum(down_pieces).T
        grad_up = low_sum(up_pieces)
        grad_attn = both[0] + attn_far.astype(F32)

    def mine_of(first):
        return lax.dynamic_index_in_dim(summed, first + at, 0, keepdims=False)

    out_vectors = [mine_of(0)[:shard], mine_of(4)[:shard], summed[12], mine_of(8)]
    out_vectors += [summed[i] for i in range(13, 18)] + [summed[18, :1], summed[19, :1]]

    return (
        layer_out,
        grad_tokens,
        grad_attn[:, :shard],
        grad_attn[:, shard : 2 * shard],
        grad_attn[:, 2 * shard : 3 * shard],
        grad_attn[:, 3 * shard :].T,
        grad_up,
        grad_down,
        *out_vectors,
    )


def solution(mesh):
    rows, weight, weight_t = P("dp", None), P("dp", "mp"), P("mp", "dp")
    placed = (rows,) * 7 + (weight,) * 3 + (weight_t, weight, weight_t) + (P(),) * 11
    return jax.shard_map(
        body,
        mesh=mesh,
        in_specs=placed,
        out_specs=(rows,) * 2
        + (weight,) * 3
        + (weight_t, weight, weight_t)
        + (P("mp"), P("mp"), P(), P("mp"))
        + (P(),) * 7,
        check_vma=False,
    )
```

```python
import functools

import jax
import jax.numpy as jnp
from jax import lax
from jax.experimental import pallas as pl
from jax.experimental.pallas import tpu as pltpu
from jax.sharding import PartitionSpec as P

HEAD_DIM = 64
HALO = 64
QUAD = 4 * HEAD_DIM
CHUNK = 208
EPSILON = 1e-06
MASKED = -1000000000.0
PRECISE = lax.Precision.HIGHEST
F32 = jnp.float32
BF16 = jnp.bfloat16
VMEM = pltpu.VMEM
SMEM = pltpu.SMEM
GROUPS = 4
LIMIT = dict(up_last=44, plane_parts=10, qkv=62, attend=62, attend_back=30, up=40, down=48, down_grad=16, up_grad=24, middle=20, input=30, attn_grad=40, z_parts=6, spread=16)


def _nt(a, b):
    return lax.dot_general(a, b, (((1,), (1,)), ((), ())), preferred_element_type=F32)


def _tn(a, b):
    return lax.dot_general(a, b, (((0,), (0,)), ((), ())), preferred_element_type=F32)


def _nn(a, b, precision=None):
    return lax.dot_general(
        a, b, (((1,), (0,)), ((), ())), precision=precision, preferred_element_type=F32
    )


def norm_parts(values):
    center = values - jnp.mean(values, axis=-1, keepdims=True)
    factor = lax.rsqrt(jnp.mean(center * center, axis=-1, keepdims=True) + EPSILON)
    return (center * factor, factor)


def norm_back(grad_rows, normed, factor, gain_vec):
    shaped = grad_rows * gain_vec
    first_mean = jnp.mean(shaped, axis=-1, keepdims=True)
    second_mean = jnp.mean(shaped * normed, axis=-1, keepdims=True)
    return factor * (shaped - first_mean - normed * second_mean)


def gelu_parts(u):
    k = 0.7978845608028654
    sq = u * u
    t = jnp.tanh(k * (u + 0.044715 * (sq * u)))
    half = 0.5 * (1.0 + t)
    slope = half + 0.5 * u * (1.0 - t * t) * (k * (1.0 + 3.0 * 0.044715 * sq))
    return u * half, slope


def col_sum(a):
    return jnp.sum(a, axis=0, keepdims=True)


def staged(kernel, spaces, n_out, early, *refs):
    n_in = len(spaces)
    moved = [i for i, c in enumerate(spaces) if c == "v"]
    ins, outs = list(refs[:n_in]), refs[n_in : n_in + n_out]
    rest = refs[n_in + n_out :]
    in_bufs, out_bufs = rest[: len(moved)], rest[len(moved) : len(moved) + n_out]
    sem = rest[len(moved) + n_out]
    rest = rest[len(moved) + n_out + 1 :]
    copies = [
        pltpu.make_async_copy(ins[i], buf, sem.at[n]) for n, (i, buf) in enumerate(zip(moved, in_bufs))
    ]
    for c in copies:
        c.start()
    own = [] if early is None else [early(*ins, *rest)]
    for c in copies:
        c.wait()
    for i, buf in zip(moved, in_bufs):
        ins[i] = buf
    kernel(*own, *ins, *out_bufs, *rest)
    copies = [
        pltpu.make_async_copy(buf, ref, sem.at[len(moved) + n])
        for n, (buf, ref) in enumerate(zip(out_bufs, outs))
    ]
    for c in copies:
        c.start()
    for c in copies:
        c.wait()


def run(kernel, name, outs, ins, spaces=None, scratch=(), early=None):
    spaces = spaces or "v" * len(ins)
    moved = [a for a, c in zip(ins, spaces) if c == "v"]
    hbm, smem = pl.BlockSpec(memory_space=pltpu.HBM), pl.BlockSpec(memory_space=SMEM)
    return pl.pallas_call(
        functools.partial(staged, kernel, spaces, len(outs), early),
        out_shape=tuple(jax.ShapeDtypeStruct(s, d) for s, d in outs),
        in_specs=[smem if c == "s" else hbm for c in spaces],
        out_specs=tuple(hbm for _ in outs),
        scratch_shapes=[VMEM(a.shape, a.dtype) for a in moved]
        + [VMEM(s, d) for s, d in outs]
        + [pltpu.SemaphoreType.DMA((len(moved) + len(outs),))]
        + list(scratch),
        compiler_params=pltpu.CompilerParams(vmem_limit_bytes=LIMIT[name] << 20),
        name=name,
    )(*ins)


def copies_of(plan, rows, at_ref, refs, buf, sem):
    z, x = at_ref[0], at_ref[1]
    out = [[] for _ in range(GROUPS)]
    for n, (src, first, zrel, dx, group, col, cut, wide) in enumerate(plan):
        slot = pl.multiple_of(((z ^ zrel) * 2 + (x ^ dx)) * rows, rows)
        out[group].append(
            pltpu.make_async_copy(
                refs[src].at[(*first, pl.ds(0, rows), pl.ds(cut, wide))],
                buf.at[group, pl.ds(slot, rows), pl.ds(col, wide)],
                sem.at[n],
            )
        )
    return out


def whole_copies(ref, buf, sem):
    return [[pltpu.make_async_copy(ref.at[g], buf.at[g], sem.at[g])] for g in range(GROUPS)]


class Weights:
    def __init__(self, arrays, plan, rows, cols):
        self.arrays, self.plan, self.rows, self.cols = arrays, plan, rows, cols

    def scratch(self, width):
        count = GROUPS if self.plan is None else len(self.plan)
        return [VMEM((GROUPS, width, self.cols), BF16), pltpu.SemaphoreType.DMA((count,))]

    def copies(self, at_ref, refs, buf, sem):
        if self.plan is None:
            return whole_copies(refs[0], buf, sem)
        return copies_of(self.plan, self.rows, at_ref, refs, buf, sem)


def _head_masks(rows):
    lane = lax.broadcasted_iota(jnp.int32, (rows, QUAD), 1) // HEAD_DIM
    return [lane == h for h in range(4)]


def _stack_heads(block, masks):
    zero = jnp.zeros_like(block)
    return jnp.concatenate([jnp.where(m, block, zero) for m in masks], axis=0)


def _pick_heads(stacked, masks):
    rows = stacked.shape[0] // 4
    out = stacked[:rows]
    for h in range(1, 4):
        out = jnp.where(masks[h], stacked[h * rows : (h + 1) * rows], out)
    return out


def _probs(k_win, q_stack, allowed):
    scores = jnp.where(allowed, _nt(k_win, q_stack), MASKED)
    top = jnp.max(scores, axis=0, keepdims=True)
    e = jnp.exp(scores - top)
    return e * (1.0 / jnp.sum(e, axis=0, keepdims=True))


def _blocks(total):
    for b in range(total // HALO):
        first = min(max(b - 1, 0) * HALO, total - 3 * HALO)
        yield b, slice(b * HALO, (b + 1) * HALO), slice(first, first + 3 * HALO)


def _qkv_early(ws, at_ref, x_ref, table_ref, *refs):
    copies = ws.copies(at_ref, refs[: len(ws.arrays)], *refs[len(ws.arrays) :])
    for group in copies:
        for c in group:
            c.start()
    return copies


def _qkv_kernel(ws, width, shard, copies, *refs):
    at_ref, x_ref, table_ref = refs[:3]
    h_ref, q_ref, k_ref, v_ref, wq_ref, wk_ref, wv_ref, wo_ref, buf, sem = refs[
        3 + len(ws.arrays) :
    ]
    normed = norm_parts(x_ref[...].astype(F32))[0]
    h_ref[...] = (normed * table_ref[4:5, :] + table_ref[5:6, :]).astype(BF16)
    h = h_ref[...]
    for g in range(GROUPS):
        for c in copies[g]:
            c.wait()
        cols = slice(g * shard, (g + 1) * shard)
        r = _nn(h, buf[g])
        own = at_ref[2] ^ g
        q_bias, v_bias = (
            sum(
                jnp.where(own == j, table_ref[i : i + 1, j * shard : (j + 1) * shard], 0.0)
                for j in range(GROUPS)
            )
            for i in range(2)
        )
        q_ref[:, cols] = ((r[:, :shard] + q_bias) * HEAD_DIM ** (-0.5)).astype(BF16)
        k_ref[:, cols] = r[:, shard : 2 * shard].astype(BF16)
        v_ref[:, cols] = (r[:, 2 * shard : 3 * shard] + v_bias).astype(BF16)
        for i, ref in enumerate((wq_ref, wk_ref, wv_ref, wo_ref)):
            ref[:, cols] = buf[g, :, i * shard : (i + 1) * shard]


def _attend_kernel(
    q_ref, k_ref, v_ref, ids_ref, own_ref, wo_ref, x_ref, table_ref,
    o_ref, after_ref, h_ref,
):
    masks = _head_masks(HALO)
    for b, rows, window in _blocks(q_ref.shape[0]):
        allowed = ids_ref[window, :] == own_ref[b]
        for c in range(q_ref.shape[1] // QUAD):
            cols = slice(c * QUAD, (c + 1) * QUAD)
            q_stack = _stack_heads(q_ref[rows, cols], masks)
            p = _probs(k_ref[window, cols], q_stack, allowed).astype(BF16)
            o_ref[rows, cols] = _pick_heads(_tn(p, v_ref[window, cols]), masks).astype(BF16)
    after_ref[...] = x_ref[...].astype(F32) + _nt(o_ref[...], wo_ref[...]) + table_ref[2:3, :]
    normed = norm_parts(after_ref[...])[0]
    h_ref[...] = (normed * table_ref[6:7, :] + table_ref[7:8, :]).astype(BF16)


def _attend_back_kernel(
    q_ref, k_ref, v_ref, do_ref, ids_ref, own_ref, dq_ref, dk_ref, dv_ref, dk_acc, dv_acc
):
    masks = _head_masks(HALO)
    dk_acc[...] = jnp.zeros_like(dk_acc)
    dv_acc[...] = jnp.zeros_like(dv_acc)
    for b, rows, window in _blocks(q_ref.shape[0]):
        allowed = ids_ref[window, :] == own_ref[b]
        q_stack = _stack_heads(q_ref[rows, :], masks)
        do_stack = _stack_heads(do_ref[rows, :], masks)
        k_win = k_ref[window, :]
        p = _probs(k_win, q_stack, allowed)
        dp = _nt(v_ref[window, :], do_stack)
        ds = (p * (dp - jnp.sum(p * dp, axis=0, keepdims=True))).astype(BF16)
        dv_acc[window, :] += _nn(p.astype(BF16), do_stack)
        dk_acc[window, :] += _nn(ds, q_stack)
        dq_ref[rows, :] = _pick_heads(_tn(ds, k_win), masks).astype(BF16)
    dk_ref[...] = dk_acc[...].astype(BF16)
    dv_ref[...] = dv_acc[...].astype(BF16)


def _columns_early(c, *refs):
    copies = [
        pltpu.make_async_copy(ref.at[:, pl.ds(c * QUAD, QUAD)], buf, refs[10].at[n])
        for n, (ref, buf) in enumerate(zip(refs[:4], refs[6:10]))
    ]
    for copy in copies:
        copy.start()
    return copies


def _attend_back_columns(copies, *refs):
    for copy in copies:
        copy.wait()
    _attend_back_kernel(*refs[9:13], *refs[4:6], *refs[6:9], *refs[14:])


def attend_back(q, k, v, do, fq, fk, c):
    rows = q.shape[0]
    return run(
        _attend_back_columns,
        "attend_back",
        [((rows, QUAD), BF16)] * 3,
        [q, k, v, do, fq, fk],
        "aaaavv",
        scratch=[VMEM((rows, QUAD), BF16)] * 4
        + [pltpu.SemaphoreType.DMA((4,))]
        + [VMEM((rows, QUAD), F32)] * 2,
        early=functools.partial(_columns_early, c),
    )


def _up_kernel(ws, *refs):
    at_ref, h_ref, b_ref = refs[:3]
    pieces = refs[3 : 3 + len(ws.arrays)]
    act_ref, slope_ref, w_ref, buf, sem = refs[3 + len(ws.arrays) :]
    g = pl.program_id(0)
    copies = ws.copies(at_ref, pieces, buf, sem)

    @pl.when(g == 0)
    def _():
        for group in copies:
            for c in group:
                c.start()

    for i in range(GROUPS):

        @pl.when(g == i)
        def _(i=i):
            for c in copies[i]:
                c.wait()

    w_ref[0] = buf[g]
    bias = b_ref[pl.ds(8 + (at_ref[2] ^ g), 1), :]
    for i in range(h_ref.shape[0] // CHUNK):
        rows = slice(i * CHUNK, (i + 1) * CHUNK)
        value, slope = gelu_parts(_nn(h_ref[rows, :], buf[g]) + bias)
        act_ref[0, rows, :] = value.astype(BF16)
        slope_ref[0, rows, :] = slope.astype(BF16)


def at_group(*shape):
    zeros = (0,) * (len(shape) - 1)
    return pl.BlockSpec((1,) + shape[1:], lambda g: (g,) + zeros)


def fixed(*shape):
    zeros = (0,) * len(shape)
    return pl.BlockSpec(shape, lambda g: zeros, pipeline_mode=pl.Buffered(1))


def up_stage(ws, at, h, bias):
    rows, width = h.shape
    hidden = ws.cols
    act = jax.ShapeDtypeStruct((GROUPS, rows, hidden), BF16)
    return pl.pallas_call(
        functools.partial(_up_kernel, ws),
        grid=(GROUPS,),
        out_shape=(act, act, jax.ShapeDtypeStruct((GROUPS, width, hidden), BF16)),
        in_specs=[pl.BlockSpec(memory_space=SMEM), fixed(rows, width), fixed(*bias.shape)]
        + [pl.BlockSpec(memory_space=pltpu.HBM)] * len(ws.arrays),
        out_specs=(
            at_group(GROUPS, rows, hidden),
            at_group(GROUPS, rows, hidden),
            at_group(GROUPS, width, hidden),
        ),
        scratch_shapes=ws.scratch(width),
        compiler_params=pltpu.CompilerParams(vmem_limit_bytes=LIMIT["up"] << 20),
        name="up",
    )(at, h, bias, *ws.arrays)


def _down_kernel(ws, total, images, *refs):
    (
        at_ref, last_ref, act_ref, after_ref, bias_ref, mine_ref, cot_ref, owned_ref, pairs_ref,
        scale_ref, logit_ref,
    ) = refs[:11]
    image_refs, refs = refs[11 : 11 + images], refs[11 + images :]
    pieces = refs[: len(ws.arrays)]
    out_ref, g_ref, low_ref, dbias_ref, dscale_ref, dlogit_ref, w_ref, give_ref, keep_ref, buf, sem, acc, text_buf, image_buf, image_sem = refs[
        len(ws.arrays) :
    ]
    g = pl.program_id(0)
    copies = ws.copies(at_ref, pieces, buf, sem)
    if images == 1:
        pics = [pltpu.make_async_copy(image_refs[0], image_buf, image_sem.at[0])]
    else:
        many = image_refs[0].shape[1] - ws.rows
        pics = [
            pltpu.make_async_copy(
                image_refs[dx].at[zrel, pl.ds(ws.rows, many), pl.ds(0, image_buf.shape[1])],
                image_buf.at[
                    pl.ds(
                        pl.multiple_of(((at_ref[0] ^ zrel) * 2 + (at_ref[1] ^ dx)) * many, many),
                        many,
                    )
                ],
                image_sem.at[2 * zrel + dx],
            )
            for zrel in range(4)
            for dx in range(2)
        ]

    @pl.when(g == 0)
    def _():
        for group in copies:
            for c in group:
                c.start()
        for c in pics:
            c.start()
        acc[...] = after_ref[...] + bias_ref[3:4, :]

    for i in range(GROUPS):

        @pl.when(g == i)
        def _(i=i):
            for c in copies[i]:
                c.wait()

    @pl.when(g < GROUPS)
    def _():
        w_ref[0] = buf[g]
        acc[...] += _nt(act_ref[0], buf[g])

    @pl.when(g == GROUPS - 1)
    def _():
        out_ref[...] = acc[...].astype(BF16)
        caps = text_buf.shape[0]
        for c in range(caps):
            text_buf[c : c + 1, :] = acc[pl.ds(last_ref[c], 1), :]
        mine = mine_ref[...]
        pooled = text_buf[...]
        text_scale = lax.rsqrt(jnp.sum(pooled * pooled, axis=1, keepdims=True) + EPSILON)
        text = pooled * text_scale
        for c in pics:
            c.wait()
        image = image_buf[...].astype(F32)
        image = image * lax.rsqrt(jnp.sum(image * image, axis=1, keepdims=True) + EPSILON)
        scale = jnp.exp(scale_ref[...])
        dots = lax.dot_general(
            text, image, (((1,), (1,)), ((), ())), precision=PRECISE, preferred_element_type=F32
        )
        sign = 2.0 * pairs_ref[...].astype(F32) - 1.0
        logits = scale * dots + logit_ref[...]
        d_logits = (-1.0 / total) * mine * sign / (1.0 + jnp.exp(sign * logits))
        dlogit_ref[...] = jnp.sum(d_logits, keepdims=True)
        dscale_ref[...] = jnp.sum(d_logits * (scale * dots), keepdims=True)
        d_text = scale * _nn(d_logits, image, PRECISE)
        d_pooled = text_scale * (d_text - text * jnp.sum(d_text * text, axis=1, keepdims=True))
        g_ref[...] = cot_ref[...].astype(F32) * owned_ref[...]
        text_buf[...] = d_pooled
        for c in range(caps):
            g_ref[pl.ds(last_ref[c], 1), :] += text_buf[c : c + 1, :]
        rows = g_ref[...]
        low_ref[...] = rows.astype(BF16)
        dbias_ref[...] = col_sum(rows)

    @pl.when((g >= GROUPS) & (g < GROUPS + 2))
    def _():
        give_ref[0] = _tn(low_ref[...], act_ref[0]).astype(BF16)

    @pl.when(g >= GROUPS + 2)
    def _():
        keep_ref[0] = _tn(low_ref[...], act_ref[0]).astype(BF16)


def down_stage(ws, at, last_at, act, after, bias, mine, cot, owned, images, pairs, scale, logit, total):
    rows, width = after.shape
    hidden = ws.cols
    caps = mine.shape[0]
    one = jax.ShapeDtypeStruct((1, 1), F32)
    pair = jax.ShapeDtypeStruct((2, width, hidden), BF16)

    def visit(i):
        return jnp.where(i < GROUPS, i, (2 * (i - GROUPS) + 1) % 5)

    return pl.pallas_call(
        functools.partial(_down_kernel, ws, total, len(images)),
        grid=(2 * GROUPS,),
        out_shape=(
            jax.ShapeDtypeStruct((rows, width), BF16),
            jax.ShapeDtypeStruct((rows, width), F32),
            jax.ShapeDtypeStruct((rows, width), BF16),
            jax.ShapeDtypeStruct((1, width), F32),
            one,
            one,
            jax.ShapeDtypeStruct((GROUPS, width, hidden), BF16),
            pair,
            pair,
        ),
        in_specs=[
            pl.BlockSpec(memory_space=SMEM),
            pl.BlockSpec(memory_space=SMEM),
            pl.BlockSpec((1, rows, hidden), lambda i: (visit(i), 0, 0)),
            fixed(rows, width),
            fixed(*bias.shape),
            fixed(caps, 1),
            fixed(rows, width),
            fixed(rows, 1),
            fixed(*pairs.shape),
            fixed(1, 1),
            fixed(1, 1),
        ]
        + [pl.BlockSpec(memory_space=pltpu.HBM)] * (len(images) + len(ws.arrays)),
        out_specs=(
            fixed(rows, width),
            fixed(rows, width),
            fixed(rows, width),
            fixed(1, width),
            fixed(1, 1),
            fixed(1, 1),
            pl.BlockSpec((1, width, hidden), lambda i: (jnp.minimum(i, GROUPS - 1), 0, 0)),
            pl.BlockSpec((1, width, hidden), lambda i: (jnp.clip(i - GROUPS, 0, 1), 0, 0)),
            pl.BlockSpec((1, width, hidden), lambda i: (jnp.clip(i - GROUPS - 2, 0, 1), 0, 0)),
        ),
        scratch_shapes=ws.scratch(width) + [VMEM((rows, width), F32), VMEM((caps, width), F32), VMEM((pairs.shape[1], width), BF16), pltpu.SemaphoreType.DMA((8,))],
        compiler_params=pltpu.CompilerParams(vmem_limit_bytes=LIMIT["down"] << 20),
        name="down",
    )(
        at, last_at, act, after, bias, mine, cot, owned, pairs, scale.reshape(1, 1),
        logit.reshape(1, 1), *images, *ws.arrays,
    )


def _up_grad_kernel(has_sum, low_ref, h_ref, slope_ref, wd_ref, wu_ref, *refs):
    i = pl.program_id(0)
    grad_ref, bias_ref, dh_ref, d_pre = refs[-4:]

    @pl.when(i == 0)
    def _():
        dh_ref[...] = refs[0][...] if has_sum else jnp.zeros_like(dh_ref)

    d_act = _nn(low_ref[...], wd_ref[0])
    d_pre[...] = (d_act * slope_ref[0].astype(F32)).astype(BF16)
    bias_ref[0] = col_sum(d_pre[...].astype(F32))
    grad_ref[0] = _tn(h_ref[...], d_pre[...]).astype(BF16)
    dh_ref[...] += _nt(d_pre[...], wu_ref[0])


def up_grad(low, h, slope, w_d, w_u, first, so_far=None):
    rows, width = low.shape
    hidden = slope.shape[2]

    def pair(a, b):
        return pl.BlockSpec((1, a, b), lambda i: (2 * i + first, 0, 0))

    extra = [] if so_far is None else [so_far]
    return pl.pallas_call(
        functools.partial(_up_grad_kernel, so_far is not None),
        grid=(2,),
        out_shape=(
            jax.ShapeDtypeStruct((2, width, hidden), BF16),
            jax.ShapeDtypeStruct((2, 1, hidden), F32),
            jax.ShapeDtypeStruct((rows, width), F32),
        ),
        in_specs=[
            fixed(rows, width),
            fixed(rows, width),
            pair(rows, hidden),
            pair(width, hidden),
            pair(width, hidden),
        ]
        + [fixed(rows, width)] * len(extra),
        out_specs=(
            at_group(2, width, hidden),
            at_group(2, 1, hidden),
            fixed(rows, width),
        ),
        scratch_shapes=[VMEM((rows, hidden), BF16)],
        compiler_params=pltpu.CompilerParams(vmem_limit_bytes=LIMIT["up_grad"] << 20),
        name="up_grad",
    )(low, h, slope, w_d, w_u, *extra)


def _up_last_kernel(
    low_ref, h_ref, slope_ref, wd_ref, wu_ref, dh_in_ref, table_ref, g_hbm, after_hbm, att_hbm,
    wo_hbm, grad_ref, bias_ref, after_grad_ref, datt_ref, ograd_ref, dgain_ref, dshift_ref, dob_ref,
    d_pre, dh_ref, g_ref, after_ref, att_ref, wo_ref, sem,
):
    i = pl.program_id(0)
    copies = [
        pltpu.make_async_copy(src, dst, sem.at[n])
        for n, (src, dst) in enumerate(
            ((g_hbm, g_ref), (after_hbm, after_ref), (att_hbm, att_ref), (wo_hbm, wo_ref))
        )
    ]

    @pl.when(i == 0)
    def _():
        for c in copies:
            c.start()

    _up_grad_kernel(
        True, low_ref, h_ref, slope_ref, wd_ref, wu_ref, dh_in_ref, grad_ref, bias_ref, dh_ref, d_pre
    )

    @pl.when(i == 1)
    def _():
        for c in copies:
            c.wait()
        normed, factor = norm_parts(after_ref[...])
        dh = dh_ref[...]
        dgain_ref[...] = col_sum(dh * normed)
        dshift_ref[...] = col_sum(dh)
        d_after = g_ref[...] + norm_back(dh, normed, factor, table_ref[6:7, :])
        after_grad_ref[...] = d_after
        dob_ref[...] = col_sum(d_after)
        low = d_after.astype(BF16)
        datt_ref[...] = _nn(low, wo_ref[...]).astype(BF16)
        ograd_ref[...] = _tn(low, att_ref[...]).astype(BF16)


def up_last(low, h, slope, w_d, w_u, so_far, table, g, after, att, wo):
    rows, width = low.shape
    hidden = slope.shape[2]

    def pair(a, b):
        return pl.BlockSpec((1, a, b), lambda i: (2 * i, 0, 0))

    hbm = pl.BlockSpec(memory_space=pltpu.HBM)
    vec = jax.ShapeDtypeStruct((1, width), F32)
    return pl.pallas_call(
        _up_last_kernel,
        grid=(2,),
        out_shape=(
            jax.ShapeDtypeStruct((2, width, hidden), BF16),
            jax.ShapeDtypeStruct((2, 1, hidden), F32),
            jax.ShapeDtypeStruct((rows, width), F32),
            jax.ShapeDtypeStruct((rows, width), BF16),
            jax.ShapeDtypeStruct((width, width), BF16),
            vec,
            vec,
            vec,
        ),
        in_specs=[
            fixed(rows, width),
            fixed(rows, width),
            pair(rows, hidden),
            pair(width, hidden),
            pair(width, hidden),
            fixed(rows, width),
            fixed(*table.shape),
            hbm,
            hbm,
            hbm,
            hbm,
        ],
        out_specs=(
            at_group(2, width, hidden),
            at_group(2, 1, hidden),
            fixed(rows, width),
            fixed(rows, width),
            fixed(width, width),
            fixed(1, width),
            fixed(1, width),
            fixed(1, width),
        ),
        scratch_shapes=[
            VMEM((rows, hidden), BF16),
            VMEM((rows, width), F32),
            VMEM((rows, width), F32),
            VMEM((rows, width), F32),
            VMEM((rows, width), BF16),
            VMEM((width, width), BF16),
            pltpu.SemaphoreType.DMA((4,)),
        ],
        compiler_params=pltpu.CompilerParams(vmem_limit_bytes=LIMIT["up_last"] << 20),
        name="up_last",
    )(low, h, slope, w_d, w_u, so_far, table, g, after, att, wo)


def _input_early(quads, *refs):
    d_buf, w_buf, sem = refs[-3:]
    width = quads * QUAD
    copies = [
        pltpu.make_async_copy(refs[n], d_buf.at[:, pl.ds(n * QUAD, QUAD)], sem.at[n])
        for n in range(3 * quads)
    ]
    copies += [
        pltpu.make_async_copy(
            refs[3 * quads + n], w_buf.at[:, pl.ds(n * width, width)], sem.at[3 * quads + n]
        )
        for n in range(3)
    ]
    for c in copies:
        c.start()
    return copies


def _input_kernel(quads, shard, copies, *refs):
    (
        after_grad_ref, x_ref, table_ref, at_ref, up_a_ref, up_b_ref,
        ob_ref, db_ref, gain_two_ref, shift_two_ref, scale_ref, logit_ref,
    ) = refs[3 * quads + 3 : 3 * quads + 15]
    out_ref, vec_ref, d_buf, w_buf, sem = refs[3 * quads + 15 :]
    width = quads * QUAD
    normed, factor = norm_parts(x_ref[...].astype(F32))
    for c in copies:
        c.wait()
    d_buf[:, :width] = d_buf[:, :width] * HEAD_DIM ** (-0.5)
    dh = _nt(d_buf[...], w_buf[...])
    vec_ref[...] = jnp.zeros_like(vec_ref)
    me = at_ref[2]
    for i, first in enumerate((0, 2 * width)):
        whole = col_sum(d_buf[:, first : first + width].astype(F32))
        for g in range(GROUPS):
            vec_ref[pl.ds(4 * i + (me ^ g), 1), :shard] = whole[:, g * shard : (g + 1) * shard]
    for g in range(GROUPS):
        ref = up_b_ref if g % 2 == 0 else up_a_ref
        vec_ref[pl.ds(8 + (me ^ g), 1), :] = ref[g // 2]
    rows = [ob_ref[...], db_ref[...], col_sum(dh * normed), col_sum(dh)]
    rows += [gain_two_ref[...], shift_two_ref[...]]
    for i, v in enumerate(rows):
        vec_ref[12 + i : 13 + i, :] = v
    vec_ref[18:19, :1] = scale_ref[...]
    vec_ref[19:20, :1] = logit_ref[...]
    out_ref[...] = (after_grad_ref[...] + norm_back(dh, normed, factor, table_ref[4:5, :])).astype(
        BF16
    )


def _attn_grad_kernel(quads, shard, *refs):
    h_ref, o_ref = refs[3 * quads : 3 * quads + 2]
    give_ref, keep_ref = refs[3 * quads + 2 :]
    place = {1: (give_ref, 0), 3: (give_ref, 1), 0: (keep_ref, 0), 2: (keep_ref, 1)}
    h = h_ref[...]
    for i in range(3):
        for c in range(quads):
            grad = _tn(h, refs[i * quads + c][...])
            if i == 0:
                grad = grad * HEAD_DIM ** (-0.5)
            grad = grad.astype(BF16)
            lo = c * QUAD
            while lo < (c + 1) * QUAD:
                g = lo // shard
                hi = min((g + 1) * shard, (c + 1) * QUAD)
                ref, slot = place[g]
                start = i * shard + lo - g * shard
                ref[slot, :, start : start + hi - lo] = grad[:, lo - c * QUAD : hi - c * QUAD]
                lo = hi
    for g in range(GROUPS):
        ref, slot = place[g]
        ref[slot, :, 3 * shard :] = o_ref[:, g * shard : (g + 1) * shard]


def _add(*vals):
    total = vals[0].astype(F32)
    for v in vals[1:]:
        total = total + v.astype(F32)
    return total.astype(BF16)


def _plane_kernel(at_ref, keep_ref, got_ref, *outs):
    for y in range(2):
        for dx in range(2):
            x = at_ref[1] ^ dx
            for z in range(keep_ref.shape[1]):
                outs[2 * y + dx][z] = _add(keep_ref[y, z, x], got_ref[y, z, x])


def _split_kernel(cut, at_ref, keep_ref, got_ref, own_ref, give_ref, *outs):
    cols = keep_ref.shape[4]
    for dx, ref in enumerate((own_ref, give_ref)):
        x = at_ref[1] ^ dx
        for y in range(2):
            for z in range(keep_ref.shape[1]):
                ref[y, z] = _add(keep_ref[y, z, x, :, :cut], got_ref[y, z, x, :, :cut])
    for j, ref in enumerate(outs):
        z = at_ref[0] ^ j
        for y in range(2):
            for x in range(2):
                ref[y, x] = _add(keep_ref[y, z, x, :, cut:], got_ref[y, z, x, :, cut:])


def by_block(mv, a):
    return a.reshape(2, mv.nz, 2, a.shape[1] // mv.n, a.shape[2])


def plane_parts(mv, keep, got):
    keep, got = by_block(mv, keep), by_block(mv, got)
    out = ((mv.nz,) + keep.shape[3:], BF16)
    return run(_plane_kernel, "plane_parts", [out] * 4, [mv.at, keep, got], "svv")


def split_parts(mv, keep, got, cut):
    keep, got = by_block(mv, keep), by_block(mv, got)
    rows, cols = keep.shape[3:]
    outs = [((2, mv.nz, rows, cut), BF16)] * 2 + [((2, 2, rows, cols - cut), BF16)] * 4
    kernel = functools.partial(_split_kernel, cut)
    return run(kernel, "plane_parts", outs, [mv.at, keep, got], "svv")


def _z_kernel(count, at_ref, *refs):
    ins, outs = refs[:count], refs[count:]
    for j in range(4):
        b = at_ref[0] ^ j
        outs[j][...] = _add(*[r[b] for r in ins])


def z_parts(mv, held):
    out = (held[0].shape[1:], BF16)
    kernel = functools.partial(_z_kernel, len(held))
    return run(kernel, "z_parts", [out] * 4, [mv.at, *held], "s" + "v" * len(held))


def _join_kernel(at_ref, a_ref, b_ref, *refs):
    ins, outs, (own_ref, give_ref) = refs[:4], refs[4:8], refs[8:]
    for j in range(4):
        b = at_ref[0] ^ j
        for y in range(2):
            outs[j][y] = _add(a_ref[y, b], b_ref[y, b])
    for dx, ref in enumerate((own_ref, give_ref)):
        x = at_ref[1] ^ dx
        for y in range(2):
            ref[y] = _add(*[r[y, x] for r in ins])


def join_parts(mv, own, got, held):
    outs = [((2,) + own.shape[2:], BF16)] * 4 + [((2,) + held[0].shape[2:], BF16)] * 2
    return run(_join_kernel, "z_parts", outs, [mv.at, own, got, *held], "s" + "v" * 6)


def _spread_kernel(piece, at_ref, keep_ref, *refs):
    out_ref = refs[-1]
    wins = [(refs[0],), (refs[1],), (refs[2], refs[3]), (refs[4], refs[5])]
    j = pl.program_id(0)
    here = j ^ at_ref[2]
    before = (j - 1) ^ at_ref[2]
    for i in range(4):

        @pl.when(here == i)
        def _(i=i):
            done = 0
            for ref in wins[i]:
                rows = min(ref.shape[0], piece - done)
                out_ref[done : done + rows, :] = ref[:rows, :].astype(out_ref.dtype)
                done += rows

    for i in range(4):

        @pl.when((before == i) & (j > 0))
        def _(i=i):
            ref = wins[i][-1]
            tail = ref[ref.shape[0] - HALO :, :].astype(out_ref.dtype)
            out_ref[:HALO, :] = jnp.where(keep_ref[0] > 0, out_ref[:HALO, :], tail)


def spread(at, keep, windows, piece, dtype):
    cols = windows[0].shape[1]
    return pl.pallas_call(
        functools.partial(_spread_kernel, piece),
        grid=(GROUPS,),
        out_shape=jax.ShapeDtypeStruct((GROUPS * piece, cols), dtype),
        in_specs=[pl.BlockSpec(memory_space=SMEM), at_group(GROUPS, HALO, 1)]
        + [fixed(*w.shape) for w in windows],
        out_specs=pl.BlockSpec((piece, cols), lambda j: (j, 0)),
        compiler_params=pltpu.CompilerParams(vmem_limit_bytes=LIMIT["spread"] << 20),
        name="spread",
    )(at, keep, *windows)


def _spread_first_kernel(piece, at_ref, own_ref, near_ref, far_ref, out_ref, *rest):
    bufs, sem = rest[:3], rest[3]
    copies = []
    for i, ref in enumerate((own_ref, near_ref, far_ref)):
        rows = min(ref.shape[0], piece)
        bufs[i][...] = ref[:rows, :].astype(F32)
        start = pl.multiple_of((at_ref[2] ^ i) * piece, piece)
        copies.append(pltpu.make_async_copy(bufs[i], out_ref.at[pl.ds(start, rows)], sem.at[i]))
        copies[-1].start()
    for c in copies:
        c.wait()


def spread_first(at, own, near, far, piece):
    rows, cols = own.shape
    wins = (own, near, far)
    return pl.pallas_call(
        functools.partial(_spread_first_kernel, piece),
        out_shape=jax.ShapeDtypeStruct((GROUPS * piece, cols), F32),
        in_specs=[pl.BlockSpec(memory_space=SMEM)] + [pl.BlockSpec(memory_space=VMEM)] * 3,
        out_specs=pl.BlockSpec(memory_space=pltpu.HBM),
        scratch_shapes=[VMEM((min(w.shape[0], piece), cols), F32) for w in wins]
        + [pltpu.SemaphoreType.DMA((3,))],
        compiler_params=pltpu.CompilerParams(vmem_limit_bytes=LIMIT["spread"] << 20),
        name="spread",
    )(at, *wins)


def _spread_last_kernel(piece, at_ref, keep_ref, *refs):
    heads, tails, parts = refs[:4], refs[4:8], refs[8:11]
    out_ref, bufs, head_bufs, sem = refs[12], refs[13:16], refs[16], refs[17]
    copies = []
    for n, (ref, side, first) in enumerate(zip(parts, (2, 3, 3), (1, 0, 1))):
        rows = bufs[n].shape[0]
        bufs[n][...] = ref[:rows, :].astype(F32)
        start = (at_ref[2] ^ side) * piece + first * (piece - rows)
        copies.append(
            pltpu.make_async_copy(
                bufs[n], out_ref.at[pl.ds(pl.multiple_of(start, HALO // 2), rows)], sem.at[n]
            )
        )
        copies[-1].start()
    for c in copies:
        c.wait()
    copies = []
    for j in range(1, GROUPS):
        for i in range(4):

            @pl.when((at_ref[2] ^ j) == i)
            def _(i=i, j=j):
                head_bufs[j - 1] = heads[i][...].astype(F32)

        for i in range(4):

            @pl.when((at_ref[2] ^ (j - 1)) == i)
            def _(i=i, j=j):
                head_bufs[j - 1] = jnp.where(
                    keep_ref[j] > 0, head_bufs[j - 1], tails[i][...].astype(F32)
                )

        copies.append(
            pltpu.make_async_copy(
                head_bufs.at[j - 1], out_ref.at[pl.ds(j * piece, HALO)], sem.at[2 + j]
            )
        )
        copies[-1].start()
    for c in copies:
        c.wait()


def spread_last(at, keep, firsts, lasts, so_far, piece):
    cols = so_far.shape[1]
    split = firsts[2].shape[0]
    heads = [f[:HALO] for f in firsts]
    tails = [t[t.shape[0] - HALO :] for t in lasts]
    vmem = pl.BlockSpec(memory_space=VMEM)
    return pl.pallas_call(
        functools.partial(_spread_last_kernel, piece),
        out_shape=jax.ShapeDtypeStruct(so_far.shape, F32),
        in_specs=[pl.BlockSpec(memory_space=SMEM)]
        + [vmem] * 12
        + [pl.BlockSpec(memory_space=pltpu.HBM)],
        out_specs=pl.BlockSpec(memory_space=pltpu.HBM),
        scratch_shapes=[VMEM((rows, cols), F32) for rows in (piece - split, split, piece - split)]
        + [VMEM((3, HALO, cols), F32), pltpu.SemaphoreType.DMA((6,))],
        input_output_aliases={13: 0},
        compiler_params=pltpu.CompilerParams(vmem_limit_bytes=LIMIT["spread"] << 20),
        name="spread",
    )(at, keep, *heads, *tails, lasts[2], firsts[3], lasts[3], so_far)


def _flip(a, axis, bit):
    n = lax.axis_size(axis)
    return lax.ppermute(a, axis, [(i, i ^ bit) for i in range(n)])


def fence(*trees):
    return lax.optimization_barrier(trees)


def add_low(a, b):
    return (a.astype(F32) + b.astype(F32)).astype(BF16)


class Moves:
    def __init__(self):
        self.n = lax.axis_size("dp")
        self.nz = self.n // 2
        at = lax.axis_index("dp")
        self.at = jnp.stack([at // 2, at % 2, lax.axis_index("mp")]).astype(jnp.int32)
        self.near = self.n == 8

    def z_all(self, a):
        return [a] + [_flip(a, "dp", 2 * j) for j in range(1, 4)]

    def cross_flip(self, a):
        return lax.ppermute(
            a,
            ("dp", "mp"),
            [(4 * d + m, 4 * (d ^ 1) + (m ^ 2)) for d in range(self.n) for m in range(4)],
        )

    def plane_all(self, a):
        return [a, _flip(a, "dp", 1), _flip(a, "mp", 2), self.cross_flip(a)]

    def core_all(self, parts):
        return [_flip(a, "mp", 1) for a in parts]

    def gather_far(self, a):
        mine = lax.all_gather(a, "dp", axis=0, tiled=True)
        far = _flip(mine, "mp", 2)
        whole = jnp.stack([mine, _flip(mine, "mp", 1), far, _flip(far, "mp", 1)])
        return Weights([whole], None, a.shape[0], a.shape[1])

    def to_core(self, give):
        return _flip(give, "mp", 1)

    def scatter_far(self, keep, got):
        both = add_low(keep, got)
        mine = add_low(both[0], _flip(both[1], "mp", 2))
        return lax.psum_scatter(mine, "dp", scatter_dimension=0, tiled=True).astype(F32)

    def plane_sides(self, parts):
        return [
            parts[0], _flip(parts[1], "dp", 1), _flip(parts[2], "mp", 2), self.cross_flip(parts[3]),
        ]

    def z_sides(self, parts):
        return [_flip(parts[j], "dp", 2 * j) for j in range(1, 4)]


PLANE = [(dx, dy) for dy in range(2) for dx in range(2)]


def z_then_plane(first, col, cut, wide):
    return [
        (first + 4 * core + i, (zrel,), zrel, dx, core + 2 * dy, col, cut, wide)
        for core in range(2)
        for i, (dx, dy) in enumerate(PLANE)
        for zrel in range(4)
    ]


def plane_then_z(first, col, cut, wide):
    return [
        (first + 4 * core + zrel, (i,), zrel, dx, core + 2 * dy, col, cut, wide)
        for core in range(2)
        for zrel in range(4)
        for i, (dx, dy) in enumerate(PLANE)
    ]


def body(
    tokens,
    out_cot,
    seg_ids,
    valid_mask,
    last_pos,
    pairs,
    images,
    q_weight,
    k_weight,
    v_weight,
    o_weight,
    up_weight,
    down_weight,
    q_bias,
    v_bias,
    o_bias,
    up_bias,
    down_bias,
    gain_one,
    shift_one,
    gain_two,
    shift_two,
    log_scale,
    logit_bias,
):
    mv = Moves()
    assert lax.axis_size("mp") == GROUPS
    row_count, seq_len = seg_ids.shape
    token_count, width = tokens.shape
    piece = token_count // GROUPS
    caption_total = pairs.shape[0] * mv.n
    at = lax.axis_index("mp")
    shard = q_weight.shape[1]
    hidden = up_weight.shape[1]
    block = q_weight.shape[0]
    quads = width // QUAD

    own_a = jnp.concatenate([q_weight, k_weight, v_weight, o_weight.T], axis=1)
    down_t = down_weight.T
    cut = QUAD
    if mv.near:
        a_z = mv.z_all(own_a)
        a_z[1], up_weight, down_t, images = fence(a_z[1], up_weight, down_t, images)
        own_1 = jnp.concatenate([up_weight, down_t[:, :cut]], axis=1)
        own_1 = jnp.concatenate([own_1, jnp.pad(images, ((0, 0), (0, cut)))], axis=0)
        w2_plane = mv.plane_all(down_t[:, cut:])
        a_z, own_1, w2_plane = fence(a_z, own_1, w2_plane)
        a_here = jnp.stack(a_z)
        a_here, tokens, out_cot, seg_ids, valid_mask, last_pos, q_bias = fence(
            a_here, tokens, out_cot, seg_ids, valid_mask, last_pos, q_bias
        )
        a_plane = mv.plane_all(a_here)
        w1_z = mv.z_all(own_1)

    start = at * piece
    tail = jnp.minimum(start + piece, token_count - HALO)

    def window(a):
        return jnp.concatenate(
            [
                lax.dynamic_slice_in_dim(a, start, piece),
                lax.dynamic_slice_in_dim(a, tail, HALO),
            ],
            axis=0,
        )

    flat_at = jnp.arange(token_count, dtype=jnp.int32)
    caption_id = jnp.where(
        valid_mask.reshape(-1) > 0,
        (flat_at // seq_len) * (last_pos.shape[1] * 2) + seg_ids.reshape(-1),
        (1 << 20) + flat_at,
    )
    inside = at < GROUPS - 1
    ids = window(caption_id)
    tail_ids = jnp.where(inside, ids[piece:], -2 - jnp.arange(HALO, dtype=jnp.int32))
    ids = jnp.concatenate([ids[:piece], tail_ids])
    before = jnp.where(
        at > 0, lax.dynamic_index_in_dim(caption_id, jnp.maximum(start - 1, 0), keepdims=False), -1
    )
    owned = jnp.concatenate([ids[:piece] != before, (tail_ids == ids[piece - 1]) & inside])
    by_piece = caption_id.reshape(GROUPS, piece)
    last_before = jnp.concatenate([jnp.full((1,), -1, jnp.int32), by_piece[:-1, -1]])
    keep_head = (by_piece[:, :HALO] != last_before[:, None]).astype(F32)[:, :, None]
    count = piece + HALO
    places = start + jnp.arange(count, dtype=jnp.int32)
    fq = ids[:, None]
    blocks = count // HALO
    fk = jnp.concatenate([ids.reshape(blocks, HALO)] * 4, axis=1)[:, None, :]

    flat_last = (
        last_pos + seq_len * jnp.arange(row_count, dtype=jnp.int32)[:, None]
    ).reshape(-1)
    last_at = jnp.clip(flat_last - start, 0, count - 1)
    mine = jnp.any((flat_last[:, None] == places[None, :]) & owned[None, :], axis=1)
    mine = mine.astype(F32)[:, None]
    x_rows = window(tokens)
    cot = window(out_cot)
    owned_rows = owned.astype(F32)[:, None]

    table = jnp.concatenate(
        [q_bias, v_bias, o_bias, down_bias, gain_one, shift_one, gain_two, shift_two, up_bias]
    ).reshape(-1, width)
    if mv.near:
        small = (x_rows, cot, fq, fk, last_at, mine, owned_rows, keep_head, table)
        a_plane, w1_z, w2_plane, small = fence(a_plane, w1_z, w2_plane, small)
        x_rows, cot, fq, fk, last_at, mine, owned_rows, keep_head, table = small
        a_core = [mv.to_core(v) for v in a_plane]
        w_a = Weights(a_plane + a_core, z_then_plane(0, 0, 0, hidden), block, hidden)
        w1_here, w2_here = jnp.stack(w1_z), jnp.stack(w2_plane)
        w1_x, w1_y = _flip(w1_here, "dp", 1), _flip(w1_here, "mp", 2)
        w2_near = [_flip(w2_here, "dp", 2), _flip(w2_here, "dp", 4)]
    else:
        w_a, w_u, w_d = (mv.gather_far(v) for v in (own_a, up_weight, down_t))
        pics = [lax.all_gather(images, "dp", axis=0, tiled=True)]

    rows_low = ((count, width), BF16)
    square = ((width, width), BF16)
    h_one, queries, keys, vals, w_q, w_k, w_v, w_o = run(
        functools.partial(_qkv_kernel, w_a, width, shard),
        "qkv",
        [rows_low] * 4 + [square] * 4,
        [mv.at, x_rows, table, *w_a.arrays],
        "svv" + "a" * len(w_a.arrays),
        scratch=w_a.scratch(width),
        early=functools.partial(_qkv_early, w_a),
    )
    if mv.near:
        queries, keys, vals, w1_here, w2_here, w1_x, w1_y, w2_near = fence(
            queries, keys, vals, w1_here, w2_here, w1_x, w1_y, w2_near
        )
        w1_cross, w2_last = mv.cross_flip(w1_here), _flip(w2_here, "dp", 6)
        w1_core = [mv.to_core(v) for v in (w1_here, w1_x, w1_y)]
    attended, after_attn, h_two = run(
        _attend_kernel,
        "attend",
        [rows_low, ((count, width), F32), rows_low],
        [queries, keys, vals, fq, fk, w_o, x_rows, table],
    )
    if mv.near:
        h_two, w1_cross, w2_last, w1_core = fence(h_two, w1_cross, w2_last, w1_core)
        pics = [w1_here, w1_x]
        w1_all = [w1_here, w1_x, w1_y, w1_cross, *w1_core, mv.to_core(w1_cross)]
        w_u = Weights(w1_all, z_then_plane(0, 0, 0, hidden), block, hidden)
        w2_all = [w2_here, *w2_near, w2_last]
        w2_all = w2_all + [mv.to_core(v) for v in w2_all]
    acts, slopes, w_up = up_stage(w_u, mv.at, h_two, table)
    if mv.near:
        w2_all, acts = fence(w2_all, acts)
        w_d = Weights(
            w1_all + w2_all,
            z_then_plane(0, 0, hidden, cut) + plane_then_z(8, cut, 0, hidden - cut),
            block,
            hidden,
        )
    out_low, g_rows, g_low, d_down_bias, d_scale, d_logit, w_down, down_give, down_keep = down_stage(
        w_d, mv.at, last_at, acts, after_attn, table, mine, cot, owned_rows, pics, pairs,
        log_scale, logit_bias, caption_total,
    )

    split = count // 2
    down_got = mv.to_core(down_give)
    out_a, out_near = _flip(out_low[:split], "mp", 2), _flip(out_low, "mp", 1)
    up_give, up_bias_a, d_h_two = up_grad(g_low, h_two, slopes, w_down, w_up, 1)
    down_got, up_give, d_h_two, out_a, out_near = fence(
        down_got, up_give, d_h_two, out_a, out_near
    )
    up_got = mv.to_core(up_give)
    out_cross_a = _flip(out_a, "mp", 1)
    if mv.near:
        sent = plane_parts(mv, down_keep, down_got)
        sent, d_h_two = fence(sent, d_h_two)
        down_held = mv.plane_sides(sent)
    up_keep, up_bias_b, d_after, d_attended, o_grad, d_gain_two, d_shift_two, d_o_bias = up_last(
        g_low, h_two, slopes, w_down, w_up, d_h_two, table, g_rows, after_attn, attended, w_o
    )
    parts = [attend_back(queries, keys, vals, d_attended, fq, fk, 0)]
    if mv.near:
        sent = plane_parts(mv, up_keep, up_got)
        down_held, sent, parts, out_cross_a = fence(
            down_held, sent, parts, out_cross_a
        )
        down_sent = z_parts(mv, down_held)
        down_sent, sent, d_attended = fence(down_sent, sent, d_attended)
        up_held = mv.plane_sides(sent)
        down_pieces = [down_sent[0]] + [_flip(down_sent[j], "dp", 2 * j) for j in (1, 2)]
    for c in range(1, quads):
        parts.append(attend_back(queries, keys, vals, d_attended, fq, fk, c))
    if mv.near:
        parts, up_held, down_pieces = fence(parts, up_held, down_pieces)
        sent = z_parts(mv, up_held)
        sent, parts = fence(sent, parts)
        up_pieces = [sent[0]] + mv.z_sides(sent)
        down_pieces.append(_flip(down_sent[3], "dp", 6))
    flat = [p[i] for i in range(3) for p in parts]
    out_b = _flip(out_low[split:], "mp", 2)
    d_tokens, summed = run(
        functools.partial(_input_kernel, quads, shard),
        "input",
        [rows_low, ((24, hidden), F32)],
        [
            *flat, w_q, w_k, w_v, d_after, x_rows, table, mv.at, up_bias_a, up_bias_b,
            d_o_bias, d_down_bias, d_gain_two, d_shift_two, d_scale, d_logit,
        ],
        "a" * (3 * quads + 3) + "vvvs" + "v" * 8,
        scratch=[
            VMEM((count, 3 * width), BF16),
            VMEM((width, 3 * width), BF16),
            pltpu.SemaphoreType.DMA((3 * quads + 3,)),
        ],
        early=functools.partial(_input_early, quads),
    )
    if mv.near:
        d_tokens, flat, summed, up_pieces, down_pieces, out_b = fence(
            d_tokens, flat, summed, up_pieces, down_pieces, out_b
        )
        summed = summed + _flip(summed, "mp", 1)
    out_cross_b = _flip(out_b, "mp", 1)
    grad_near = _flip(d_tokens, "mp", 1)
    attn_give, attn_keep = run(
        functools.partial(_attn_grad_kernel, quads, shard),
        "attn_grad",
        [((2, width, hidden), BF16)] * 2,
        [*flat, h_one, o_grad],
    )
    attn_give, attn_keep, summed, out_cross_b, d_tokens, grad_near = fence(
        attn_give, attn_keep, summed, out_cross_b, d_tokens, grad_near
    )
    attn_got = mv.to_core(attn_give)
    if mv.near:
        summed = mv.plane_all(summed)
        attn_got, summed = fence(attn_got, summed)
        cut = 2 * QUAD
        own_a, sent_a, *sent = split_parts(mv, attn_keep, attn_got, cut)
        sent_a, sent, d_tokens = fence(sent_a, sent, d_tokens)
        side_a = _flip(sent_a, "dp", 1)
        pieces_b = [sent[0]] + mv.z_sides(sent)
    far_a = _flip(d_tokens[:split], "mp", 2)

    def low_sum(pieces):
        return sum(v.astype(F32) for v in pieces)

    if mv.near:
        side_a, pieces_b, far_a, out_cross_b = fence(side_a, pieces_b, far_a, out_cross_b)
        *sent, own_b, sent_b = join_parts(mv, own_a, side_a, pieces_b)
        sent, sent_b, d_tokens, out_cross_b = fence(sent, sent_b, d_tokens, out_cross_b)
        pieces_a = [sent[0]] + mv.z_sides(sent)
        side_b = _flip(sent_b, "dp", 1)
    far_b = _flip(d_tokens[split:], "mp", 2)
    grad_first = spread_first(mv.at, d_tokens, grad_near, far_a, piece)
    layer_out = spread(
        mv.at, keep_head, [out_low, out_near, out_a, out_b, out_cross_a, out_cross_b], piece, BF16
    )
    if mv.near:
        pieces_a, side_b, far_a, far_b, summed, layer_out, grad_first = fence(
            pieces_a, side_b, far_a, far_b, summed, layer_out, grad_first
        )
    if mv.near:
        summed = mv.z_all((summed[0] + summed[1]) + (summed[2] + summed[3]))
        sum_a, sum_b = low_sum(pieces_a), low_sum([own_b, side_b])
        both = jnp.concatenate([sum_a, sum_b], axis=2)
        attn_far = _flip(both[1].astype(BF16), "mp", 2)
    else:
        summed = lax.psum(summed, ("dp", "mp"))
        grad_down = mv.scatter_far(down_keep, down_got).T
        grad_up = mv.scatter_far(up_keep, up_got)
        grad_attn = mv.scatter_far(attn_keep, attn_got)
    grad_cross_a, grad_cross_b = _flip(far_a, "mp", 1), _flip(far_b, "mp", 1)
    grad_tokens = spread_last(
        mv.at, keep_head, [d_tokens, grad_near, far_a, grad_cross_a],
        [d_tokens, grad_near, far_b, grad_cross_b], grad_first, piece,
    )
    if mv.near:
        grad_tokens, summed, attn_far = fence(grad_tokens, summed, attn_far)
        summed = (summed[0] + summed[1]) + (summed[2] + summed[3])
        grad_down = low_sum(down_pieces).T
        grad_up = low_sum(up_pieces)
        grad_attn = both[0] + attn_far.astype(F32)

    def mine_of(first):
        return lax.dynamic_index_in_dim(summed, first + at, 0, keepdims=False)

    out_vectors = [mine_of(0)[:shard], mine_of(4)[:shard], summed[12], mine_of(8)]
    out_vectors += [summed[i] for i in range(13, 18)] + [summed[18, :1], summed[19, :1]]

    return (
        layer_out,
        grad_tokens,
        grad_attn[:, :shard],
        grad_attn[:, shard : 2 * shard],
        grad_attn[:, 2 * shard : 3 * shard],
        grad_attn[:, 3 * shard :].T,
        grad_up,
        grad_down,
        *out_vectors,
    )


def solution(mesh):
    rows, weight, weight_t = P("dp", None), P("dp", "mp"), P("mp", "dp")
    placed = (rows,) * 7 + (weight,) * 3 + (weight_t, weight, weight_t) + (P(),) * 11
    return jax.shard_map(
        body,
        mesh=mesh,
        in_specs=placed,
        out_specs=(rows,) * 2
        + (weight,) * 3
        + (weight_t, weight, weight_t)
        + (P("mp"), P("mp"), P(), P("mp"))
        + (P(),) * 7,
        check_vma=False,
    )
```

```python
import functools

import jax
import jax.numpy as jnp
from jax import lax
from jax.experimental import pallas as pl
from jax.experimental.pallas import tpu as pltpu
from jax.sharding import PartitionSpec as P

HEAD_DIM = 64
HALO = 64
QUAD = 4 * HEAD_DIM
CHUNK = 208
EPSILON = 1e-06
MASKED = -1000000000.0
PRECISE = lax.Precision.HIGHEST
F32 = jnp.float32
BF16 = jnp.bfloat16
VMEM = pltpu.VMEM
SMEM = pltpu.SMEM
GROUPS = 4
LIMIT = dict(up_last=44, plane_parts=10, qkv=62, attend=62, attend_back=30, up=40, down=48, down_grad=16, up_grad=32, middle=20, input=30, attn_grad=40, z_parts=6, spread=40)


def _nt(a, b):
    return lax.dot_general(a, b, (((1,), (1,)), ((), ())), preferred_element_type=F32)


def _tn(a, b):
    return lax.dot_general(a, b, (((0,), (0,)), ((), ())), preferred_element_type=F32)


def _nn(a, b, precision=None):
    return lax.dot_general(
        a, b, (((1,), (0,)), ((), ())), precision=precision, preferred_element_type=F32
    )


def norm_parts(values):
    center = values - jnp.mean(values, axis=-1, keepdims=True)
    factor = lax.rsqrt(jnp.mean(center * center, axis=-1, keepdims=True) + EPSILON)
    return (center * factor, factor)


def norm_back(grad_rows, normed, factor, gain_vec):
    shaped = grad_rows * gain_vec
    first_mean = jnp.mean(shaped, axis=-1, keepdims=True)
    second_mean = jnp.mean(shaped * normed, axis=-1, keepdims=True)
    return factor * (shaped - first_mean - normed * second_mean)


def gelu_parts(u):
    k = 0.7978845608028654
    sq = u * u
    t = jnp.tanh(k * (u + 0.044715 * (sq * u)))
    half = 0.5 * (1.0 + t)
    slope = half + 0.5 * u * (1.0 - t * t) * (k * (1.0 + 3.0 * 0.044715 * sq))
    return u * half, slope


def col_sum(a):
    return jnp.sum(a, axis=0, keepdims=True)


def staged(kernel, spaces, n_out, early, *refs):
    n_in = len(spaces)
    moved = [i for i, c in enumerate(spaces) if c == "v"]
    ins, outs = list(refs[:n_in]), refs[n_in : n_in + n_out]
    rest = refs[n_in + n_out :]
    in_bufs, out_bufs = rest[: len(moved)], rest[len(moved) : len(moved) + n_out]
    sem = rest[len(moved) + n_out]
    rest = rest[len(moved) + n_out + 1 :]
    copies = [
        pltpu.make_async_copy(ins[i], buf, sem.at[n]) for n, (i, buf) in enumerate(zip(moved, in_bufs))
    ]
    for c in copies:
        c.start()
    own = [] if early is None else [early(*ins, *rest)]
    for c in copies:
        c.wait()
    for i, buf in zip(moved, in_bufs):
        ins[i] = buf
    kernel(*own, *ins, *out_bufs, *rest)
    copies = [
        pltpu.make_async_copy(buf, ref, sem.at[len(moved) + n])
        for n, (buf, ref) in enumerate(zip(out_bufs, outs))
    ]
    for c in copies:
        c.start()
    for c in copies:
        c.wait()


def run(kernel, name, outs, ins, spaces=None, scratch=(), early=None):
    spaces = spaces or "v" * len(ins)
    moved = [a for a, c in zip(ins, spaces) if c == "v"]
    hbm, smem = pl.BlockSpec(memory_space=pltpu.HBM), pl.BlockSpec(memory_space=SMEM)
    return pl.pallas_call(
        functools.partial(staged, kernel, spaces, len(outs), early),
        out_shape=tuple(jax.ShapeDtypeStruct(s, d) for s, d in outs),
        in_specs=[smem if c == "s" else hbm for c in spaces],
        out_specs=tuple(hbm for _ in outs),
        scratch_shapes=[VMEM(a.shape, a.dtype) for a in moved]
        + [VMEM(s, d) for s, d in outs]
        + [pltpu.SemaphoreType.DMA((len(moved) + len(outs),))]
        + list(scratch),
        compiler_params=pltpu.CompilerParams(vmem_limit_bytes=LIMIT[name] << 20),
        name=name,
    )(*ins)


def copies_of(plan, rows, at_ref, refs, buf, sem):
    z, x = at_ref[0], at_ref[1]
    out = [[] for _ in range(GROUPS)]
    for n, (src, first, zrel, dx, group, col, cut, wide) in enumerate(plan):
        slot = pl.multiple_of(((z ^ zrel) * 2 + (x ^ dx)) * rows, rows)
        out[group].append(
            pltpu.make_async_copy(
                refs[src].at[(*first, pl.ds(0, rows), pl.ds(cut, wide))],
                buf.at[group, pl.ds(slot, rows), pl.ds(col, wide)],
                sem.at[n],
            )
        )
    return out


def whole_copies(ref, buf, sem):
    return [[pltpu.make_async_copy(ref.at[g], buf.at[g], sem.at[g])] for g in range(GROUPS)]


class Weights:
    def __init__(self, arrays, plan, rows, cols):
        self.arrays, self.plan, self.rows, self.cols = arrays, plan, rows, cols

    def scratch(self, width):
        count = GROUPS if self.plan is None else len(self.plan)
        return [VMEM((GROUPS, width, self.cols), BF16), pltpu.SemaphoreType.DMA((count,))]

    def copies(self, at_ref, refs, buf, sem):
        if self.plan is None:
            return whole_copies(refs[0], buf, sem)
        return copies_of(self.plan, self.rows, at_ref, refs, buf, sem)


def _head_masks(rows):
    lane = lax.broadcasted_iota(jnp.int32, (rows, QUAD), 1) // HEAD_DIM
    return [lane == h for h in range(4)]


def _stack_heads(block, masks):
    zero = jnp.zeros_like(block)
    return jnp.concatenate([jnp.where(m, block, zero) for m in masks], axis=0)


def _pick_heads(stacked, masks):
    rows = stacked.shape[0] // 4
    out = stacked[:rows]
    for h in range(1, 4):
        out = jnp.where(masks[h], stacked[h * rows : (h + 1) * rows], out)
    return out


def _probs(k_win, q_stack, allowed):
    scores = jnp.where(allowed, _nt(k_win, q_stack), MASKED)
    top = jnp.max(scores, axis=0, keepdims=True)
    e = jnp.exp(scores - top)
    return e * (1.0 / jnp.sum(e, axis=0, keepdims=True))


def _blocks(total):
    for b in range(total // HALO):
        first = min(max(b - 1, 0) * HALO, total - 3 * HALO)
        yield b, slice(b * HALO, (b + 1) * HALO), slice(first, first + 3 * HALO)


def _qkv_early(ws, at_ref, x_ref, table_ref, *refs):
    copies = ws.copies(at_ref, refs[: len(ws.arrays)], *refs[len(ws.arrays) :])
    for group in copies:
        for c in group:
            c.start()
    return copies


def _qkv_kernel(ws, width, shard, copies, *refs):
    at_ref, x_ref, table_ref = refs[:3]
    h_ref, q_ref, k_ref, v_ref, wq_ref, wk_ref, wv_ref, wo_ref, buf, sem = refs[
        3 + len(ws.arrays) :
    ]
    normed = norm_parts(x_ref[...].astype(F32))[0]
    h_ref[...] = (normed * table_ref[4:5, :] + table_ref[5:6, :]).astype(BF16)
    h = h_ref[...]
    for g in range(GROUPS):
        for c in copies[g]:
            c.wait()
        cols = slice(g * shard, (g + 1) * shard)
        r = _nn(h, buf[g])
        own = at_ref[2] ^ g
        q_bias, v_bias = (
            sum(
                jnp.where(own == j, table_ref[i : i + 1, j * shard : (j + 1) * shard], 0.0)
                for j in range(GROUPS)
            )
            for i in range(2)
        )
        q_ref[:, cols] = ((r[:, :shard] + q_bias) * HEAD_DIM ** (-0.5)).astype(BF16)
        k_ref[:, cols] = r[:, shard : 2 * shard].astype(BF16)
        v_ref[:, cols] = (r[:, 2 * shard : 3 * shard] + v_bias).astype(BF16)
        for i, ref in enumerate((wq_ref, wk_ref, wv_ref, wo_ref)):
            ref[:, cols] = buf[g, :, i * shard : (i + 1) * shard]


def _attend_kernel(
    q_ref, k_ref, v_ref, ids_ref, own_ref, wo_ref, x_ref, table_ref,
    o_ref, after_ref, h_ref,
):
    masks = _head_masks(HALO)
    for b, rows, window in _blocks(q_ref.shape[0]):
        allowed = ids_ref[window, :] == own_ref[b]
        for c in range(q_ref.shape[1] // QUAD):
            cols = slice(c * QUAD, (c + 1) * QUAD)
            q_stack = _stack_heads(q_ref[rows, cols], masks)
            p = _probs(k_ref[window, cols], q_stack, allowed).astype(BF16)
            o_ref[rows, cols] = _pick_heads(_tn(p, v_ref[window, cols]), masks).astype(BF16)
    after_ref[...] = x_ref[...].astype(F32) + _nt(o_ref[...], wo_ref[...]) + table_ref[2:3, :]
    normed = norm_parts(after_ref[...])[0]
    h_ref[...] = (normed * table_ref[6:7, :] + table_ref[7:8, :]).astype(BF16)


def _attend_back_kernel(
    q_ref, k_ref, v_ref, do_ref, ids_ref, own_ref, dq_ref, dk_ref, dv_ref, dk_acc, dv_acc
):
    masks = _head_masks(HALO)
    dk_acc[...] = jnp.zeros_like(dk_acc)
    dv_acc[...] = jnp.zeros_like(dv_acc)
    for b, rows, window in _blocks(q_ref.shape[0]):
        allowed = ids_ref[window, :] == own_ref[b]
        q_stack = _stack_heads(q_ref[rows, :], masks)
        do_stack = _stack_heads(do_ref[rows, :], masks)
        k_win = k_ref[window, :]
        p = _probs(k_win, q_stack, allowed)
        dp = _nt(v_ref[window, :], do_stack)
        ds = (p * (dp - jnp.sum(p * dp, axis=0, keepdims=True))).astype(BF16)
        dv_acc[window, :] += _nn(p.astype(BF16), do_stack)
        dk_acc[window, :] += _nn(ds, q_stack)
        dq_ref[rows, :] = _pick_heads(_tn(ds, k_win), masks).astype(BF16)
    dk_ref[...] = dk_acc[...].astype(BF16)
    dv_ref[...] = dv_acc[...].astype(BF16)


def _columns_early(c, *refs):
    copies = [
        pltpu.make_async_copy(ref.at[:, pl.ds(c * QUAD, QUAD)], buf, refs[10].at[n])
        for n, (ref, buf) in enumerate(zip(refs[:4], refs[6:10]))
    ]
    for copy in copies:
        copy.start()
    return copies


def _attend_back_columns(copies, *refs):
    for copy in copies:
        copy.wait()
    _attend_back_kernel(*refs[9:13], *refs[4:6], *refs[6:9], *refs[14:])


def attend_back(q, k, v, do, fq, fk, c):
    rows = q.shape[0]
    return run(
        _attend_back_columns,
        "attend_back",
        [((rows, QUAD), BF16)] * 3,
        [q, k, v, do, fq, fk],
        "aaaavv",
        scratch=[VMEM((rows, QUAD), BF16)] * 4
        + [pltpu.SemaphoreType.DMA((4,))]
        + [VMEM((rows, QUAD), F32)] * 2,
        early=functools.partial(_columns_early, c),
    )


def _up_kernel(ws, *refs):
    at_ref, h_ref, b_ref = refs[:3]
    pieces = refs[3 : 3 + len(ws.arrays)]
    act_ref, slope_ref, w_ref, buf, sem = refs[3 + len(ws.arrays) :]
    g = pl.program_id(0)
    copies = ws.copies(at_ref, pieces, buf, sem)

    @pl.when(g == 0)
    def _():
        for group in copies:
            for c in group:
                c.start()

    for i in range(GROUPS):

        @pl.when(g == i)
        def _(i=i):
            for c in copies[i]:
                c.wait()

    w_ref[0] = buf[g]
    bias = b_ref[pl.ds(8 + (at_ref[2] ^ g), 1), :]
    for i in range(h_ref.shape[0] // CHUNK):
        rows = slice(i * CHUNK, (i + 1) * CHUNK)
        value, slope = gelu_parts(_nn(h_ref[rows, :], buf[g]) + bias)
        act_ref[0, rows, :] = value.astype(BF16)
        slope_ref[0, rows, :] = slope.astype(BF16)


def at_group(*shape):
    zeros = (0,) * (len(shape) - 1)
    return pl.BlockSpec((1,) + shape[1:], lambda g: (g,) + zeros)


def fixed(*shape):
    zeros = (0,) * len(shape)
    return pl.BlockSpec(shape, lambda g: zeros, pipeline_mode=pl.Buffered(1))


def up_stage(ws, at, h, bias):
    rows, width = h.shape
    hidden = ws.cols
    act = jax.ShapeDtypeStruct((GROUPS, rows, hidden), BF16)
    return pl.pallas_call(
        functools.partial(_up_kernel, ws),
        grid=(GROUPS,),
        out_shape=(act, act, jax.ShapeDtypeStruct((GROUPS, width, hidden), BF16)),
        in_specs=[pl.BlockSpec(memory_space=SMEM), fixed(rows, width), fixed(*bias.shape)]
        + [pl.BlockSpec(memory_space=pltpu.HBM)] * len(ws.arrays),
        out_specs=(
            at_group(GROUPS, rows, hidden),
            at_group(GROUPS, rows, hidden),
            at_group(GROUPS, width, hidden),
        ),
        scratch_shapes=ws.scratch(width),
        compiler_params=pltpu.CompilerParams(vmem_limit_bytes=LIMIT["up"] << 20),
        name="up",
    )(at, h, bias, *ws.arrays)


def _down_kernel(ws, total, images, *refs):
    (
        at_ref, last_ref, act_ref, after_ref, bias_ref, mine_ref, cot_ref, owned_ref, pairs_ref,
        scale_ref, logit_ref,
    ) = refs[:11]
    image_refs, refs = refs[11 : 11 + images], refs[11 + images :]
    pieces = refs[: len(ws.arrays)]
    out_ref, g_ref, low_ref, dbias_ref, dscale_ref, dlogit_ref, w_ref, give_ref, keep_ref, buf, sem, acc, text_buf, image_buf, image_sem = refs[
        len(ws.arrays) :
    ]
    g = pl.program_id(0)
    copies = ws.copies(at_ref, pieces, buf, sem)
    if images == 1:
        pics = [pltpu.make_async_copy(image_refs[0], image_buf, image_sem.at[0])]
    else:
        many = image_refs[0].shape[1] - ws.rows
        pics = [
            pltpu.make_async_copy(
                image_refs[dx].at[zrel, pl.ds(ws.rows, many), pl.ds(0, image_buf.shape[1])],
                image_buf.at[
                    pl.ds(
                        pl.multiple_of(((at_ref[0] ^ zrel) * 2 + (at_ref[1] ^ dx)) * many, many),
                        many,
                    )
                ],
                image_sem.at[2 * zrel + dx],
            )
            for zrel in range(4)
            for dx in range(2)
        ]

    @pl.when(g == 0)
    def _():
        for group in copies:
            for c in group:
                c.start()
        for c in pics:
            c.start()
        acc[...] = after_ref[...] + bias_ref[3:4, :]

    for i in range(GROUPS):

        @pl.when(g == i)
        def _(i=i):
            for c in copies[i]:
                c.wait()

    @pl.when(g < GROUPS)
    def _():
        w_ref[0] = buf[g]
        acc[...] += _nt(act_ref[0], buf[g])

    @pl.when(g == GROUPS - 1)
    def _():
        out_ref[...] = acc[...].astype(BF16)
        caps = text_buf.shape[0]
        for c in range(caps):
            text_buf[c : c + 1, :] = acc[pl.ds(last_ref[c], 1), :]
        mine = mine_ref[...]
        pooled = text_buf[...]
        text_scale = lax.rsqrt(jnp.sum(pooled * pooled, axis=1, keepdims=True) + EPSILON)
        text = pooled * text_scale
        for c in pics:
            c.wait()
        image = image_buf[...].astype(F32)
        image = image * lax.rsqrt(jnp.sum(image * image, axis=1, keepdims=True) + EPSILON)
        scale = jnp.exp(scale_ref[...])
        dots = lax.dot_general(
            text, image, (((1,), (1,)), ((), ())), precision=PRECISE, preferred_element_type=F32
        )
        sign = 2.0 * pairs_ref[...].astype(F32) - 1.0
        logits = scale * dots + logit_ref[...]
        d_logits = (-1.0 / total) * mine * sign / (1.0 + jnp.exp(sign * logits))
        dlogit_ref[...] = jnp.sum(d_logits, keepdims=True)
        dscale_ref[...] = jnp.sum(d_logits * (scale * dots), keepdims=True)
        d_text = scale * _nn(d_logits, image, PRECISE)
        d_pooled = text_scale * (d_text - text * jnp.sum(d_text * text, axis=1, keepdims=True))
        g_ref[...] = cot_ref[...].astype(F32) * owned_ref[...]
        text_buf[...] = d_pooled
        for c in range(caps):
            g_ref[pl.ds(last_ref[c], 1), :] += text_buf[c : c + 1, :]
        rows = g_ref[...]
        low_ref[...] = rows.astype(BF16)
        dbias_ref[...] = col_sum(rows)

    @pl.when((g >= GROUPS) & (g < GROUPS + 2))
    def _():
        give_ref[0] = _tn(low_ref[...], act_ref[0]).astype(BF16)

    @pl.when(g >= GROUPS + 2)
    def _():
        keep_ref[0] = _tn(low_ref[...], act_ref[0]).astype(BF16)


def down_stage(ws, at, last_at, act, after, bias, mine, cot, owned, images, pairs, scale, logit, total):
    rows, width = after.shape
    hidden = ws.cols
    caps = mine.shape[0]
    one = jax.ShapeDtypeStruct((1, 1), F32)
    pair = jax.ShapeDtypeStruct((2, width, hidden), BF16)

    def visit(i):
        return jnp.where(i < GROUPS, i, (2 * (i - GROUPS) + 1) % 5)

    return pl.pallas_call(
        functools.partial(_down_kernel, ws, total, len(images)),
        grid=(2 * GROUPS,),
        out_shape=(
            jax.ShapeDtypeStruct((rows, width), BF16),
            jax.ShapeDtypeStruct((rows, width), F32),
            jax.ShapeDtypeStruct((rows, width), BF16),
            jax.ShapeDtypeStruct((1, width), F32),
            one,
            one,
            jax.ShapeDtypeStruct((GROUPS, width, hidden), BF16),
            pair,
            pair,
        ),
        in_specs=[
            pl.BlockSpec(memory_space=SMEM),
            pl.BlockSpec(memory_space=SMEM),
            pl.BlockSpec((1, rows, hidden), lambda i: (visit(i), 0, 0)),
            fixed(rows, width),
            fixed(*bias.shape),
            fixed(caps, 1),
            fixed(rows, width),
            fixed(rows, 1),
            fixed(*pairs.shape),
            fixed(1, 1),
            fixed(1, 1),
        ]
        + [pl.BlockSpec(memory_space=pltpu.HBM)] * (len(images) + len(ws.arrays)),
        out_specs=(
            fixed(rows, width),
            fixed(rows, width),
            fixed(rows, width),
            fixed(1, width),
            fixed(1, 1),
            fixed(1, 1),
            pl.BlockSpec((1, width, hidden), lambda i: (jnp.minimum(i, GROUPS - 1), 0, 0)),
            pl.BlockSpec((1, width, hidden), lambda i: (jnp.clip(i - GROUPS, 0, 1), 0, 0)),
            pl.BlockSpec((1, width, hidden), lambda i: (jnp.clip(i - GROUPS - 2, 0, 1), 0, 0)),
        ),
        scratch_shapes=ws.scratch(width) + [VMEM((rows, width), F32), VMEM((caps, width), F32), VMEM((pairs.shape[1], width), BF16), pltpu.SemaphoreType.DMA((8,))],
        compiler_params=pltpu.CompilerParams(vmem_limit_bytes=LIMIT["down"] << 20),
        name="down",
    )(
        at, last_at, act, after, bias, mine, cot, owned, pairs, scale.reshape(1, 1),
        logit.reshape(1, 1), *images, *ws.arrays,
    )


def _up_grad_kernel(has_sum, low_ref, h_ref, slope_ref, wd_ref, wu_ref, *refs):
    i = pl.program_id(0)
    grad_ref, bias_ref, dh_ref, d_pre = refs[-4:]

    @pl.when(i == 0)
    def _():
        dh_ref[...] = refs[0][...] if has_sum else jnp.zeros_like(dh_ref)

    d_act = _nn(low_ref[...], wd_ref[0])
    d_pre[...] = (d_act * slope_ref[0].astype(F32)).astype(BF16)
    bias_ref[0] = col_sum(d_pre[...].astype(F32))
    grad_ref[0] = _tn(h_ref[...], d_pre[...]).astype(BF16)
    dh_ref[...] += _nt(d_pre[...], wu_ref[0])


def up_grad(low, h, slope, w_d, w_u, first, so_far=None):
    rows, width = low.shape
    hidden = slope.shape[2]

    def pair(a, b):
        return pl.BlockSpec((1, a, b), lambda i: (2 * i + first, 0, 0))

    extra = [] if so_far is None else [so_far]
    return pl.pallas_call(
        functools.partial(_up_grad_kernel, so_far is not None),
        grid=(2,),
        out_shape=(
            jax.ShapeDtypeStruct((2, width, hidden), BF16),
            jax.ShapeDtypeStruct((2, 1, hidden), F32),
            jax.ShapeDtypeStruct((rows, width), F32),
        ),
        in_specs=[
            fixed(rows, width),
            fixed(rows, width),
            pair(rows, hidden),
            pair(width, hidden),
            pair(width, hidden),
        ]
        + [fixed(rows, width)] * len(extra),
        out_specs=(
            at_group(2, width, hidden),
            at_group(2, 1, hidden),
            fixed(rows, width),
        ),
        scratch_shapes=[VMEM((rows, hidden), BF16)],
        compiler_params=pltpu.CompilerParams(vmem_limit_bytes=LIMIT["up_grad"] << 20),
        name="up_grad",
    )(low, h, slope, w_d, w_u, *extra)


def _up_last_kernel(
    low_ref, h_ref, slope_ref, wd_ref, wu_ref, dh_in_ref, table_ref, g_hbm, after_hbm, att_hbm,
    wo_hbm, grad_ref, bias_ref, after_grad_ref, datt_ref, ograd_ref, dgain_ref, dshift_ref, dob_ref,
    d_pre, dh_ref, g_ref, after_ref, att_ref, wo_ref, sem,
):
    i = pl.program_id(0)
    copies = [
        pltpu.make_async_copy(src, dst, sem.at[n])
        for n, (src, dst) in enumerate(
            ((g_hbm, g_ref), (after_hbm, after_ref), (att_hbm, att_ref), (wo_hbm, wo_ref))
        )
    ]

    @pl.when(i == 0)
    def _():
        for c in copies:
            c.start()

    _up_grad_kernel(
        True, low_ref, h_ref, slope_ref, wd_ref, wu_ref, dh_in_ref, grad_ref, bias_ref, dh_ref, d_pre
    )

    @pl.when(i == 1)
    def _():
        for c in copies:
            c.wait()
        normed, factor = norm_parts(after_ref[...])
        dh = dh_ref[...]
        dgain_ref[...] = col_sum(dh * normed)
        dshift_ref[...] = col_sum(dh)
        d_after = g_ref[...] + norm_back(dh, normed, factor, table_ref[6:7, :])
        after_grad_ref[...] = d_after
        dob_ref[...] = col_sum(d_after)
        low = d_after.astype(BF16)
        datt_ref[...] = _nn(low, wo_ref[...]).astype(BF16)
        ograd_ref[...] = _tn(low, att_ref[...]).astype(BF16)


def up_last(low, h, slope, w_d, w_u, so_far, table, g, after, att, wo):
    rows, width = low.shape
    hidden = slope.shape[2]

    def pair(a, b):
        return pl.BlockSpec((1, a, b), lambda i: (2 * i, 0, 0))

    hbm = pl.BlockSpec(memory_space=pltpu.HBM)
    vec = jax.ShapeDtypeStruct((1, width), F32)
    return pl.pallas_call(
        _up_last_kernel,
        grid=(2,),
        out_shape=(
            jax.ShapeDtypeStruct((2, width, hidden), BF16),
            jax.ShapeDtypeStruct((2, 1, hidden), F32),
            jax.ShapeDtypeStruct((rows, width), F32),
            jax.ShapeDtypeStruct((rows, width), BF16),
            jax.ShapeDtypeStruct((width, width), BF16),
            vec,
            vec,
            vec,
        ),
        in_specs=[
            fixed(rows, width),
            fixed(rows, width),
            pair(rows, hidden),
            pair(width, hidden),
            pair(width, hidden),
            fixed(rows, width),
            fixed(*table.shape),
            hbm,
            hbm,
            hbm,
            hbm,
        ],
        out_specs=(
            at_group(2, width, hidden),
            at_group(2, 1, hidden),
            fixed(rows, width),
            fixed(rows, width),
            fixed(width, width),
            fixed(1, width),
            fixed(1, width),
            fixed(1, width),
        ),
        scratch_shapes=[
            VMEM((rows, hidden), BF16),
            VMEM((rows, width), F32),
            VMEM((rows, width), F32),
            VMEM((rows, width), F32),
            VMEM((rows, width), BF16),
            VMEM((width, width), BF16),
            pltpu.SemaphoreType.DMA((4,)),
        ],
        compiler_params=pltpu.CompilerParams(vmem_limit_bytes=LIMIT["up_last"] << 20),
        name="up_last",
    )(low, h, slope, w_d, w_u, so_far, table, g, after, att, wo)


def _input_early(quads, *refs):
    d_buf, w_buf, sem = refs[-3:]
    width = quads * QUAD
    copies = [
        pltpu.make_async_copy(refs[n], d_buf.at[:, pl.ds(n * QUAD, QUAD)], sem.at[n])
        for n in range(3 * quads)
    ]
    copies += [
        pltpu.make_async_copy(
            refs[3 * quads + n], w_buf.at[:, pl.ds(n * width, width)], sem.at[3 * quads + n]
        )
        for n in range(3)
    ]
    for c in copies:
        c.start()
    return copies


def _input_kernel(quads, shard, copies, *refs):
    (
        after_grad_ref, x_ref, table_ref, at_ref, up_a_ref, up_b_ref,
        ob_ref, db_ref, gain_two_ref, shift_two_ref, scale_ref, logit_ref,
    ) = refs[3 * quads + 3 : 3 * quads + 15]
    out_ref, vec_ref, d_buf, w_buf, sem = refs[3 * quads + 15 :]
    width = quads * QUAD
    normed, factor = norm_parts(x_ref[...].astype(F32))
    for c in copies:
        c.wait()
    d_buf[:, :width] = d_buf[:, :width] * HEAD_DIM ** (-0.5)
    dh = _nt(d_buf[...], w_buf[...])
    vec_ref[...] = jnp.zeros_like(vec_ref)
    me = at_ref[2]
    for i, first in enumerate((0, 2 * width)):
        whole = col_sum(d_buf[:, first : first + width].astype(F32))
        for g in range(GROUPS):
            vec_ref[pl.ds(4 * i + (me ^ g), 1), :shard] = whole[:, g * shard : (g + 1) * shard]
    for g in range(GROUPS):
        ref = up_b_ref if g % 2 == 0 else up_a_ref
        vec_ref[pl.ds(8 + (me ^ g), 1), :] = ref[g // 2]
    rows = [ob_ref[...], db_ref[...], col_sum(dh * normed), col_sum(dh)]
    rows += [gain_two_ref[...], shift_two_ref[...]]
    for i, v in enumerate(rows):
        vec_ref[12 + i : 13 + i, :] = v
    vec_ref[18:19, :1] = scale_ref[...]
    vec_ref[19:20, :1] = logit_ref[...]
    out_ref[...] = (after_grad_ref[...] + norm_back(dh, normed, factor, table_ref[4:5, :])).astype(
        BF16
    )


def _attn_grad_kernel(quads, shard, *refs):
    h_ref, o_ref = refs[3 * quads : 3 * quads + 2]
    give_ref, keep_ref = refs[3 * quads + 2 :]
    place = {1: (give_ref, 0), 3: (give_ref, 1), 0: (keep_ref, 0), 2: (keep_ref, 1)}
    h = h_ref[...]
    for i in range(3):
        for c in range(quads):
            grad = _tn(h, refs[i * quads + c][...])
            if i == 0:
                grad = grad * HEAD_DIM ** (-0.5)
            grad = grad.astype(BF16)
            lo = c * QUAD
            while lo < (c + 1) * QUAD:
                g = lo // shard
                hi = min((g + 1) * shard, (c + 1) * QUAD)
                ref, slot = place[g]
                start = i * shard + lo - g * shard
                ref[slot, :, start : start + hi - lo] = grad[:, lo - c * QUAD : hi - c * QUAD]
                lo = hi
    for g in range(GROUPS):
        ref, slot = place[g]
        ref[slot, :, 3 * shard :] = o_ref[:, g * shard : (g + 1) * shard]


def _add(*vals):
    total = vals[0].astype(F32)
    for v in vals[1:]:
        total = total + v.astype(F32)
    return total.astype(BF16)


def _plane_kernel(at_ref, keep_ref, got_ref, *outs):
    for y in range(2):
        for dx in range(2):
            x = at_ref[1] ^ dx
            for z in range(keep_ref.shape[1]):
                outs[2 * y + dx][z] = _add(keep_ref[y, z, x], got_ref[y, z, x])


def _split_kernel(cut, at_ref, keep_ref, got_ref, own_ref, give_ref, *outs):
    cols = keep_ref.shape[4]
    for dx, ref in enumerate((own_ref, give_ref)):
        x = at_ref[1] ^ dx
        for y in range(2):
            for z in range(keep_ref.shape[1]):
                ref[y, z] = _add(keep_ref[y, z, x, :, :cut], got_ref[y, z, x, :, :cut])
    for j, ref in enumerate(outs):
        z = at_ref[0] ^ j
        for y in range(2):
            for x in range(2):
                ref[y, x] = _add(keep_ref[y, z, x, :, cut:], got_ref[y, z, x, :, cut:])


def by_block(mv, a):
    return a.reshape(2, mv.nz, 2, a.shape[1] // mv.n, a.shape[2])


def plane_parts(mv, keep, got):
    keep, got = by_block(mv, keep), by_block(mv, got)
    out = ((mv.nz,) + keep.shape[3:], BF16)
    return run(_plane_kernel, "plane_parts", [out] * 4, [mv.at, keep, got], "svv")


def split_parts(mv, keep, got, cut):
    keep, got = by_block(mv, keep), by_block(mv, got)
    rows, cols = keep.shape[3:]
    outs = [((2, mv.nz, rows, cut), BF16)] * 2 + [((2, 2, rows, cols - cut), BF16)] * 4
    kernel = functools.partial(_split_kernel, cut)
    return run(kernel, "plane_parts", outs, [mv.at, keep, got], "svv")


def _z_kernel(count, at_ref, *refs):
    ins, outs = refs[:count], refs[count:]
    for j in range(4):
        b = at_ref[0] ^ j
        outs[j][...] = _add(*[r[b] for r in ins])


def z_parts(mv, held):
    out = (held[0].shape[1:], BF16)
    kernel = functools.partial(_z_kernel, len(held))
    return run(kernel, "z_parts", [out] * 4, [mv.at, *held], "s" + "v" * len(held))


def _join_kernel(at_ref, a_ref, b_ref, *refs):
    ins, outs, (own_ref, give_ref) = refs[:4], refs[4:8], refs[8:]
    for j in range(4):
        b = at_ref[0] ^ j
        for y in range(2):
            outs[j][y] = _add(a_ref[y, b], b_ref[y, b])
    for dx, ref in enumerate((own_ref, give_ref)):
        x = at_ref[1] ^ dx
        for y in range(2):
            ref[y] = _add(*[r[y, x] for r in ins])


def join_parts(mv, own, got, held):
    outs = [((2,) + own.shape[2:], BF16)] * 4 + [((2,) + held[0].shape[2:], BF16)] * 2
    return run(_join_kernel, "z_parts", outs, [mv.at, own, got, *held], "s" + "v" * 6)


def _spread_kernel(piece, at_ref, keep_ref, *refs):
    out_ref = refs[-1]
    wins = [(refs[0],), (refs[1],), (refs[2], refs[3]), (refs[4], refs[5])]
    j = pl.program_id(0)
    here = j ^ at_ref[2]
    before = (j - 1) ^ at_ref[2]
    for i in range(4):

        @pl.when(here == i)
        def _(i=i):
            done = 0
            for ref in wins[i]:
                rows = min(ref.shape[0], piece - done)
                out_ref[done : done + rows, :] = ref[:rows, :].astype(out_ref.dtype)
                done += rows

    for i in range(4):

        @pl.when((before == i) & (j > 0))
        def _(i=i):
            ref = wins[i][-1]
            tail = ref[ref.shape[0] - HALO :, :].astype(out_ref.dtype)
            out_ref[:HALO, :] = jnp.where(keep_ref[0] > 0, out_ref[:HALO, :], tail)


def spread(at, keep, windows, piece, dtype):
    cols = windows[0].shape[1]
    return pl.pallas_call(
        functools.partial(_spread_kernel, piece),
        grid=(GROUPS,),
        out_shape=jax.ShapeDtypeStruct((GROUPS * piece, cols), dtype),
        in_specs=[pl.BlockSpec(memory_space=SMEM), at_group(GROUPS, HALO, 1)]
        + [fixed(*w.shape) for w in windows],
        out_specs=pl.BlockSpec((piece, cols), lambda j: (j, 0)),
        compiler_params=pltpu.CompilerParams(vmem_limit_bytes=LIMIT["spread"] << 20),
        name="spread",
    )(at, keep, *windows)


def _spread_first_kernel(piece, at_ref, own_ref, near_ref, far_ref, out_ref, *rest):
    bufs, sem = rest[:3], rest[3]
    copies = []
    for i, ref in enumerate((own_ref, near_ref, far_ref)):
        rows = min(ref.shape[0], piece)
        bufs[i][...] = ref[:rows, :].astype(F32)
        start = pl.multiple_of((at_ref[2] ^ i) * piece, piece)
        copies.append(pltpu.make_async_copy(bufs[i], out_ref.at[pl.ds(start, rows)], sem.at[i]))
        copies[-1].start()
    for c in copies:
        c.wait()


def spread_first(at, own, near, far, piece):
    rows, cols = own.shape
    wins = (own, near, far)
    return pl.pallas_call(
        functools.partial(_spread_first_kernel, piece),
        out_shape=jax.ShapeDtypeStruct((GROUPS * piece, cols), F32),
        in_specs=[pl.BlockSpec(memory_space=SMEM)] + [pl.BlockSpec(memory_space=VMEM)] * 3,
        out_specs=pl.BlockSpec(memory_space=pltpu.HBM),
        scratch_shapes=[VMEM((min(w.shape[0], piece), cols), F32) for w in wins]
        + [pltpu.SemaphoreType.DMA((3,))],
        compiler_params=pltpu.CompilerParams(vmem_limit_bytes=LIMIT["spread"] << 20),
        name="spread",
    )(at, *wins)


def _spread_last_kernel(piece, at_ref, keep_ref, *refs):
    heads, tails, parts = refs[:4], refs[4:8], refs[8:11]
    out_ref, bufs, head_bufs, sem = refs[12], refs[13:16], refs[16], refs[17]
    copies = []
    for n, (ref, side, first) in enumerate(zip(parts, (2, 3, 3), (1, 0, 1))):
        rows = bufs[n].shape[0]
        bufs[n][...] = ref[:rows, :].astype(F32)
        start = (at_ref[2] ^ side) * piece + first * (piece - rows)
        copies.append(
            pltpu.make_async_copy(
                bufs[n], out_ref.at[pl.ds(pl.multiple_of(start, HALO // 2), rows)], sem.at[n]
            )
        )
        copies[-1].start()
    for c in copies:
        c.wait()
    copies = []
    for j in range(1, GROUPS):
        for i in range(4):

            @pl.when((at_ref[2] ^ j) == i)
            def _(i=i, j=j):
                head_bufs[j - 1] = heads[i][...].astype(F32)

        for i in range(4):

            @pl.when((at_ref[2] ^ (j - 1)) == i)
            def _(i=i, j=j):
                head_bufs[j - 1] = jnp.where(
                    keep_ref[j] > 0, head_bufs[j - 1], tails[i][...].astype(F32)
                )

        copies.append(
            pltpu.make_async_copy(
                head_bufs.at[j - 1], out_ref.at[pl.ds(j * piece, HALO)], sem.at[2 + j]
            )
        )
        copies[-1].start()
    for c in copies:
        c.wait()


def spread_last(at, keep, firsts, lasts, so_far, piece):
    cols = so_far.shape[1]
    split = firsts[2].shape[0]
    heads = [f[:HALO] for f in firsts]
    tails = [t[t.shape[0] - HALO :] for t in lasts]
    vmem = pl.BlockSpec(memory_space=VMEM)
    return pl.pallas_call(
        functools.partial(_spread_last_kernel, piece),
        out_shape=jax.ShapeDtypeStruct(so_far.shape, F32),
        in_specs=[pl.BlockSpec(memory_space=SMEM)]
        + [vmem] * 12
        + [pl.BlockSpec(memory_space=pltpu.HBM)],
        out_specs=pl.BlockSpec(memory_space=pltpu.HBM),
        scratch_shapes=[VMEM((rows, cols), F32) for rows in (piece - split, split, piece - split)]
        + [VMEM((3, HALO, cols), F32), pltpu.SemaphoreType.DMA((6,))],
        input_output_aliases={13: 0},
        compiler_params=pltpu.CompilerParams(vmem_limit_bytes=LIMIT["spread"] << 20),
        name="spread",
    )(at, keep, *heads, *tails, lasts[2], firsts[3], lasts[3], so_far)


def _flip(a, axis, bit):
    n = lax.axis_size(axis)
    return lax.ppermute(a, axis, [(i, i ^ bit) for i in range(n)])


def fence(*trees):
    return lax.optimization_barrier(trees)


def add_low(a, b):
    return (a.astype(F32) + b.astype(F32)).astype(BF16)


class Moves:
    def __init__(self):
        self.n = lax.axis_size("dp")
        self.nz = self.n // 2
        at = lax.axis_index("dp")
        self.at = jnp.stack([at // 2, at % 2, lax.axis_index("mp")]).astype(jnp.int32)
        self.near = self.n == 8

    def z_all(self, a):
        return [a] + [_flip(a, "dp", 2 * j) for j in range(1, 4)]

    def cross_flip(self, a):
        return lax.ppermute(
            a,
            ("dp", "mp"),
            [(4 * d + m, 4 * (d ^ 1) + (m ^ 2)) for d in range(self.n) for m in range(4)],
        )

    def plane_all(self, a):
        return [a, _flip(a, "dp", 1), _flip(a, "mp", 2), self.cross_flip(a)]

    def core_all(self, parts):
        return [_flip(a, "mp", 1) for a in parts]

    def gather_far(self, a):
        mine = lax.all_gather(a, "dp", axis=0, tiled=True)
        far = _flip(mine, "mp", 2)
        whole = jnp.stack([mine, _flip(mine, "mp", 1), far, _flip(far, "mp", 1)])
        return Weights([whole], None, a.shape[0], a.shape[1])

    def to_core(self, give):
        return _flip(give, "mp", 1)

    def scatter_far(self, keep, got):
        both = add_low(keep, got)
        mine = add_low(both[0], _flip(both[1], "mp", 2))
        return lax.psum_scatter(mine, "dp", scatter_dimension=0, tiled=True).astype(F32)

    def plane_sides(self, parts):
        return [
            parts[0], _flip(parts[1], "dp", 1), _flip(parts[2], "mp", 2), self.cross_flip(parts[3]),
        ]

    def z_sides(self, parts):
        return [_flip(parts[j], "dp", 2 * j) for j in range(1, 4)]


PLANE = [(dx, dy) for dy in range(2) for dx in range(2)]


def z_then_plane(first, col, cut, wide):
    return [
        (first + 4 * core + i, (zrel,), zrel, dx, core + 2 * dy, col, cut, wide)
        for core in range(2)
        for i, (dx, dy) in enumerate(PLANE)
        for zrel in range(4)
    ]


def plane_then_z(first, col, cut, wide):
    return [
        (first + 4 * core + zrel, (i,), zrel, dx, core + 2 * dy, col, cut, wide)
        for core in range(2)
        for zrel in range(4)
        for i, (dx, dy) in enumerate(PLANE)
    ]


def body(
    tokens,
    out_cot,
    seg_ids,
    valid_mask,
    last_pos,
    pairs,
    images,
    q_weight,
    k_weight,
    v_weight,
    o_weight,
    up_weight,
    down_weight,
    q_bias,
    v_bias,
    o_bias,
    up_bias,
    down_bias,
    gain_one,
    shift_one,
    gain_two,
    shift_two,
    log_scale,
    logit_bias,
):
    mv = Moves()
    assert lax.axis_size("mp") == GROUPS
    row_count, seq_len = seg_ids.shape
    token_count, width = tokens.shape
    piece = token_count // GROUPS
    caption_total = pairs.shape[0] * mv.n
    at = lax.axis_index("mp")
    shard = q_weight.shape[1]
    hidden = up_weight.shape[1]
    block = q_weight.shape[0]
    quads = width // QUAD

    own_a = jnp.concatenate([q_weight, k_weight, v_weight, o_weight.T], axis=1)
    down_t = down_weight.T
    cut = QUAD
    if mv.near:
        a_z = mv.z_all(own_a)
        a_z[1], up_weight, down_t, images = fence(a_z[1], up_weight, down_t, images)
        own_1 = jnp.concatenate([up_weight, down_t[:, :cut]], axis=1)
        own_1 = jnp.concatenate([own_1, jnp.pad(images, ((0, 0), (0, cut)))], axis=0)
        w2_plane = mv.plane_all(down_t[:, cut:])
        a_z, own_1, w2_plane = fence(a_z, own_1, w2_plane)
        a_here = jnp.stack(a_z)
        a_here, tokens, out_cot, seg_ids, valid_mask, last_pos, q_bias = fence(
            a_here, tokens, out_cot, seg_ids, valid_mask, last_pos, q_bias
        )
        a_plane = mv.plane_all(a_here)
        w1_z = mv.z_all(own_1)

    start = at * piece
    tail = jnp.minimum(start + piece, token_count - HALO)

    def window(a):
        return jnp.concatenate(
            [
                lax.dynamic_slice_in_dim(a, start, piece),
                lax.dynamic_slice_in_dim(a, tail, HALO),
            ],
            axis=0,
        )

    flat_at = jnp.arange(token_count, dtype=jnp.int32)
    caption_id = jnp.where(
        valid_mask.reshape(-1) > 0,
        (flat_at // seq_len) * (last_pos.shape[1] * 2) + seg_ids.reshape(-1),
        (1 << 20) + flat_at,
    )
    inside = at < GROUPS - 1
    ids = window(caption_id)
    tail_ids = jnp.where(inside, ids[piece:], -2 - jnp.arange(HALO, dtype=jnp.int32))
    ids = jnp.concatenate([ids[:piece], tail_ids])
    before = jnp.where(
        at > 0, lax.dynamic_index_in_dim(caption_id, jnp.maximum(start - 1, 0), keepdims=False), -1
    )
    owned = jnp.concatenate([ids[:piece] != before, (tail_ids == ids[piece - 1]) & inside])
    by_piece = caption_id.reshape(GROUPS, piece)
    last_before = jnp.concatenate([jnp.full((1,), -1, jnp.int32), by_piece[:-1, -1]])
    keep_head = (by_piece[:, :HALO] != last_before[:, None]).astype(F32)[:, :, None]
    count = piece + HALO
    places = start + jnp.arange(count, dtype=jnp.int32)
    fq = ids[:, None]
    blocks = count // HALO
    fk = jnp.concatenate([ids.reshape(blocks, HALO)] * 4, axis=1)[:, None, :]

    flat_last = (
        last_pos + seq_len * jnp.arange(row_count, dtype=jnp.int32)[:, None]
    ).reshape(-1)
    last_at = jnp.clip(flat_last - start, 0, count - 1)
    mine = jnp.any((flat_last[:, None] == places[None, :]) & owned[None, :], axis=1)
    mine = mine.astype(F32)[:, None]
    x_rows = window(tokens)
    cot = window(out_cot)
    owned_rows = owned.astype(F32)[:, None]

    table = jnp.concatenate(
        [q_bias, v_bias, o_bias, down_bias, gain_one, shift_one, gain_two, shift_two, up_bias]
    ).reshape(-1, width)
    if mv.near:
        small = (x_rows, cot, fq, fk, last_at, mine, owned_rows, keep_head, table)
        a_plane, w1_z, w2_plane, small = fence(a_plane, w1_z, w2_plane, small)
        x_rows, cot, fq, fk, last_at, mine, owned_rows, keep_head, table = small
        a_core = [mv.to_core(v) for v in a_plane]
        w_a = Weights(a_plane + a_core, z_then_plane(0, 0, 0, hidden), block, hidden)
        w1_here, w2_here = jnp.stack(w1_z), jnp.stack(w2_plane)
        w1_x, w1_y = _flip(w1_here, "dp", 1), _flip(w1_here, "mp", 2)
        w2_near = [_flip(w2_here, "dp", 2), _flip(w2_here, "dp", 4)]
    else:
        w_a, w_u, w_d = (mv.gather_far(v) for v in (own_a, up_weight, down_t))
        pics = [lax.all_gather(images, "dp", axis=0, tiled=True)]

    rows_low = ((count, width), BF16)
    square = ((width, width), BF16)
    h_one, queries, keys, vals, w_q, w_k, w_v, w_o = run(
        functools.partial(_qkv_kernel, w_a, width, shard),
        "qkv",
        [rows_low] * 4 + [square] * 4,
        [mv.at, x_rows, table, *w_a.arrays],
        "svv" + "a" * len(w_a.arrays),
        scratch=w_a.scratch(width),
        early=functools.partial(_qkv_early, w_a),
    )
    if mv.near:
        queries, keys, vals, w1_here, w2_here, w1_x, w1_y, w2_near = fence(
            queries, keys, vals, w1_here, w2_here, w1_x, w1_y, w2_near
        )
        w1_cross, w2_last = mv.cross_flip(w1_here), _flip(w2_here, "dp", 6)
        w1_core = [mv.to_core(v) for v in (w1_here, w1_x, w1_y)]
    attended, after_attn, h_two = run(
        _attend_kernel,
        "attend",
        [rows_low, ((count, width), F32), rows_low],
        [queries, keys, vals, fq, fk, w_o, x_rows, table],
    )
    if mv.near:
        h_two, w1_cross, w2_last, w1_core = fence(h_two, w1_cross, w2_last, w1_core)
        pics = [w1_here, w1_x]
        w1_all = [w1_here, w1_x, w1_y, w1_cross, *w1_core, mv.to_core(w1_cross)]
        w_u = Weights(w1_all, z_then_plane(0, 0, 0, hidden), block, hidden)
        w2_all = [w2_here, *w2_near, w2_last]
        w2_all = w2_all + [mv.to_core(v) for v in w2_all]
    acts, slopes, w_up = up_stage(w_u, mv.at, h_two, table)
    if mv.near:
        w2_all, acts = fence(w2_all, acts)
        w_d = Weights(
            w1_all + w2_all,
            z_then_plane(0, 0, hidden, cut) + plane_then_z(8, cut, 0, hidden - cut),
            block,
            hidden,
        )
    out_low, g_rows, g_low, d_down_bias, d_scale, d_logit, w_down, down_give, down_keep = down_stage(
        w_d, mv.at, last_at, acts, after_attn, table, mine, cot, owned_rows, pics, pairs,
        log_scale, logit_bias, caption_total,
    )

    split = count // 2
    down_got = mv.to_core(down_give)
    out_a, out_near = _flip(out_low[:split], "mp", 2), _flip(out_low, "mp", 1)
    up_give, up_bias_a, d_h_two = up_grad(g_low, h_two, slopes, w_down, w_up, 1)
    down_got, up_give, d_h_two, out_a, out_near = fence(
        down_got, up_give, d_h_two, out_a, out_near
    )
    up_got = mv.to_core(up_give)
    out_cross_a = _flip(out_a, "mp", 1)
    if mv.near:
        sent = plane_parts(mv, down_keep, down_got)
        sent, d_h_two = fence(sent, d_h_two)
        down_held = mv.plane_sides(sent)
    up_keep, up_bias_b, d_after, d_attended, o_grad, d_gain_two, d_shift_two, d_o_bias = up_last(
        g_low, h_two, slopes, w_down, w_up, d_h_two, table, g_rows, after_attn, attended, w_o
    )
    parts = [attend_back(queries, keys, vals, d_attended, fq, fk, 0)]
    if mv.near:
        sent = plane_parts(mv, up_keep, up_got)
        down_held, sent, parts, out_cross_a = fence(
            down_held, sent, parts, out_cross_a
        )
        down_sent = z_parts(mv, down_held)
        down_sent, sent, d_attended = fence(down_sent, sent, d_attended)
        up_held = mv.plane_sides(sent)
        down_pieces = [down_sent[0]] + [_flip(down_sent[j], "dp", 2 * j) for j in (1, 2)]
    for c in range(1, quads):
        parts.append(attend_back(queries, keys, vals, d_attended, fq, fk, c))
    if mv.near:
        parts, up_held, down_pieces = fence(parts, up_held, down_pieces)
        sent = z_parts(mv, up_held)
        sent, parts = fence(sent, parts)
        up_pieces = [sent[0]] + mv.z_sides(sent)
        down_pieces.append(_flip(down_sent[3], "dp", 6))
    flat = [p[i] for i in range(3) for p in parts]
    out_b = _flip(out_low[split:], "mp", 2)
    d_tokens, summed = run(
        functools.partial(_input_kernel, quads, shard),
        "input",
        [rows_low, ((24, hidden), F32)],
        [
            *flat, w_q, w_k, w_v, d_after, x_rows, table, mv.at, up_bias_a, up_bias_b,
            d_o_bias, d_down_bias, d_gain_two, d_shift_two, d_scale, d_logit,
        ],
        "a" * (3 * quads + 3) + "vvvs" + "v" * 8,
        scratch=[
            VMEM((count, 3 * width), BF16),
            VMEM((width, 3 * width), BF16),
            pltpu.SemaphoreType.DMA((3 * quads + 3,)),
        ],
        early=functools.partial(_input_early, quads),
    )
    if mv.near:
        d_tokens, flat, summed, up_pieces, down_pieces, out_b = fence(
            d_tokens, flat, summed, up_pieces, down_pieces, out_b
        )
        summed = summed + _flip(summed, "mp", 1)
    out_cross_b = _flip(out_b, "mp", 1)
    grad_near = _flip(d_tokens, "mp", 1)
    attn_give, attn_keep = run(
        functools.partial(_attn_grad_kernel, quads, shard),
        "attn_grad",
        [((2, width, hidden), BF16)] * 2,
        [*flat, h_one, o_grad],
    )
    attn_give, attn_keep, summed, out_cross_b, d_tokens, grad_near = fence(
        attn_give, attn_keep, summed, out_cross_b, d_tokens, grad_near
    )
    attn_got = mv.to_core(attn_give)
    if mv.near:
        summed = mv.plane_all(summed)
        attn_got, summed = fence(attn_got, summed)
        cut = 2 * QUAD
        own_a, sent_a, *sent = split_parts(mv, attn_keep, attn_got, cut)
        sent_a, sent, d_tokens = fence(sent_a, sent, d_tokens)
        side_a = _flip(sent_a, "dp", 1)
        pieces_b = [sent[0]] + mv.z_sides(sent)
    far_a = _flip(d_tokens[:split], "mp", 2)

    def low_sum(pieces):
        return sum(v.astype(F32) for v in pieces)

    if mv.near:
        side_a, pieces_b, far_a, out_cross_b = fence(side_a, pieces_b, far_a, out_cross_b)
        *sent, own_b, sent_b = join_parts(mv, own_a, side_a, pieces_b)
        sent, sent_b, d_tokens, out_cross_b = fence(sent, sent_b, d_tokens, out_cross_b)
        pieces_a = [sent[0]] + mv.z_sides(sent)
        side_b = _flip(sent_b, "dp", 1)
    far_b = _flip(d_tokens[split:], "mp", 2)
    grad_first = spread_first(mv.at, d_tokens, grad_near, far_a, piece)
    layer_out = spread(
        mv.at, keep_head, [out_low, out_near, out_a, out_b, out_cross_a, out_cross_b], piece, BF16
    )
    if mv.near:
        pieces_a, side_b, far_a, far_b, summed, layer_out, grad_first = fence(
            pieces_a, side_b, far_a, far_b, summed, layer_out, grad_first
        )
    if mv.near:
        summed = mv.z_all((summed[0] + summed[1]) + (summed[2] + summed[3]))
        sum_a, sum_b = low_sum(pieces_a), low_sum([own_b, side_b])
        both = jnp.concatenate([sum_a, sum_b], axis=2)
        attn_far = _flip(both[1].astype(BF16), "mp", 2)
    else:
        summed = lax.psum(summed, ("dp", "mp"))
        grad_down = mv.scatter_far(down_keep, down_got).T
        grad_up = mv.scatter_far(up_keep, up_got)
        grad_attn = mv.scatter_far(attn_keep, attn_got)
    grad_cross_a, grad_cross_b = _flip(far_a, "mp", 1), _flip(far_b, "mp", 1)
    grad_tokens = spread_last(
        mv.at, keep_head, [d_tokens, grad_near, far_a, grad_cross_a],
        [d_tokens, grad_near, far_b, grad_cross_b], grad_first, piece,
    )
    if mv.near:
        grad_tokens, summed, attn_far = fence(grad_tokens, summed, attn_far)
        summed = (summed[0] + summed[1]) + (summed[2] + summed[3])
        grad_down = low_sum(down_pieces).T
        grad_up = low_sum(up_pieces)
        grad_attn = both[0] + attn_far.astype(F32)

    def mine_of(first):
        return lax.dynamic_index_in_dim(summed, first + at, 0, keepdims=False)

    out_vectors = [mine_of(0)[:shard], mine_of(4)[:shard], summed[12], mine_of(8)]
    out_vectors += [summed[i] for i in range(13, 18)] + [summed[18, :1], summed[19, :1]]

    return (
        layer_out,
        grad_tokens,
        grad_attn[:, :shard],
        grad_attn[:, shard : 2 * shard],
        grad_attn[:, 2 * shard : 3 * shard],
        grad_attn[:, 3 * shard :].T,
        grad_up,
        grad_down,
        *out_vectors,
    )


def solution(mesh):
    rows, weight, weight_t = P("dp", None), P("dp", "mp"), P("mp", "dp")
    placed = (rows,) * 7 + (weight,) * 3 + (weight_t, weight, weight_t) + (P(),) * 11
    return jax.shard_map(
        body,
        mesh=mesh,
        in_specs=placed,
        out_specs=(rows,) * 2
        + (weight,) * 3
        + (weight_t, weight, weight_t)
        + (P("mp"), P("mp"), P(), P("mp"))
        + (P(),) * 7,
        check_vma=False,
    )
```
